512 devices in a mesh: dp: 2 (over core), ctx: 32 (over x, z_lo), tensor: 8 (over z_hi, y).
Axes of the slice: x: 4, y: 4, z: 16 (z_hi: 2, z_lo: 8; z = z_hi * 8 + z_lo), core: 2. Of those that a mesh axis runs over, the one named last changes fastest.
Arguments:
- tokens: bfloat16 [2, 4096, 2048], P('dp', 'ctx', 'tensor'), may hold values from -6 to 6
- cotangent: bfloat16 [2, 4096, 2048], P('dp', 'ctx', 'tensor'), may hold values from -6 to 6
- w_value: bfloat16 [2048, 2048], P('ctx', 'tensor'), may hold values from -0.125 to 0.125
- w_gate: bfloat16 [2048, 2048], P('ctx', 'tensor'), may hold values from -0.125 to 0.125
- decay_rate: float32 [4, 2048], P(None, 'tensor'), as said below
- residue: float32 [4, 2048], P(None, 'tensor'), may hold values from -4 to 4
- skip_gain: float32 [2048], P('tensor'), may hold values from -4 to 4
- contig_len: int32 [2, 8], P('dp'), may hold values from 1 to 1536, 4096 in all within a row
Outputs:
- output: bfloat16 [2, 4096, 2048], P('dp', 'ctx', 'tensor')
- grad_tokens: bfloat16 [2, 4096, 2048], P('dp', 'ctx', 'tensor')
- grad_w_value: float32 [2048, 2048], P('ctx', 'tensor')
- grad_w_gate: float32 [2048, 2048], P('ctx', 'tensor')
- grad_skip: float32 [2048], P('tensor')
- grad_residue: float32 [4, 2048], P(None, 'tensor')
- grad_rate: float32 [4, 2048], P(None, 'tensor')
The draws below stay inside these ranges and needn't reach their ends.
Inputs may be any that keep to these rules, and one draw needn't show every extreme that they name: `contig_len`: each row's lengths sum to 4096; the largest of each row is exactly 1536. `decay_rate`: every rate lies between 0.25 / 4096 and 1 / 30.
All inputs are finite; a program needn't handle non-finite values.
Results may differ from the reference program's by a relative error of at most 0.012.
Values may be sent and summed in bfloat16 or wider, within the bound.
A program may use at most 64 MiB of HBM per device.

```python
import math
import jax
import jax.numpy as jnp
import numpy as np
from jax import lax

D = 2048
MODES = 4
NCTG = 8
SEQ = 4096
ROWS = 2
N_TENSOR = 8


def draw_decay_rate(key, part):
    key_pick, key_slow, key_fast = jax.random.split(key, 3)
    slow_share = 0.5
    pick = jax.random.uniform(key_pick, (MODES, D), jnp.float32) < slow_share
    slow_low = jnp.log(jnp.float32(0.25) / SEQ)
    slow_high = jnp.log(jnp.float32(2.0) / SEQ)
    slow = jnp.exp(jax.random.uniform(key_slow, (MODES, D), jnp.float32, slow_low, slow_high))
    fast_low = jnp.log(jnp.float32(1.0 / 512.0))
    fast_high = jnp.log(jnp.float32(1.0 / 30.0))
    fast = jnp.exp(jax.random.uniform(key_fast, (MODES, D), jnp.float32, fast_low, fast_high))
    return jnp.where(pick, slow, fast).astype(jnp.float32)


def with_spikes(drawn, stream_key, source, target, parts, factor):
    owner, partner = [(jnp.arange(drawn.shape[dim]) // (drawn.shape[dim] // parts)).reshape([-1 if axis == dim else 1 for axis in range(drawn.ndim)]) for dim in (source, target)]
    chosen = jax.random.permutation(stream_key, parts)[partner]
    strong = (owner == chosen) | (owner == (partner + parts // 2) % parts)
    return jnp.where(strong, factor * drawn, drawn)


def block_scale(own_key, dims, cuts, low, largest):
    level = 1.0
    for position, shards_of in cuts:
        draws = jax.random.uniform(jax.random.fold_in(jax.random.fold_in(own_key, 6), position), (shards_of,), jnp.float32, low / len(cuts), largest / len(cuts))
        level = level * jnp.repeat(jnp.exp(draws), dims[position] // shards_of).reshape((-1,) + (1,) * (len(dims) - 1 - position))
    return level


def split_up(amount, total, bound, skew):
    weights = [(1 << 20) // math.isqrt(rank ** skew) + 1 for rank in range(2, amount + 1)]
    spare, given = total - bound - (amount - 1), [1] * (amount - 1)
    while spare > 0:
        movable = [i for i in range(amount - 1) if given[i] < bound]
        mass, budget = sum([weights[i] for i in movable]), spare
        for i in movable:
            extra = min(bound - given[i], max(1, budget * weights[i] // mass), spare)
            given[i] = given[i] + extra
            spare = spare - extra
    return np.array([bound] + given)


def ragged(stream_key, number_of, total, bound, slope):
    if number_of == 2:
        one = jax.random.randint(stream_key, (), max(1, total - bound), min(bound, total - 1) + 1)
        return jnp.stack([one, total - one])
    tallies = jnp.asarray(split_up(number_of, total, bound, slope), jnp.int32)
    twos = (number_of - 1) // 2
    donor, sink = tallies[1:1 + 2 * twos:2], tallies[2:2 + 2 * twos:2]
    slack = jnp.minimum(donor - 1, bound - sink)
    shifted = jax.random.randint(jax.random.fold_in(stream_key, 1), (twos,), 0, 1 << 20) % (slack + 1)
    tallies = tallies.at[1:1 + 2 * twos:2].set(donor - shifted).at[2:2 + 2 * twos:2].set(sink + shifted)
    return tallies[jax.random.permutation(jax.random.fold_in(stream_key, 2), number_of)]


def normal_values(rng, shape, spread, limit, shards=(), kind=jnp.bfloat16):
    values = jax.random.normal(rng, shape, jnp.float32) * spread
    if len(shards) > 0:
        values = block_scale(rng, shape, shards, -0.22, 0.18) * values
    return jnp.clip(values, min=-limit, max=limit).astype(kind)


def noise_with(key, shape, spread, most, shards, heavy, kind=jnp.bfloat16):
    drawn = spread * jax.random.normal(key, shape, jnp.float32)
    if shards:
        drawn = drawn * block_scale(key, shape, shards, -0.22, 0.18)
    return jnp.clip(with_spikes(drawn, jax.random.fold_in(key, 3), *heavy), -most, most).astype(kind)


def setup_inputs(seed: int = 0) -> dict:
    key_of = jax.random.split(jax.random.key(seed), 9)
    tokens = noise_with(key_of[0], (ROWS, SEQ, D), 1.0, 6.0, ((0, 2), (1, 32), (2, 8)), (1, 2, 32, 2.75))
    cotangent = normal_values(key_of[1], (ROWS, SEQ, D), 1.0, 6.0, ((0, 2), (1, 32), (2, 8)))
    w_value = normal_values(key_of[2], (D, D), D ** -0.5, 0.125, ((0, 32), (1, 8)))
    w_gate = normal_values(key_of[3], (D, D), D ** -0.5, 0.125, ((0, 32), (1, 8)))
    decay_rate = draw_decay_rate(jax.random.fold_in(key_of[8], 71), 0)
    residue = normal_values(key_of[5], (MODES, D), 1.0, 4.0, ((1, 8),), jnp.float32)
    skip_gain = normal_values(key_of[6], (D,), 1.0, 4.0, ((0, 8),), jnp.float32)
    contig_len = jax.vmap(lambda own: ragged(own, NCTG, SEQ, 3 * SEQ // NCTG, 2))(jax.random.split(key_of[7], ROWS)).reshape((ROWS, NCTG)).astype(jnp.int32)
    return {"tokens": tokens, "cotangent": cotangent, "w_value": w_value, "w_gate": w_gate, "decay_rate": decay_rate, "residue": residue, "skip_gain": skip_gain, "contig_len": contig_len}


def link(first, second):
    return (first[0] * second[0], second[0] * first[1] + second[1])

def channel_block(pieces, reset, reset_next):
    value, gate, upstream, rate, residue, skip_gain = pieces
    pole = jnp.exp(-rate)
    factor = jnp.sqrt(-jnp.expm1(-2.0 * rate))
    keep = (1.0 - reset)[:, None, None] * pole[None]
    drive = jnp.broadcast_to(value[:, None, :], keep.shape)
    state = lax.associative_scan(link, (keep, drive), axis=0)[1]
    mixed = lax.optimization_barrier(jnp.sum((residue * factor)[None] * state, axis=1)) + skip_gain[None] * value
    output = gate * mixed
    grad_mixed = upstream * gate
    grad_gate = upstream * mixed
    keep_back = (1.0 - reset_next)[:, None, None] * pole[None]
    source = grad_mixed[:, None, :] * (residue * factor)[None]
    back = lax.associative_scan(link, (keep_back[::-1], source[::-1]), axis=0)[1][::-1]
    grad_value = lax.optimization_barrier(jnp.sum(back, axis=1)) + skip_gain[None] * grad_mixed
    grad_skip = lax.optimization_barrier(jnp.sum(grad_mixed * value, axis=0))
    paired = lax.optimization_barrier(jnp.sum(grad_mixed[:, None, :] * state, axis=0))
    carried = lax.optimization_barrier(jnp.sum(back * (state - drive), axis=0))
    return (output, grad_value, grad_gate, grad_skip, paired, carried)

def reference(tokens, cotangent, w_value, w_gate, decay_rate, residue, skip_gain, contig_len):
    rows = tokens.shape[0]
    block = math.gcd(D, 128)
    count = D // block
    slab = D // N_TENSOR
    positions = jnp.arange(SEQ, dtype=jnp.int32)
    both_weights = jnp.concatenate([w_value, w_gate], axis=1)
    rate_blocks = jnp.moveaxis(decay_rate.reshape(MODES, count, block), 1, 0)
    residue_blocks = jnp.moveaxis(residue.reshape(MODES, count, block), 1, 0)
    skip_blocks = skip_gain.reshape(count, block)
    outputs = []
    grads = []
    grad_w = jnp.zeros((D, 2 * D), jnp.float32)
    sum_skip = jnp.zeros((count, block), jnp.float32)
    sum_paired = jnp.zeros((count, MODES, block), jnp.float32)
    sum_carried = jnp.zeros((count, MODES, block), jnp.float32)
    for row in range(rows):
        lengths = contig_len[row].astype(jnp.int32)
        starts = (jnp.cumsum(lengths) - lengths).astype(jnp.int32)
        reset = jnp.any(positions[:, None] == starts[None, :], axis=1).astype(jnp.float32)
        reset_next = jnp.any((positions + 1)[:, None] == starts[None, :], axis=1).astype(jnp.float32)
        both = jnp.dot(tokens[row], both_weights, preferred_element_type=jnp.float32)

        def split(field):
            return jnp.moveaxis(field.reshape(SEQ, count, block), 1, 0)
        value_blocks = split(both[:, :D])
        gate_blocks = split(both[:, D:])
        up_blocks = split(cotangent[row].astype(jnp.float32))
        result = lax.map(lambda pieces: channel_block(pieces, reset, reset_next), (value_blocks, gate_blocks, up_blocks, rate_blocks, residue_blocks, skip_blocks))
        out_b, gval_b, ggate_b, skip_part, paired_part, carried_part = result

        def join(field):
            return jnp.moveaxis(field, 0, 1).reshape(SEQ, D)
        outputs.append(join(out_b).astype(jnp.bfloat16))
        value_cot = join(gval_b).astype(jnp.bfloat16)
        gate_cot = join(ggate_b).astype(jnp.bfloat16)
        sum_skip = sum_skip + skip_part
        sum_paired = sum_paired + paired_part
        sum_carried = sum_carried + carried_part
        grad_sum = jnp.zeros((SEQ, D), jnp.float32)
        for index in range(N_TENSOR):
            lo = index * slab
            hi = lo + slab
            part = jnp.dot(value_cot[:, lo:hi], w_value[:, lo:hi].T, preferred_element_type=jnp.float32)
            part = part + jnp.dot(gate_cot[:, lo:hi], w_gate[:, lo:hi].T, preferred_element_type=jnp.float32)
            grad_sum = grad_sum + lax.optimization_barrier(part.astype(jnp.bfloat16)).astype(jnp.float32)
        grads.append(grad_sum.astype(jnp.bfloat16))
        cot_both = jnp.concatenate([value_cot, gate_cot], axis=1)
        grad_w = grad_w + jnp.dot(tokens[row].T, cot_both, preferred_element_type=jnp.float32)
    factor = jnp.sqrt(-jnp.expm1(-2.0 * decay_rate))
    paired = jnp.moveaxis(sum_paired, 0, 1).reshape(MODES, D)
    carried = jnp.moveaxis(sum_carried, 0, 1).reshape(MODES, D)
    grad_skip = sum_skip.reshape(D)
    grad_residue = factor * paired
    grad_rate = -carried + residue * jnp.exp(-2.0 * decay_rate) / factor * paired
    return (jnp.stack(outputs), jnp.stack(grads), grad_w[:, :D], grad_w[:, D:], grad_skip, grad_residue, grad_rate)
```

```python
import jax
import jax.numpy as jnp
from jax import lax
from jax.experimental import pallas as pl
from jax.experimental.pallas import tpu as pltpu
from jax.sharding import PartitionSpec as P

MESH = pl.DeviceIdType.MESH
F32 = jnp.float32
BF = jnp.bfloat16
SPAN = 128
WID = 256
MODES = 4
LINE = 8 * SPAN
NSTAT = 9 * WID

RT, RZ, RX, RS, RF = 0, 8, 16, 20, 24
RE, REX, RC, RP, RPA = 25, 33, 37, 38, 42
RG, RM, RB, RQS, RQX, RQZ, RW2 = 43, 47, 51, 52, 53, 57, 65
NRECV = 66
NSEND = 96


def dot(a, b, dims):
    return lax.dot_general(a, b, (dims, ((), ())), preferred_element_type=F32)


def split(u):
    hi = u.astype(BF)
    lo = (u - hi.astype(F32)).astype(BF)
    return hi, lo


def kernel(
    tok, cot, wv, wg, rate, resid, skip, clen,
    out, gtok, gwv, gwg, gskip, gres, grate,
    fown, fsib, wb, cbuf, ep, em, sloc, bloc, sb, zb, xsb, xb,
    cb, cs, pout, pin, pa_out, pa_in, gout, gin, mout, min_, bout, bin_, gfin,
    stq, stx, stz, ssem, rsem, lsem,
):
    d = lax.axis_index("dp")
    c = lax.axis_index("ctx")
    t = lax.axis_index("tensor")
    x, zl = c // 8, c % 8
    zh, y = t // 4, t % 4
    half, mate = zl // 4, zl % 4

    sib = {"dp": 1 - d}
    anti = {"tensor": (1 - zh) * 4 + y}
    partner = {"ctx": x * 8 + (1 - half) * 4 + mate}
    ys = [lax.rem(y + i, 4) for i in (1, 2, 3)]
    xs = [lax.rem(x + i, 4) for i in (1, 2, 3)]
    zs = [lax.rem(zl + i, 8) for i in range(1, 8)]
    ms = [lax.rem(mate + i, 4) for i in (1, 2, 3)]

    def ydev(k):
        return {"tensor": zh * 4 + k}

    def xdev(k):
        return {"ctx": k * 8 + zl}

    def zdev(k):
        return {"ctx": x * 8 + k}

    def mdev(k):
        return {"ctx": x * 8 + half * 4 + k}

    loads = [
        pltpu.make_async_copy(tok.at[0], fown.at[t], lsem.at[0]),
        pltpu.make_async_copy(cot.at[0], cbuf, lsem.at[1]),
    ]
    for cp in loads:
        cp.start()

    @pl.when(d == 0)
    def _():
        pltpu.make_async_copy(wv, wb.at[0, c], lsem.at[2]).start()

    @pl.when(d == 1)
    def _():
        pltpu.make_async_copy(wg, wb.at[1, c], lsem.at[2]).start()

    barrier = pltpu.get_barrier_semaphore()
    peers = (
        [sib, anti]
        + [ydev(k) for k in ys]
        + [xdev(k) for k in xs]
        + [zdev(k) for k in zs]
    )
    for who in peers:
        pl.semaphore_signal(barrier, inc=1, device_id=who, device_id_type=MESH)

    first = c * SPAN
    starts = [jnp.int32(0)]
    for k in range(7):
        starts.append(starts[-1] + clen[0, k])

    def seg(pos):
        total = (pos >= starts[0]).astype(jnp.int32)
        for s in starts[1:]:
            total = total + (pos >= s).astype(jnp.int32)
        return total

    def row(a):
        return jnp.concatenate([a[m : m + 1, :] for m in range(MODES)], axis=1)

    rt = rate[...]
    factor = jnp.sqrt(one_minus_exp(2.0 * rt))
    wm = resid[...] * factor
    r1 = row(rt)
    tcol = lax.broadcasted_iota(jnp.int32, (SPAN, WID), 0).astype(F32)
    for m in range(MODES):
        rm = rt[m : m + 1, :]
        ep[m] = jnp.exp(rm * tcol)
        em[m] = jnp.exp(-rm * tcol)
    ri = lax.broadcasted_iota(jnp.int32, (SPAN, SPAN), 0)
    ci = lax.broadcasted_iota(jnp.int32, (SPAN, SPAN), 1)
    sr, sc = seg(first + ri), seg(first + ci)
    lower = jnp.where((sr == sc) & (ci <= ri), 1.0, 0.0).astype(BF)
    upper = jnp.where((sr == sc) & (ci >= ri), 1.0, 0.0).astype(BF)
    seg_prev, seg_next = seg(first - 1), seg(first + SPAN)
    stc = seg(first + lax.broadcasted_iota(jnp.int32, (SPAN, WID), 0))
    clearf = jnp.where(stc == seg_prev, 1.0, 0.0)
    clearb = jnp.where(stc == seg_next, 1.0, 0.0)

    k8 = lax.broadcasted_iota(jnp.int32, (8, MODES * WID), 0)
    k4 = lax.broadcasted_iota(jnp.int32, (4, MODES * WID), 0)

    def weight(ok, dist):
        return jnp.where(ok, jnp.exp(-r1 * jnp.maximum(dist, 0).astype(F32)), 0.0)

    base = x * LINE
    endpos = base + SPAN * k8 + (SPAN - 1)
    topos = base + SPAN * k8
    seg_end, seg_top = seg(endpos), seg(topos)
    w_tot_f = weight(seg_end == seg(base + LINE - 1), base + LINE - 1 - endpos)
    w_tot_b = weight(seg_top == seg(base), topos - base)
    w_in_f = weight((k8 < zl) & (seg_end == seg_prev), first - 1 - endpos)
    w_in_b = weight((k8 > zl) & (seg_top == seg_next), topos - (first + SPAN))
    xend = (k4 + 1) * LINE - 1
    xtop = k4 * LINE
    w_x_f = weight((k4 < x) & (seg(xend) == seg_prev), first - 1 - xend)
    w_x_b = weight((k4 > x) & (seg(xtop) == seg_next), xtop - (first + SPAN))

    sends = []

    def send(src, dst, recv, who):
        cp = pltpu.make_async_remote_copy(
            src_ref=src,
            dst_ref=dst,
            send_sem=ssem.at[len(sends)],
            recv_sem=rsem.at[recv],
            device_id=who,
            device_id_type=MESH,
        )
        cp.start()
        sends.append(cp)

    def arrived(ref, recv):
        pltpu.make_async_copy(ref, ref, rsem.at[recv]).wait()

    for cp in loads:
        cp.wait()
    pltpu.make_async_copy(wv, wb.at[d, c], lsem.at[2]).wait()
    pl.semaphore_wait(barrier, len(peers))

    def spread_x(k):
        for i in xs:
            send(wb.at[d, x * 8 + k], wb.at[d, x * 8 + k], RX + x, xdev(i))

    send(fown.at[t], fown.at[t], RT + t, anti)
    send(wb.at[d, c], wb.at[d, c], RZ + zl, partner)
    for i in ms:
        send(wb.at[d, c], wb.at[d, c], RZ + zl, mdev(i))
    spread_x(zl)
    for i in ys:
        send(fown.at[t], fown.at[t], RT + t, ydev(i))
    for i in ms:
        k = half * 4 + i
        arrived(wb.at[d, x * 8 + k], RZ + k)
        spread_x(k)
    k = (1 - half) * 4 + mate
    arrived(wb.at[d, x * 8 + k], RZ + k)
    for i in ms:
        send(wb.at[d, x * 8 + k], wb.at[d, x * 8 + k], RZ + k, mdev(i))
    spread_x(k)
    ta = (1 - zh) * 4 + y
    arrived(fown.at[ta], RT + ta)
    for i in ys:
        send(fown.at[ta], fown.at[ta], RT + ta, ydev(i))
    for i in ms:
        k = (1 - half) * 4 + i
        arrived(wb.at[d, x * 8 + k], RZ + k)
        spread_x(k)

    def line(core, k):
        return wb.at[core, pl.ds(k * 8, 8)]

    send(line(d, x), line(d, x), RS + x, sib)
    for i in ys:
        arrived(fown.at[zh * 4 + i], RT + zh * 4 + i)
    for i in ys:
        arrived(fown.at[(1 - zh) * 4 + i], RT + (1 - zh) * 4 + i)
    send(fown, fsib, RF, sib)
    for i in (xs[0], xs[2], xs[1]):
        arrived(line(d, i), RX + i)
        send(line(d, i), line(d, i), RS + i, sib)
    for i in range(4):
        arrived(line(1 - d, i), RS + i)

    def wblock(core, j):
        return wb[core, 4 * j : 4 * j + 4].reshape(WID, WID)

    mm = ((1,), (0,))
    value = dot(fown[0], wblock(0, 0), mm)
    gate = dot(fown[0], wblock(1, 0), mm)
    for j in range(1, 8):
        value = value + dot(fown[j], wblock(0, j), mm)
        gate = gate + dot(fown[j], wblock(1, j), mm)
    upstream = cbuf[...].astype(F32)
    gm = upstream * gate

    for m in range(MODES):
        hi, lo = split(value * ep[m])
        s = dot(lower, hi, mm) + dot(lower, lo, mm)
        sloc[m] = s
        sb[0:1, m * WID : (m + 1) * WID] = s[SPAN - 1 :, :] * em[m, SPAN - 1 :, :]
        hi, lo = split(gm * wm[m : m + 1, :] * em[m])
        b = dot(upper, hi, mm) + dot(upper, lo, mm)
        bloc[m] = b
        sb[1:2, m * WID : (m + 1) * WID] = b[0:1, :]
    zb[zl] = sb[...]
    for i in (zs[6], zs[0], zs[5], zs[1], zs[4], zs[2], zs[3]):
        send(sb, zb.at[zl], RE + zl, zdev(i))
    for i in zs:
        arrived(zb.at[i], RE + i)
    fz, bz = zb[:, 0, :], zb[:, 1, :]
    xsb[0:1, :] = jnp.sum(w_tot_f * fz, axis=0, keepdims=True)
    xsb[1:2, :] = jnp.sum(w_tot_b * bz, axis=0, keepdims=True)
    xb[x] = xsb[...]
    for i in xs:
        send(xsb, xb.at[x], REX + x, xdev(i))
    inc_f = jnp.sum(w_in_f * fz, axis=0, keepdims=True)
    inc_b = jnp.sum(w_in_b * bz, axis=0, keepdims=True)
    for i in xs:
        arrived(xb.at[i], REX + i)
    inc_f = inc_f + jnp.sum(w_x_f * xb[:, 0, :], axis=0, keepdims=True)
    inc_b = inc_b + jnp.sum(w_x_b * xb[:, 1, :], axis=0, keepdims=True)
    inc_f = inc_f * jnp.exp(-r1)
    inc_b = inc_b * jnp.exp(-float(SPAN) * r1)

    sk = skip[...]
    mixed = sk * value
    gval = sk * gm
    stq[d, :, 0:WID] = jnp.sum(gm * value, axis=0, keepdims=True)
    for m in range(MODES):
        lanes = slice(m * WID, (m + 1) * WID)
        state = em[m] * (sloc[m] + clearf * inc_f[:, lanes])
        gst = ep[m] * (bloc[m] + clearb * inc_b[:, lanes])
        mixed = mixed + wm[m : m + 1, :] * state
        gval = gval + gst
        lo = WID * (1 + m)
        stq[d, :, lo : lo + WID] = jnp.sum(gm * state, axis=0, keepdims=True)
        lo = WID * (5 + m)
        stq[d, :, lo : lo + WID] = jnp.sum(gst * (state - value), axis=0, keepdims=True)
    out[0] = (gate * mixed).astype(BF)
    cv = gval.astype(BF)
    cg = (upstream * mixed).astype(BF)
    cb[0] = cv
    cb[1] = cg
    send(cb.at[1 - d], cs, RC, sib)
    send(stq.at[d], stq.at[d], RQS, sib)

    nt = ((1,), (1,))

    def share(j):
        wj = wb[:, pl.ds(4 * j, 4)]
        return dot(cv, wj[0].reshape(WID, WID), nt) + dot(cg, wj[1].reshape(WID, WID), nt)

    for i in (ys[1], ys[0], ys[2]):
        for h in range(2):
            pout[i, h] = share(h * 4 + i).astype(BF)
        send(pout.at[i], pin.at[y], RP + y, ydev(i))
    for h in range(2):
        pin[y, h] = share(h * 4 + y).astype(BF)

    tn = ((0,), (0,))
    arrived(fsib, RF)
    arrived(cs, RC)
    mine, theirs = cb[d], cs[...]

    def slab(j):
        g = dot(fown[j], mine, tn) + dot(fsib[j], theirs, tn)
        return g.reshape(4, 64, WID)

    for i in (xs[1], xs[0], xs[2]):
        for h in range(2):
            gout[i, 4 * h : 4 * h + 4] = slab(2 * i + h).astype(BF)
        send(gout.at[i], gin.at[x], RG + x, xdev(i))
    own = [slab(2 * x + h) for h in range(2)]

    arrived(stq.at[1 - d], RQS)
    stx[x] = stq[0] + stq[1]
    for i in xs:
        send(stx.at[x], stx.at[x], RQX + x, xdev(i))

    for i in ys:
        arrived(pin.at[i], RP + i)
    other = pin[0, 1 - zh].astype(F32)
    for k in range(1, 4):
        other = other + pin[k, 1 - zh].astype(F32)
    pa_out[...] = other.astype(BF)
    send(pa_out, pa_in, RPA, anti)
    kept = pin[0, zh].astype(F32)
    for k in range(1, 4):
        kept = kept + pin[k, zh].astype(F32)

    for i in xs:
        arrived(stx.at[i], RQX + i)
    stz[zl] = (stx[0] + stx[1]) + (stx[2] + stx[3])
    for i in zs:
        send(stz.at[zl], stz.at[zl], RQZ + zl, zdev(i))

    for i in xs:
        arrived(gin.at[i], RG + i)
    for h in range(2):
        g = own[h]
        for i in xs:
            g = g + gin[i, 4 * h : 4 * h + 4].astype(F32)
        mout[:, h] = g.astype(BF)
    for i in ms:
        send(mout.at[i], min_.at[mate], RM + mate, mdev(i))
    for i in ms:
        arrived(min_.at[i], RM + i)

    def summed(h):
        g = mout[mate, h].astype(F32)
        for i in ms:
            g = g + min_[i, h].astype(F32)
        return g

    bout[...] = summed(1 - half).astype(BF)
    send(bout, bin_, RB, partner)
    g = summed(half)

    for i in zs:
        arrived(stz.at[i], RQZ + i)
    tot = stz[0]
    for k in range(1, 8):
        tot = tot + stz[k]
    gskip[...] = tot[:, 0:WID]
    ratio = resid[...] * jnp.exp(-2.0 * rt) / factor
    for m in range(MODES):
        paired = tot[:, WID * (1 + m) : WID * (2 + m)]
        carried = tot[:, WID * (5 + m) : WID * (6 + m)]
        gres[m : m + 1, :] = factor[m : m + 1, :] * paired
        grate[m : m + 1, :] = ratio[m : m + 1, :] * paired - carried

    arrived(bin_, RB)
    gfin[d] = g + bin_[...].astype(F32)
    send(gfin.at[d], gfin.at[d], RW2, sib)
    arrived(pa_in, RPA)
    gtok[0] = (kept + pa_in[...].astype(F32)).astype(BF)
    arrived(gfin.at[1 - d], RW2)
    gwv[...] = gfin[0]
    gwg[...] = gfin[1]
    for cp in sends:
        cp.wait_send()


def one_minus_exp(a):
    term = a
    total = a
    for k in range(2, 8):
        term = term * (-a / k)
        total = total + term
    return total


def body(tokens, cotangent, w_value, w_gate, decay_rate, residue, skip_gain, contig_len):
    vm = pl.BlockSpec(memory_space=pltpu.VMEM)
    hbm = pl.BlockSpec(memory_space=pl.ANY)
    smem = pl.BlockSpec(memory_space=pltpu.SMEM)
    sds = jax.ShapeDtypeStruct
    outs = pl.pallas_call(
        kernel,
        out_shape=(
            sds((1, SPAN, WID), BF),
            sds((1, SPAN, WID), BF),
            sds((64, WID), F32),
            sds((64, WID), F32),
            sds((1, WID), F32),
            sds((MODES, WID), F32),
            sds((MODES, WID), F32),
        ),
        in_specs=[hbm, hbm, hbm, hbm, vm, vm, vm, smem],
        out_specs=(vm,) * 7,
        scratch_shapes=[
            pltpu.VMEM((8, SPAN, WID), BF),
            pltpu.VMEM((8, SPAN, WID), BF),
            pltpu.VMEM((2, 32, 64, WID), BF),
            pltpu.VMEM((SPAN, WID), BF),
            pltpu.VMEM((MODES, SPAN, WID), F32),
            pltpu.VMEM((MODES, SPAN, WID), F32),
            pltpu.VMEM((MODES, SPAN, WID), F32),
            pltpu.VMEM((MODES, SPAN, WID), F32),
            pltpu.VMEM((2, MODES * WID), F32),
            pltpu.VMEM((8, 2, MODES * WID), F32),
            pltpu.VMEM((2, MODES * WID), F32),
            pltpu.VMEM((4, 2, MODES * WID), F32),
            pltpu.VMEM((2, SPAN, WID), BF),
            pltpu.VMEM((SPAN, WID), BF),
            pltpu.VMEM((4, 2, SPAN, WID), BF),
            pltpu.VMEM((4, 2, SPAN, WID), BF),
            pltpu.VMEM((SPAN, WID), BF),
            pltpu.VMEM((SPAN, WID), BF),
            pltpu.VMEM((4, 8, 64, WID), BF),
            pltpu.VMEM((4, 8, 64, WID), BF),
            pltpu.VMEM((4, 2, 64, WID), BF),
            pltpu.VMEM((4, 2, 64, WID), BF),
            pltpu.VMEM((64, WID), BF),
            pltpu.VMEM((64, WID), BF),
            pltpu.VMEM((2, 64, WID), F32),
            pltpu.VMEM((2, 1, NSTAT), F32),
            pltpu.VMEM((4, 1, NSTAT), F32),
            pltpu.VMEM((8, 1, NSTAT), F32),
            pltpu.SemaphoreType.DMA((NSEND,)),
            pltpu.SemaphoreType.DMA((NRECV,)),
            pltpu.SemaphoreType.DMA((3,)),
        ],
        compiler_params=pltpu.CompilerParams(
            collective_id=0, has_side_effects=True, vmem_limit_bytes=48 << 20
        ),
        name="step",
    )(
        tokens, cotangent, w_value, w_gate, decay_rate, residue,
        skip_gain.reshape(1, WID), contig_len,
    )
    outs = list(outs)
    outs[4] = outs[4].reshape(WID)
    return tuple(outs)


def solution(mesh):
    in_specs = (
        P("dp", "ctx", "tensor"),
        P("dp", "ctx", "tensor"),
        P("ctx", "tensor"),
        P("ctx", "tensor"),
        P(None, "tensor"),
        P(None, "tensor"),
        P("tensor"),
        P("dp", None),
    )
    out_specs = (
        P("dp", "ctx", "tensor"),
        P("dp", "ctx", "tensor"),
        P("ctx", "tensor"),
        P("ctx", "tensor"),
        P("tensor"),
        P(None, "tensor"),
        P(None, "tensor"),
    )
    return jax.shard_map(body, mesh=mesh, in_specs=in_specs, out_specs=out_specs, check_vma=False)
```

```python
import jax
import jax.numpy as jnp
from jax import lax
from jax.experimental import pallas as pl
from jax.experimental.pallas import tpu as pltpu
from jax.sharding import PartitionSpec as P

MESH = pl.DeviceIdType.MESH
F32 = jnp.float32
BF = jnp.bfloat16
SPAN = 128
WID = 256
MODES = 4
LINE = 8 * SPAN
NSTAT = 9 * WID

RT, RZ, RX, RS, RF = 0, 8, 16, 24, 32
RE, REX, RC, RP, RPA = 33, 41, 45, 46, 54
RG, RM, RB, RQS, RQX, RQZ, RW2 = 55, 63, 71, 72, 73, 77, 85
NRECV = 86
NSEND = 104


def dot(a, b, dims):
    return lax.dot_general(a, b, (dims, ((), ())), preferred_element_type=F32)


def split(u):
    hi = u.astype(BF)
    lo = (u - hi.astype(F32)).astype(BF)
    return hi, lo


def kernel(
    tok, cot, wv, wg, rate_h, resid_h, skip_h, clen_h,
    out, gtok, gwv, gwg, gskip, gres, grate,
    fown, fsib, wb, cbuf, ep, em, sloc, bloc, sb, zb, xsb, xb,
    cb, cs, pout, pin, pa_out, pa_in, gout, gin, gown, mout, min_, bout, bin_, gfin,
    wt, ft, stq, stx, stz, rate, resid, skip, clen, ssem, rsem, lsem,
):
    d = lax.axis_index("dp")
    c = lax.axis_index("ctx")
    t = lax.axis_index("tensor")
    x, zl = c // 8, c % 8
    zh, y = t // 4, t % 4
    half, mate = zl // 4, zl % 4

    sib = {"dp": 1 - d}
    anti = {"tensor": (1 - zh) * 4 + y}
    partner = {"ctx": x * 8 + (1 - half) * 4 + mate}
    ys = [lax.rem(y + i, 4) for i in (1, 2, 3)]
    xs = [lax.rem(x + i, 4) for i in (1, 2, 3)]
    zs = [lax.rem(zl + i, 8) for i in range(1, 8)]
    ms = [lax.rem(mate + i, 4) for i in (1, 2, 3)]

    def ydev(k):
        return {"tensor": zh * 4 + k}

    def xdev(k):
        return {"ctx": k * 8 + zl}

    def zdev(k):
        return {"ctx": x * 8 + k}

    def mdev(k):
        return {"ctx": x * 8 + half * 4 + k}

    loads = [
        pltpu.make_async_copy(tok.at[0], fown.at[t], lsem.at[0]),
        pltpu.make_async_copy(cot.at[0], cbuf, lsem.at[1]),
    ]
    small = [
        pltpu.make_async_copy(rate_h, rate, lsem.at[3]),
        pltpu.make_async_copy(resid_h, resid, lsem.at[4]),
        pltpu.make_async_copy(skip_h, skip, lsem.at[5]),
        pltpu.make_async_copy(clen_h, clen, lsem.at[6]),
    ]
    for cp in small + loads:
        cp.start()

    @pl.when(d == 0)
    def _():
        pltpu.make_async_copy(wv, wb.at[0, c], lsem.at[2]).start()

    @pl.when(d == 1)
    def _():
        pltpu.make_async_copy(wg, wb.at[1, c], lsem.at[2]).start()

    barrier = pltpu.get_barrier_semaphore()
    peers = (
        [sib, anti]
        + [ydev(k) for k in ys]
        + [xdev(k) for k in xs]
        + [zdev(k) for k in zs]
    )
    for who in peers:
        pl.semaphore_signal(barrier, inc=1, device_id=who, device_id_type=MESH)

    for cp in small:
        cp.wait()
    first = c * SPAN
    starts = [jnp.int32(0)]
    for k in range(7):
        starts.append(starts[-1] + clen[0, k])

    def seg(pos):
        total = (pos >= starts[0]).astype(jnp.int32)
        for s in starts[1:]:
            total = total + (pos >= s).astype(jnp.int32)
        return total

    def row(a):
        return jnp.concatenate([a[m : m + 1, :] for m in range(MODES)], axis=1)

    rt = rate[...]
    factor = jnp.sqrt(one_minus_exp(2.0 * rt))
    wm = resid[...] * factor
    r1 = row(rt)
    tcol = lax.broadcasted_iota(jnp.int32, (SPAN, WID), 0).astype(F32)
    for m in range(MODES):
        rm = rt[m : m + 1, :]
        ep[m] = jnp.exp(rm * tcol)
        em[m] = jnp.exp(-rm * tcol)
    ri = lax.broadcasted_iota(jnp.int32, (SPAN, SPAN), 0)
    ci = lax.broadcasted_iota(jnp.int32, (SPAN, SPAN), 1)
    sr, sc = seg(first + ri), seg(first + ci)
    lower = jnp.where((sr == sc) & (ci <= ri), 1.0, 0.0).astype(BF)
    upper = jnp.where((sr == sc) & (ci >= ri), 1.0, 0.0).astype(BF)
    seg_prev, seg_next = seg(first - 1), seg(first + SPAN)
    stc = seg(first + lax.broadcasted_iota(jnp.int32, (SPAN, WID), 0))
    clearf = jnp.where(stc == seg_prev, 1.0, 0.0)
    clearb = jnp.where(stc == seg_next, 1.0, 0.0)

    k8 = lax.broadcasted_iota(jnp.int32, (8, MODES * WID), 0)
    k4 = lax.broadcasted_iota(jnp.int32, (4, MODES * WID), 0)

    def weight(ok, dist):
        return jnp.where(ok, jnp.exp(-r1 * jnp.maximum(dist, 0).astype(F32)), 0.0)

    base = x * LINE
    endpos = base + SPAN * k8 + (SPAN - 1)
    topos = base + SPAN * k8
    seg_end, seg_top = seg(endpos), seg(topos)
    w_tot_f = weight(seg_end == seg(base + LINE - 1), base + LINE - 1 - endpos)
    w_tot_b = weight(seg_top == seg(base), topos - base)
    w_in_f = weight((k8 < zl) & (seg_end == seg_prev), first - 1 - endpos)
    w_in_b = weight((k8 > zl) & (seg_top == seg_next), topos - (first + SPAN))
    xend = (k4 + 1) * LINE - 1
    xtop = k4 * LINE
    w_x_f = weight((k4 < x) & (seg(xend) == seg_prev), first - 1 - xend)
    w_x_b = weight((k4 > x) & (seg(xtop) == seg_next), xtop - (first + SPAN))

    sends = []

    def send(src, dst, recv, who):
        cp = pltpu.make_async_remote_copy(
            src_ref=src,
            dst_ref=dst,
            send_sem=ssem.at[len(sends)],
            recv_sem=rsem.at[recv],
            device_id=who,
            device_id_type=MESH,
        )
        cp.start()
        sends.append(cp)

    def arrived(ref, recv):
        pltpu.make_async_copy(ref, ref, rsem.at[recv]).wait()

    for cp in loads:
        cp.wait()
    pltpu.make_async_copy(wv, wb.at[d, c], lsem.at[2]).wait()
    pl.semaphore_wait(barrier, len(peers))

    def spread_x(k):
        for i in (xs[1], xs[0], xs[2]):
            send(wb.at[d, x * 8 + k], wb.at[d, x * 8 + k], RX + 2 * x + k // 4, xdev(i))

    def quad(core, k, g):
        return wb.at[core, pl.ds(k * 8 + 4 * g, 4)]

    def to_sib(k, g):
        send(quad(d, k, g), quad(d, k, g), RS + 2 * k + g, sib)

    near, far = half, 1 - half
    for i in (ms[1], ms[0], ms[2]):
        send(wb.at[d, c], wb.at[d, c], RZ + zl, mdev(i))
    send(wb.at[d, c], wb.at[d, c], RZ + zl, partner)
    send(fown.at[t], fown.at[t], RT + t, anti)
    spread_x(zl)
    for i in ys:
        send(fown.at[t], fown.at[t], RT + t, ydev(i))
    for i in ms:
        k = near * 4 + i
        arrived(wb.at[d, x * 8 + k], RZ + k)
        spread_x(k)
    to_sib(x, near)
    k = far * 4 + mate
    arrived(wb.at[d, x * 8 + k], RZ + k)
    for i in (ms[1], ms[0], ms[2]):
        send(wb.at[d, x * 8 + k], wb.at[d, x * 8 + k], RZ + k, mdev(i))
    spread_x(k)
    ta = (1 - zh) * 4 + y
    arrived(fown.at[ta], RT + ta)
    for i in ys:
        send(fown.at[ta], fown.at[ta], RT + ta, ydev(i))
    for i in ms:
        k = far * 4 + i
        arrived(wb.at[d, x * 8 + k], RZ + k)
        spread_x(k)
    to_sib(x, far)
    for i in (xs[0], xs[2], xs[1]):
        arrived(quad(d, i, near), RX + 2 * i + near)
        to_sib(i, near)
    for i in ys:
        arrived(fown.at[zh * 4 + i], RT + zh * 4 + i)
    for i in ys:
        arrived(fown.at[(1 - zh) * 4 + i], RT + (1 - zh) * 4 + i)
    for i in (xs[0], xs[2], xs[1]):
        arrived(quad(d, i, far), RX + 2 * i + far)
        to_sib(i, far)
    send(fown, fsib, RF, sib)
    for i in range(4):
        for g in range(2):
            arrived(quad(1 - d, i, g), RS + 2 * i + g)

    def wblock(core, j):
        return wb[core, 4 * j : 4 * j + 4].reshape(WID, WID)

    mm = ((1,), (0,))
    value = dot(fown[0], wblock(0, 0), mm)
    gate = dot(fown[0], wblock(1, 0), mm)
    for j in range(1, 8):
        value = value + dot(fown[j], wblock(0, j), mm)
        gate = gate + dot(fown[j], wblock(1, j), mm)
    upstream = cbuf[...].astype(F32)
    gm = upstream * gate

    for m in range(MODES):
        hi, lo = split(value * ep[m])
        s = dot(lower, hi, mm) + dot(lower, lo, mm)
        sloc[m] = s
        sb[0:1, m * WID : (m + 1) * WID] = s[SPAN - 1 :, :] * em[m, SPAN - 1 :, :]
        hi, lo = split(gm * wm[m : m + 1, :] * em[m])
        b = dot(upper, hi, mm) + dot(upper, lo, mm)
        bloc[m] = b
        sb[1:2, m * WID : (m + 1) * WID] = b[0:1, :]
    zb[zl] = sb[...]
    for i in (zs[6], zs[0], zs[5], zs[1], zs[4], zs[2], zs[3]):
        send(sb, zb.at[zl], RE + zl, zdev(i))
    arrived(fsib, RF)
    for j in range(8):
        wt[j, 0:WID] = wblock(0, j).T
        wt[j, WID:] = wblock(1, j).T
        ft[j, :, 0:SPAN] = fown[j].T
        ft[j, :, SPAN:] = fsib[j].T
    for i in zs:
        arrived(zb.at[i], RE + i)
    fz, bz = zb[:, 0, :], zb[:, 1, :]
    xsb[0:1, :] = jnp.sum(w_tot_f * fz, axis=0, keepdims=True)
    xsb[1:2, :] = jnp.sum(w_tot_b * bz, axis=0, keepdims=True)
    xb[x] = xsb[...]
    for i in xs:
        send(xsb, xb.at[x], REX + x, xdev(i))
    inc_f = jnp.sum(w_in_f * fz, axis=0, keepdims=True)
    inc_b = jnp.sum(w_in_b * bz, axis=0, keepdims=True)
    for i in xs:
        arrived(xb.at[i], REX + i)
    inc_f = inc_f + jnp.sum(w_x_f * xb[:, 0, :], axis=0, keepdims=True)
    inc_b = inc_b + jnp.sum(w_x_b * xb[:, 1, :], axis=0, keepdims=True)
    inc_f = inc_f * jnp.exp(-r1)
    inc_b = inc_b * jnp.exp(-float(SPAN) * r1)

    sk = skip[...]
    mixed = sk * value
    gval = sk * gm
    stq[d, :, 0:WID] = jnp.sum(gm * value, axis=0, keepdims=True)
    for m in range(MODES):
        lanes = slice(m * WID, (m + 1) * WID)
        state = em[m] * (sloc[m] + clearf * inc_f[:, lanes])
        gst = ep[m] * (bloc[m] + clearb * inc_b[:, lanes])
        mixed = mixed + wm[m : m + 1, :] * state
        gval = gval + gst
        lo = WID * (1 + m)
        stq[d, :, lo : lo + WID] = jnp.sum(gm * state, axis=0, keepdims=True)
        lo = WID * (5 + m)
        stq[d, :, lo : lo + WID] = jnp.sum(gst * (state - value), axis=0, keepdims=True)
    out[0] = (gate * mixed).astype(BF)
    cv = gval.astype(BF)
    cg = (upstream * mixed).astype(BF)
    cb[0] = cv
    cb[1] = cg
    send(cb.at[1 - d], cs, RC, sib)
    send(stq.at[d], stq.at[d], RQS, sib)

    both = jnp.concatenate([cv, cg], axis=1)

    def share(h, i):
        return dot(both, wt[h * 4 + i], mm).astype(BF)

    def shares(h):
        for i in (ys[1], ys[0], ys[2]):
            pout[h, i] = share(h, i)
            send(pout.at[h, i], pin.at[h, y], RP + 4 * h + y, ydev(i))
        pin[h, y] = share(h, y)

    def shares_sum(h):
        for i in ys:
            arrived(pin.at[h, i], RP + 4 * h + i)
        total = pin[h, 0].astype(F32)
        for k in range(1, 4):
            total = total + pin[h, k].astype(F32)
        return total

    def slab(cots, h, i):
        return dot(ft[2 * i + h], cots, mm).reshape(4, 64, WID)

    def slabs(cots, h):
        for i in (xs[1], xs[0], xs[2]):
            gout[h, i] = slab(cots, h, i).astype(BF)
            send(gout.at[h, i], gin.at[h, x], RG + 4 * h + x, xdev(i))
        gown[h] = slab(cots, h, x)

    def slabs_sum(h):
        for i in xs:
            arrived(gin.at[h, i], RG + 4 * h + i)
        g = gown[h]
        for i in xs:
            g = g + gin[h, i].astype(F32)
        mout[h] = g.astype(BF)
        for i in (ms[1], ms[0], ms[2]):
            send(mout.at[h, i], min_.at[h, mate], RM + 4 * h + mate, mdev(i))

    def mates_sum(h):
        for i in ms:
            arrived(min_.at[h, i], RM + 4 * h + i)
        g = mout[h, mate].astype(F32)
        for i in ms:
            g = g + min_[h, i].astype(F32)
        return g

    shares(1 - zh)
    arrived(cs, RC)
    cots = jnp.concatenate([cb[d], cs[...]], axis=0)
    slabs(cots, far)
    shares(zh)
    slabs(cots, near)
    arrived(stq.at[1 - d], RQS)
    stx[x] = stq[0] + stq[1]
    for i in xs:
        send(stx.at[x], stx.at[x], RQX + x, xdev(i))
    pa_out[...] = shares_sum(1 - zh).astype(BF)
    send(pa_out, pa_in, RPA, anti)
    slabs_sum(far)
    for i in xs:
        arrived(stx.at[i], RQX + i)
    stz[zl] = (stx[0] + stx[1]) + (stx[2] + stx[3])
    for i in zs:
        send(stz.at[zl], stz.at[zl], RQZ + zl, zdev(i))
    slabs_sum(near)
    bout[...] = mates_sum(far).astype(BF)
    send(bout, bin_, RB, partner)
    kept = shares_sum(zh)
    g = mates_sum(near)

    for i in zs:
        arrived(stz.at[i], RQZ + i)
    tot = stz[0]
    for k in range(1, 8):
        tot = tot + stz[k]
    gskip[...] = tot[:, 0:WID]
    ratio = resid[...] * jnp.exp(-2.0 * rt) / factor
    for m in range(MODES):
        paired = tot[:, WID * (1 + m) : WID * (2 + m)]
        carried = tot[:, WID * (5 + m) : WID * (6 + m)]
        gres[m : m + 1, :] = factor[m : m + 1, :] * paired
        grate[m : m + 1, :] = ratio[m : m + 1, :] * paired - carried

    arrived(bin_, RB)
    gfin[d] = g + bin_[...].astype(F32)
    send(gfin.at[d], gfin.at[d], RW2, sib)
    arrived(pa_in, RPA)
    gtok[0] = (kept + pa_in[...].astype(F32)).astype(BF)
    arrived(gfin.at[1 - d], RW2)
    gwv[...] = gfin[0]
    gwg[...] = gfin[1]
    for cp in sends:
        cp.wait_send()


def one_minus_exp(a):
    term = a
    total = a
    for k in range(2, 8):
        term = term * (-a / k)
        total = total + term
    return total


def store(*refs):
    sem = refs[14]
    copies = [pltpu.make_async_copy(refs[k], refs[7 + k], sem.at[k]) for k in range(7)]
    for cp in copies:
        cp.start()
    for cp in copies:
        cp.wait()


def body(tokens, cotangent, w_value, w_gate, decay_rate, residue, skip_gain, contig_len):
    vm = pl.BlockSpec(memory_space=pltpu.VMEM)
    hbm = pl.BlockSpec(memory_space=pltpu.HBM)
    sds = jax.ShapeDtypeStruct
    shapes = (
        sds((1, SPAN, WID), BF),
        sds((1, SPAN, WID), BF),
        sds((64, WID), F32),
        sds((64, WID), F32),
        sds((1, WID), F32),
        sds((MODES, WID), F32),
        sds((MODES, WID), F32),
    )
    outs = pl.pallas_call(
        kernel,
        out_shape=shapes,
        in_specs=[hbm] * 8,
        out_specs=(vm,) * 7,
        scratch_shapes=[
            pltpu.VMEM((8, SPAN, WID), BF),
            pltpu.VMEM((8, SPAN, WID), BF),
            pltpu.VMEM((2, 32, 64, WID), BF),
            pltpu.VMEM((SPAN, WID), BF),
            pltpu.VMEM((MODES, SPAN, WID), F32),
            pltpu.VMEM((MODES, SPAN, WID), F32),
            pltpu.VMEM((MODES, SPAN, WID), F32),
            pltpu.VMEM((MODES, SPAN, WID), F32),
            pltpu.VMEM((2, MODES * WID), F32),
            pltpu.VMEM((8, 2, MODES * WID), F32),
            pltpu.VMEM((2, MODES * WID), F32),
            pltpu.VMEM((4, 2, MODES * WID), F32),
            pltpu.VMEM((2, SPAN, WID), BF),
            pltpu.VMEM((SPAN, WID), BF),
            pltpu.VMEM((2, 4, SPAN, WID), BF),
            pltpu.VMEM((2, 4, SPAN, WID), BF),
            pltpu.VMEM((SPAN, WID), BF),
            pltpu.VMEM((SPAN, WID), BF),
            pltpu.VMEM((2, 4, 4, 64, WID), BF),
            pltpu.VMEM((2, 4, 4, 64, WID), BF),
            pltpu.VMEM((2, 4, 64, WID), F32),
            pltpu.VMEM((2, 4, 64, WID), BF),
            pltpu.VMEM((2, 4, 64, WID), BF),
            pltpu.VMEM((64, WID), BF),
            pltpu.VMEM((64, WID), BF),
            pltpu.VMEM((2, 64, WID), F32),
            pltpu.VMEM((8, 2 * WID, WID), BF),
            pltpu.VMEM((8, WID, 2 * SPAN), BF),
            pltpu.VMEM((2, 1, NSTAT), F32),
            pltpu.VMEM((4, 1, NSTAT), F32),
            pltpu.VMEM((8, 1, NSTAT), F32),
            pltpu.VMEM((MODES, WID), F32),
            pltpu.VMEM((MODES, WID), F32),
            pltpu.VMEM((1, WID), F32),
            pltpu.SMEM((1, 8), jnp.int32),
            pltpu.SemaphoreType.DMA((NSEND,)),
            pltpu.SemaphoreType.DMA((NRECV,)),
            pltpu.SemaphoreType.DMA((7,)),
        ],
        compiler_params=pltpu.CompilerParams(
            collective_id=0, has_side_effects=True, vmem_limit_bytes=67043328
        ),
        name="step",
    )(
        tokens, cotangent, w_value, w_gate, decay_rate, residue,
        skip_gain.reshape(1, WID), contig_len,
    )
    outs = pl.pallas_call(
        store,
        out_shape=shapes,
        in_specs=[vm] * 7,
        out_specs=(hbm,) * 7,
        scratch_shapes=[pltpu.SemaphoreType.DMA((7,))],
        name="store",
    )(*outs)
    outs = list(outs)
    outs[4] = outs[4].reshape(WID)
    return tuple(outs)


def solution(mesh):
    in_specs = (
        P("dp", "ctx", "tensor"),
        P("dp", "ctx", "tensor"),
        P("ctx", "tensor"),
        P("ctx", "tensor"),
        P(None, "tensor"),
        P(None, "tensor"),
        P("tensor"),
        P("dp", None),
    )
    out_specs = (
        P("dp", "ctx", "tensor"),
        P("dp", "ctx", "tensor"),
        P("ctx", "tensor"),
        P("ctx", "tensor"),
        P("tensor"),
        P(None, "tensor"),
        P(None, "tensor"),
    )
    return jax.shard_map(body, mesh=mesh, in_specs=in_specs, out_specs=out_specs, check_vma=False)
```

```python
import jax
import jax.numpy as jnp
from jax import lax
from jax.experimental import pallas as pl
from jax.experimental.pallas import tpu as pltpu
from jax.sharding import PartitionSpec as P

MESH = pl.DeviceIdType.MESH
F32 = jnp.float32
BF = jnp.bfloat16
SPAN = 128
WID = 256
MODES = 4
LINE = 8 * SPAN
NSTAT = 9 * WID

RT, RZ, RX, RS, RF = 0, 16, 24, 32, 40
RE, REX, RC, RP, RPA = 41, 49, 53, 54, 62
RG, RR, RM, RB, RW2 = 63, 71, 75, 83, 84
RQS, RQX, RQM, RQP = 85, 86, 90, 94
NRECV = 95
NSEND = 128


def dot(a, b, dims):
    return lax.dot_general(a, b, (dims, ((), ())), preferred_element_type=F32)


def split(u):
    hi = u.astype(BF)
    lo = (u - hi.astype(F32)).astype(BF)
    return hi, lo


def kernel(
    tok, cot, wv, wg, rate_h, resid_h, skip_h, clen_h,
    out, gtok, gwv, gwg, gskip, gres, grate,
    fown, fsib, wb, cbuf, ep, em, sloc, bloc, sb, zb, xsb, xb,
    cb, cs, pout, pin, pa_out, pa_in, gr_out, gr_in, gk, gd, gc, gin, gown,
    mout, min_, bout, bin_, gfin, wt, ft, stq, stx, stm, stp, rate, resid, skip, clen, ssem, rsem, lsem,
):
    d = lax.axis_index("dp")
    c = lax.axis_index("ctx")
    t = lax.axis_index("tensor")
    x, zl = c // 8, c % 8
    zh, y = t // 4, t % 4
    half, mate = zl // 4, zl % 4

    sib = {"dp": 1 - d}
    anti = {"tensor": (1 - zh) * 4 + y}
    partner = {"ctx": x * 8 + (1 - half) * 4 + mate}
    ys = [lax.rem(y + i, 4) for i in (1, 2, 3)]
    xs = [lax.rem(x + i, 4) for i in (1, 2, 3)]
    zs = [lax.rem(zl + i, 8) for i in range(1, 8)]
    ms = [lax.rem(mate + i, 4) for i in (1, 2, 3)]

    def ydev(k):
        return {"tensor": zh * 4 + k}

    def xdev(k):
        return {"ctx": k * 8 + zl}

    def zdev(k):
        return {"ctx": x * 8 + k}

    def mdev(k):
        return {"ctx": x * 8 + half * 4 + k}

    loads = [
        pltpu.make_async_copy(tok.at[0], fown.at[t], lsem.at[0]),
        pltpu.make_async_copy(cot.at[0], cbuf, lsem.at[1]),
    ]
    small = [
        pltpu.make_async_copy(rate_h, rate, lsem.at[3]),
        pltpu.make_async_copy(resid_h, resid, lsem.at[4]),
        pltpu.make_async_copy(skip_h, skip, lsem.at[5]),
        pltpu.make_async_copy(clen_h, clen, lsem.at[6]),
    ]
    for cp in small + loads:
        cp.start()

    @pl.when(d == 0)
    def _():
        pltpu.make_async_copy(wv, wb.at[0, c], lsem.at[2]).start()

    @pl.when(d == 1)
    def _():
        pltpu.make_async_copy(wg, wb.at[1, c], lsem.at[2]).start()

    barrier = pltpu.get_barrier_semaphore()
    peers = (
        [sib, anti]
        + [ydev(k) for k in ys]
        + [xdev(k) for k in xs]
        + [zdev(k) for k in zs]
    )
    for who in peers:
        pl.semaphore_signal(barrier, inc=1, device_id=who, device_id_type=MESH)

    for cp in small:
        cp.wait()
    first = c * SPAN
    starts = [jnp.int32(0)]
    for k in range(7):
        starts.append(starts[-1] + clen[0, k])

    def seg(pos):
        total = (pos >= starts[0]).astype(jnp.int32)
        for s in starts[1:]:
            total = total + (pos >= s).astype(jnp.int32)
        return total

    def row(a):
        return jnp.concatenate([a[m : m + 1, :] for m in range(MODES)], axis=1)

    rt = rate[...]
    factor = jnp.sqrt(one_minus_exp(2.0 * rt))
    wm = resid[...] * factor
    r1 = row(rt)
    tcol = lax.broadcasted_iota(jnp.int32, (SPAN, WID), 0).astype(F32)
    for m in range(MODES):
        rm = rt[m : m + 1, :]
        ep[m] = jnp.exp(rm * tcol)
        em[m] = jnp.exp(-rm * tcol)
    ri = lax.broadcasted_iota(jnp.int32, (SPAN, SPAN), 0)
    ci = lax.broadcasted_iota(jnp.int32, (SPAN, SPAN), 1)
    sr, sc = seg(first + ri), seg(first + ci)
    lower = jnp.where((sr == sc) & (ci <= ri), 1.0, 0.0).astype(BF)
    upper = jnp.where((sr == sc) & (ci >= ri), 1.0, 0.0).astype(BF)
    seg_prev, seg_next = seg(first - 1), seg(first + SPAN)
    stc = seg(first + lax.broadcasted_iota(jnp.int32, (SPAN, WID), 0))
    clearf = jnp.where(stc == seg_prev, 1.0, 0.0)
    clearb = jnp.where(stc == seg_next, 1.0, 0.0)

    k8 = lax.broadcasted_iota(jnp.int32, (8, MODES * WID), 0)
    k4 = lax.broadcasted_iota(jnp.int32, (4, MODES * WID), 0)

    def weight(ok, dist):
        return jnp.where(ok, jnp.exp(-r1 * jnp.maximum(dist, 0).astype(F32)), 0.0)

    base = x * LINE
    endpos = base + SPAN * k8 + (SPAN - 1)
    topos = base + SPAN * k8
    seg_end, seg_top = seg(endpos), seg(topos)
    w_tot_f = weight(seg_end == seg(base + LINE - 1), base + LINE - 1 - endpos)
    w_tot_b = weight(seg_top == seg(base), topos - base)
    w_in_f = weight((k8 < zl) & (seg_end == seg_prev), first - 1 - endpos)
    w_in_b = weight((k8 > zl) & (seg_top == seg_next), topos - (first + SPAN))
    xend = (k4 + 1) * LINE - 1
    xtop = k4 * LINE
    w_x_f = weight((k4 < x) & (seg(xend) == seg_prev), first - 1 - xend)
    w_x_b = weight((k4 > x) & (seg(xtop) == seg_next), xtop - (first + SPAN))

    sends = []

    def send(src, dst, recv, who):
        cp = pltpu.make_async_remote_copy(
            src_ref=src,
            dst_ref=dst,
            send_sem=ssem.at[len(sends)],
            recv_sem=rsem.at[recv],
            device_id=who,
            device_id_type=MESH,
        )
        cp.start()
        sends.append(cp)

    def arrived(ref, recv):
        pltpu.make_async_copy(ref, ref, rsem.at[recv]).wait()

    for cp in loads:
        cp.wait()
    pltpu.make_async_copy(wv, wb.at[d, c], lsem.at[2]).wait()
    pl.semaphore_wait(barrier, len(peers))

    def spread_x(k):
        for i in (xs[1], xs[0], xs[2]):
            send(wb.at[d, x * 8 + k], wb.at[d, x * 8 + k], RX + 2 * x + k // 4, xdev(i))

    def quad(core, k, g):
        return wb.at[core, pl.ds(k * 8 + 4 * g, 4)]

    def to_sib(k, g):
        send(quad(d, k, g), quad(d, k, g), RS + 2 * k + g, sib)

    near, far = half, 1 - half
    def piece(j, q):
        return fown.at[j, pl.ds(q * (SPAN // 2), SPAN // 2)]

    send(wb.at[d, c], wb.at[d, c], RZ + zl, partner)
    for i in (ms[1], ms[0], ms[2]):
        send(wb.at[d, c], wb.at[d, c], RZ + zl, mdev(i))
    for q in range(2):
        send(piece(t, q), piece(t, q), RT + 2 * t + q, anti)
    spread_x(zl)
    for i in ys:
        send(fown.at[t], fown.at[t], RT + 2 * t, ydev(i))
    for i in ms:
        k = near * 4 + i
        arrived(wb.at[d, x * 8 + k], RZ + k)
        spread_x(k)
    to_sib(x, near)
    k = far * 4 + mate
    arrived(wb.at[d, x * 8 + k], RZ + k)
    for i in (ms[1], ms[0], ms[2]):
        send(wb.at[d, x * 8 + k], wb.at[d, x * 8 + k], RZ + k, mdev(i))
    spread_x(k)
    for i in ms:
        k = far * 4 + i
        arrived(wb.at[d, x * 8 + k], RZ + k)
        spread_x(k)
    to_sib(x, far)
    ta = (1 - zh) * 4 + y
    for q in range(2):
        arrived(piece(ta, q), RT + 2 * ta + q)
        for i in ys:
            send(piece(ta, q), piece(ta, q), RT + 2 * ta + q, ydev(i))
    for i in (xs[0], xs[2], xs[1]):
        arrived(quad(d, i, near), RX + 2 * i + near)
        to_sib(i, near)
    for i in ys:
        arrived(fown.at[zh * 4 + i], RT + 2 * (zh * 4 + i))
    for q in range(2):
        for i in ys:
            arrived(piece((1 - zh) * 4 + i, q), RT + 2 * ((1 - zh) * 4 + i) + q)
    for i in (xs[0], xs[2], xs[1]):
        arrived(quad(d, i, far), RX + 2 * i + far)
        to_sib(i, far)
    send(fown, fsib, RF, sib)
    for i in range(4):
        for g in range(2):
            arrived(quad(1 - d, i, g), RS + 2 * i + g)

    def wblock(core, j):
        return wb[core, 4 * j : 4 * j + 4].reshape(WID, WID)

    mm = ((1,), (0,))
    value = dot(fown[0], wblock(0, 0), mm)
    gate = dot(fown[0], wblock(1, 0), mm)
    for j in range(1, 8):
        value = value + dot(fown[j], wblock(0, j), mm)
        gate = gate + dot(fown[j], wblock(1, j), mm)
    upstream = cbuf[...].astype(F32)
    gm = upstream * gate

    for m in range(MODES):
        hi, lo = split(value * ep[m])
        s = dot(lower, hi, mm) + dot(lower, lo, mm)
        sloc[m] = s
        sb[0:1, m * WID : (m + 1) * WID] = s[SPAN - 1 :, :] * em[m, SPAN - 1 :, :]
        hi, lo = split(gm * wm[m : m + 1, :] * em[m])
        b = dot(upper, hi, mm) + dot(upper, lo, mm)
        bloc[m] = b
        sb[1:2, m * WID : (m + 1) * WID] = b[0:1, :]
    zb[zl] = sb[...]
    for i in (zs[6], zs[0], zs[5], zs[1], zs[4], zs[2], zs[3]):
        send(sb, zb.at[zl], RE + zl, zdev(i))
    arrived(fsib, RF)
    for j in range(8):
        wt[j, 0:WID] = wblock(0, j).T
        wt[j, WID:] = wblock(1, j).T
        ft[j, :, 0:SPAN] = fown[j].T
        ft[j, :, SPAN:] = fsib[j].T
    for i in zs:
        arrived(zb.at[i], RE + i)
    fz, bz = zb[:, 0, :], zb[:, 1, :]
    xsb[0:1, :] = jnp.sum(w_tot_f * fz, axis=0, keepdims=True)
    xsb[1:2, :] = jnp.sum(w_tot_b * bz, axis=0, keepdims=True)
    xb[x] = xsb[...]
    for i in xs:
        send(xsb, xb.at[x], REX + x, xdev(i))
    inc_f = jnp.sum(w_in_f * fz, axis=0, keepdims=True)
    inc_b = jnp.sum(w_in_b * bz, axis=0, keepdims=True)
    for i in xs:
        arrived(xb.at[i], REX + i)
    inc_f = inc_f + jnp.sum(w_x_f * xb[:, 0, :], axis=0, keepdims=True)
    inc_b = inc_b + jnp.sum(w_x_b * xb[:, 1, :], axis=0, keepdims=True)
    inc_f = inc_f * jnp.exp(-r1)
    inc_b = inc_b * jnp.exp(-float(SPAN) * r1)

    sk = skip[...]
    mixed = sk * value
    gval = sk * gm
    stq[d, :, 0:WID] = jnp.sum(gm * value, axis=0, keepdims=True)
    for m in range(MODES):
        lanes = slice(m * WID, (m + 1) * WID)
        state = em[m] * (sloc[m] + clearf * inc_f[:, lanes])
        gst = ep[m] * (bloc[m] + clearb * inc_b[:, lanes])
        mixed = mixed + wm[m : m + 1, :] * state
        gval = gval + gst
        lo = WID * (1 + m)
        stq[d, :, lo : lo + WID] = jnp.sum(gm * state, axis=0, keepdims=True)
        lo = WID * (5 + m)
        stq[d, :, lo : lo + WID] = jnp.sum(gst * (state - value), axis=0, keepdims=True)
    out[0] = (gate * mixed).astype(BF)
    cv = gval.astype(BF)
    cg = (upstream * mixed).astype(BF)
    cb[0] = cv
    cb[1] = cg
    send(cb.at[1 - d], cs, RC, sib)
    send(stq.at[d], stq.at[d], RQS, sib)

    both = jnp.concatenate([cv, cg], axis=1)

    def share(h, i):
        return dot(both, wt[h * 4 + i], mm).astype(BF)

    def shares(h):
        for i in (ys[1], ys[0], ys[2]):
            pout[h, i] = share(h, i)
            send(pout.at[h, i], pin.at[h, y], RP + 4 * h + y, ydev(i))
        pin[h, y] = share(h, y)

    def shares_sum(h):
        for i in ys:
            arrived(pin.at[h, i], RP + 4 * h + i)
        total = pin[h, 0].astype(F32)
        for k in range(1, 4):
            total = total + pin[h, k].astype(F32)
        return total

    right, left = xs[0], xs[2]

    def slab(h, i):
        return dot(ft[2 * i + h], cots, mm).reshape(4, 64, WID)

    def x_start(h):
        g = slab(h, xs[1]).astype(BF)
        gr_out[h, 0] = g[0:2]
        send(gr_out.at[h, 0], gr_in.at[h, 0], RR + 2 * h, xdev(right))
        gr_out[h, 1] = g[2:4]
        send(gr_out.at[h, 1], gr_in.at[h, 1], RR + 2 * h + 1, xdev(left))

    def x_direct(h):
        g = slab(h, right)
        gk[h, 0] = g[0:2]
        gd[h, 0] = g[2:4].astype(BF)
        send(gd.at[h, 0], gin.at[h, 0, 1], RG + 4 * h + 1, xdev(right))
        g = slab(h, left)
        gk[h, 1] = g[2:4]
        gd[h, 1] = g[0:2].astype(BF)
        send(gd.at[h, 1], gin.at[h, 1, 0], RG + 4 * h + 2, xdev(left))

    def x_relay(h):
        for side, who, part in ((0, right, 0), (1, left, 1)):
            arrived(gr_in.at[h, side], RR + 2 * h + side)
            gc[h, side] = (gk[h, side] + gr_in[h, side].astype(F32)).astype(BF)
            send(gc.at[h, side], gin.at[h, side, part], RG + 4 * h + 3 * side, xdev(who))

    def x_sum(h):
        for side in range(2):
            for part in range(2):
                arrived(gin.at[h, side, part], RG + 4 * h + 2 * side + part)
        for part in range(2):
            g = gown[h, 2 * part : 2 * part + 2]
            g = g + gin[h, 0, part].astype(F32) + gin[h, 1, part].astype(F32)
            mout[h, 2 * part : 2 * part + 2] = g.astype(BF)
        for i in (ms[1], ms[0], ms[2]):
            send(mout.at[h, i], min_.at[h, mate], RM + 4 * h + mate, mdev(i))

    def mates_sum(h):
        for i in ms:
            arrived(min_.at[h, i], RM + 4 * h + i)
        g = mout[h, mate].astype(F32)
        for i in ms:
            g = g + min_[h, i].astype(F32)
        return g

    shares(1 - zh)
    arrived(stq.at[1 - d], RQS)
    stx[x] = stq[0] + stq[1]
    for i in xs:
        send(stx.at[x], stx.at[x], RQX + x, xdev(i))
    arrived(cs, RC)
    cots = jnp.concatenate([cb[d], cs[...]], axis=0)
    x_start(far)
    x_direct(far)
    x_start(near)
    shares(zh)
    for h in (far, near):
        gown[h] = slab(h, x)
    x_relay(far)
    x_direct(near)
    pa_out[...] = shares_sum(1 - zh).astype(BF)
    send(pa_out, pa_in, RPA, anti)
    x_relay(near)
    for i in xs:
        arrived(stx.at[i], RQX + i)
    stm[mate] = (stx[0] + stx[1]) + (stx[2] + stx[3])
    for i in ms:
        send(stm.at[mate], stm.at[mate], RQM + mate, mdev(i))
    x_sum(far)
    for i in ms:
        arrived(stm.at[i], RQM + i)
    stp[half] = (stm[0] + stm[1]) + (stm[2] + stm[3])
    send(stp.at[half], stp.at[half], RQP, partner)
    x_sum(near)
    bout[...] = mates_sum(far).astype(BF)
    send(bout, bin_, RB, partner)
    kept = shares_sum(zh)
    arrived(stp.at[1 - half], RQP)
    tot = stp[0] + stp[1]
    gskip[...] = tot[:, 0:WID]
    ratio = resid[...] * jnp.exp(-2.0 * rt) / factor
    for m in range(MODES):
        paired = tot[:, WID * (1 + m) : WID * (2 + m)]
        carried = tot[:, WID * (5 + m) : WID * (6 + m)]
        gres[m : m + 1, :] = factor[m : m + 1, :] * paired
        grate[m : m + 1, :] = ratio[m : m + 1, :] * paired - carried
    g = mates_sum(near)

    arrived(bin_, RB)
    gfin[d] = g + bin_[...].astype(F32)
    send(gfin.at[d], gfin.at[d], RW2, sib)
    arrived(pa_in, RPA)
    gtok[0] = (kept + pa_in[...].astype(F32)).astype(BF)
    arrived(gfin.at[1 - d], RW2)
    gwv[...] = gfin[0]
    gwg[...] = gfin[1]
    for cp in sends:
        cp.wait_send()


def one_minus_exp(a):
    term = a
    total = a
    for k in range(2, 8):
        term = term * (-a / k)
        total = total + term
    return total


def store(*refs):
    sem = refs[14]
    copies = [pltpu.make_async_copy(refs[k], refs[7 + k], sem.at[k]) for k in range(7)]
    for cp in copies:
        cp.start()
    for cp in copies:
        cp.wait()


def body(tokens, cotangent, w_value, w_gate, decay_rate, residue, skip_gain, contig_len):
    vm = pl.BlockSpec(memory_space=pltpu.VMEM)
    hbm = pl.BlockSpec(memory_space=pltpu.HBM)
    sds = jax.ShapeDtypeStruct
    shapes = (
        sds((1, SPAN, WID), BF),
        sds((1, SPAN, WID), BF),
        sds((64, WID), F32),
        sds((64, WID), F32),
        sds((1, WID), F32),
        sds((MODES, WID), F32),
        sds((MODES, WID), F32),
    )
    outs = pl.pallas_call(
        kernel,
        out_shape=shapes,
        in_specs=[hbm] * 8,
        out_specs=(vm,) * 7,
        scratch_shapes=[
            pltpu.VMEM((8, SPAN, WID), BF),
            pltpu.VMEM((8, SPAN, WID), BF),
            pltpu.VMEM((2, 32, 64, WID), BF),
            pltpu.VMEM((SPAN, WID), BF),
            pltpu.VMEM((MODES, SPAN, WID), F32),
            pltpu.VMEM((MODES, SPAN, WID), F32),
            pltpu.VMEM((MODES, SPAN, WID), F32),
            pltpu.VMEM((MODES, SPAN, WID), F32),
            pltpu.VMEM((2, MODES * WID), F32),
            pltpu.VMEM((8, 2, MODES * WID), F32),
            pltpu.VMEM((2, MODES * WID), F32),
            pltpu.VMEM((4, 2, MODES * WID), F32),
            pltpu.VMEM((2, SPAN, WID), BF),
            pltpu.VMEM((SPAN, WID), BF),
            pltpu.VMEM((2, 4, SPAN, WID), BF),
            pltpu.VMEM((2, 4, SPAN, WID), BF),
            pltpu.VMEM((SPAN, WID), BF),
            pltpu.VMEM((SPAN, WID), BF),
            pltpu.VMEM((2, 2, 2, 64, WID), BF),
            pltpu.VMEM((2, 2, 2, 64, WID), BF),
            pltpu.VMEM((2, 2, 2, 64, WID), F32),
            pltpu.VMEM((2, 2, 2, 64, WID), BF),
            pltpu.VMEM((2, 2, 2, 64, WID), BF),
            pltpu.VMEM((2, 2, 2, 2, 64, WID), BF),
            pltpu.VMEM((2, 4, 64, WID), F32),
            pltpu.VMEM((2, 4, 64, WID), BF),
            pltpu.VMEM((2, 4, 64, WID), BF),
            pltpu.VMEM((64, WID), BF),
            pltpu.VMEM((64, WID), BF),
            pltpu.VMEM((2, 64, WID), F32),
            pltpu.VMEM((8, 2 * WID, WID), BF),
            pltpu.VMEM((8, WID, 2 * SPAN), BF),
            pltpu.VMEM((2, 1, NSTAT), F32),
            pltpu.VMEM((4, 1, NSTAT), F32),
            pltpu.VMEM((4, 1, NSTAT), F32),
            pltpu.VMEM((2, 1, NSTAT), F32),
            pltpu.VMEM((MODES, WID), F32),
            pltpu.VMEM((MODES, WID), F32),
            pltpu.VMEM((1, WID), F32),
            pltpu.SMEM((1, 8), jnp.int32),
            pltpu.SemaphoreType.DMA((NSEND,)),
            pltpu.SemaphoreType.DMA((NRECV,)),
            pltpu.SemaphoreType.DMA((7,)),
        ],
        compiler_params=pltpu.CompilerParams(
            collective_id=0, has_side_effects=True, vmem_limit_bytes=67043328
        ),
        name="step",
    )(
        tokens, cotangent, w_value, w_gate, decay_rate, residue,
        skip_gain.reshape(1, WID), contig_len,
    )
    outs = pl.pallas_call(
        store,
        out_shape=shapes,
        in_specs=[vm] * 7,
        out_specs=(hbm,) * 7,
        scratch_shapes=[pltpu.SemaphoreType.DMA((7,))],
        name="store",
    )(*outs)
    outs = list(outs)
    outs[4] = outs[4].reshape(WID)
    return tuple(outs)


def solution(mesh):
    in_specs = (
        P("dp", "ctx", "tensor"),
        P("dp", "ctx", "tensor"),
        P("ctx", "tensor"),
        P("ctx", "tensor"),
        P(None, "tensor"),
        P(None, "tensor"),
        P("tensor"),
        P("dp", None),
    )
    out_specs = (
        P("dp", "ctx", "tensor"),
        P("dp", "ctx", "tensor"),
        P("ctx", "tensor"),
        P("ctx", "tensor"),
        P("tensor"),
        P(None, "tensor"),
        P(None, "tensor"),
    )
    return jax.shard_map(body, mesh=mesh, in_specs=in_specs, out_specs=out_specs, check_vma=False)
```

```python
import jax
import jax.numpy as jnp
from jax import lax
from jax.experimental import pallas as pl
from jax.experimental.pallas import tpu as pltpu
from jax.sharding import PartitionSpec as P

MESH = pl.DeviceIdType.MESH
F32 = jnp.float32
BF = jnp.bfloat16
SPAN = 128
WID = 256
MODES = 4
LINE = 8 * SPAN
NSTAT = 9 * WID // 2
PART = SPAN // 2

RT, RZ, RX, RS, RF = 0, 16, 24, 32, 40
RE, REX, RC, RP, RPA = 41, 49, 53, 54, 62
RG, RR, RM, RB, RW2 = 63, 71, 75, 83, 84
RQS, RQX, RQM, RQP, RQ2 = 85, 86, 90, 94, 95
RP2, RPA2 = 96, 104
NRECV = 105
NSEND = 140


def dot(a, b, dims):
    return lax.dot_general(a, b, (dims, ((), ())), preferred_element_type=F32)


def split(u):
    hi = u.astype(BF)
    lo = (u - hi.astype(F32)).astype(BF)
    return hi, lo


def kernel(
    tok, cot, wv, wg, rate_h, resid_h, skip_h, clen_h,
    out, gtok, gwv, gwg, gskip, gres, grate,
    fown, fsib, wb, cbuf, ep, em, sloc, bloc, sb, sh, zb, zf, xsb, xb,
    cb, cs, pout, pin, pa_out, pa_in, gr_out, gr_in, gk, gd, gc, gin, gown,
    mout, min_, bout, bin_, gfin, wt, ft, stl, sti, stx, stm, stp, tfin, rate, resid, skip, clen, ssem, rsem, lsem,
):
    d = lax.axis_index("dp")
    c = lax.axis_index("ctx")
    t = lax.axis_index("tensor")
    x, zl = c // 8, c % 8
    zh, y = t // 4, t % 4
    half, mate = zl // 4, zl % 4

    sib = {"dp": 1 - d}
    anti = {"tensor": (1 - zh) * 4 + y}
    partner = {"ctx": x * 8 + (1 - half) * 4 + mate}
    ys = [lax.rem(y + i, 4) for i in (1, 2, 3)]
    xs = [lax.rem(x + i, 4) for i in (1, 2, 3)]
    zs = [lax.rem(zl + i, 8) for i in range(1, 8)]
    ms = [lax.rem(mate + i, 4) for i in (1, 2, 3)]

    def ydev(k):
        return {"tensor": zh * 4 + k}

    def xdev(k):
        return {"ctx": k * 8 + zl}

    def zdev(k):
        return {"ctx": x * 8 + k}

    def mdev(k):
        return {"ctx": x * 8 + half * 4 + k}

    loads = [
        pltpu.make_async_copy(tok.at[0], fown.at[t], lsem.at[0]),
        pltpu.make_async_copy(cot.at[0], cbuf, lsem.at[1]),
    ]
    small = [
        pltpu.make_async_copy(rate_h, rate, lsem.at[3]),
        pltpu.make_async_copy(resid_h, resid, lsem.at[4]),
        pltpu.make_async_copy(skip_h, skip, lsem.at[5]),
        pltpu.make_async_copy(clen_h, clen, lsem.at[6]),
    ]
    for cp in small + loads:
        cp.start()

    @pl.when(d == 0)
    def _():
        pltpu.make_async_copy(wv, wb.at[0, c], lsem.at[2]).start()

    @pl.when(d == 1)
    def _():
        pltpu.make_async_copy(wg, wb.at[1, c], lsem.at[2]).start()

    barrier = pltpu.get_barrier_semaphore()
    peers = (
        [sib, anti]
        + [ydev(k) for k in ys]
        + [xdev(k) for k in xs]
        + [zdev(k) for k in zs]
    )
    for who in peers:
        pl.semaphore_signal(barrier, inc=1, device_id=who, device_id_type=MESH)

    for cp in small:
        cp.wait()
    first = c * SPAN
    starts = [jnp.int32(0)]
    for k in range(7):
        starts.append(starts[-1] + clen[0, k])

    def seg(pos):
        total = (pos >= starts[0]).astype(jnp.int32)
        for s in starts[1:]:
            total = total + (pos >= s).astype(jnp.int32)
        return total

    def row(a):
        return jnp.concatenate([a[m : m + 1, :] for m in range(MODES)], axis=1)

    rt = rate[...]
    factor = jnp.sqrt(one_minus_exp(2.0 * rt))
    wm = resid[...] * factor
    r1 = row(rt)
    step_f = jnp.exp(-r1)
    step_b = jnp.exp(-float(SPAN) * r1)
    tcol = lax.broadcasted_iota(jnp.int32, (SPAN, WID), 0).astype(F32)
    for m in range(MODES):
        rm = rt[m : m + 1, :]
        ep[m] = jnp.exp(rm * tcol)
        em[m] = jnp.exp(-rm * tcol)
    ri = lax.broadcasted_iota(jnp.int32, (SPAN, SPAN), 0)
    ci = lax.broadcasted_iota(jnp.int32, (SPAN, SPAN), 1)
    sr, sc = seg(first + ri), seg(first + ci)
    lower = jnp.where((sr == sc) & (ci <= ri), 1.0, 0.0).astype(BF)
    upper = jnp.where((sr == sc) & (ci >= ri), 1.0, 0.0).astype(BF)
    seg_prev, seg_next = seg(first - 1), seg(first + SPAN)
    stc = seg(first + lax.broadcasted_iota(jnp.int32, (SPAN, WID), 0))
    clearf = jnp.where(stc == seg_prev, 1.0, 0.0)
    clearb = jnp.where(stc == seg_next, 1.0, 0.0)

    k8 = lax.broadcasted_iota(jnp.int32, (8, MODES * WID), 0)
    k4 = lax.broadcasted_iota(jnp.int32, (4, MODES * WID), 0)

    def weight(ok, dist):
        return jnp.where(ok, jnp.exp(-r1 * jnp.maximum(dist, 0).astype(F32)), 0.0)

    base = x * LINE
    endpos = base + SPAN * k8 + (SPAN - 1)
    topos = base + SPAN * k8
    seg_end, seg_top = seg(endpos), seg(topos)
    w_tot_f = weight(seg_end == seg(base + LINE - 1), base + LINE - 1 - endpos)
    w_tot_b = weight(seg_top == seg(base), topos - base)
    w_in_f = weight((k8 < zl) & (seg_end == seg_prev), first - 1 - endpos)
    w_in_b = weight((k8 > zl) & (seg_top == seg_next), topos - (first + SPAN))
    xend = (k4 + 1) * LINE - 1
    xtop = k4 * LINE
    w_x_f = weight((k4 < x) & (seg(xend) == seg_prev), first - 1 - xend)
    w_x_b = weight((k4 > x) & (seg(xtop) == seg_next), xtop - (first + SPAN))

    sends = []

    def send(src, dst, recv, who):
        cp = pltpu.make_async_remote_copy(
            src_ref=src,
            dst_ref=dst,
            send_sem=ssem.at[len(sends)],
            recv_sem=rsem.at[recv],
            device_id=who,
            device_id_type=MESH,
        )
        cp.start()
        sends.append(cp)

    def arrived(ref, recv):
        pltpu.make_async_copy(ref, ref, rsem.at[recv]).wait()

    for cp in loads:
        cp.wait()
    pltpu.make_async_copy(wv, wb.at[d, c], lsem.at[2]).wait()
    pl.semaphore_wait(barrier, len(peers))

    def spread_x(k):
        for i in (xs[1], xs[0], xs[2]):
            send(wb.at[d, x * 8 + k], wb.at[d, x * 8 + k], RX + 2 * x + k // 4, xdev(i))

    def quad(core, k, g):
        return wb.at[core, pl.ds(k * 8 + 4 * g, 4)]

    def to_sib(k, g):
        send(quad(d, k, g), quad(d, k, g), RS + 2 * k + g, sib)

    near, far = half, 1 - half
    def piece(j, q):
        return fown.at[j, pl.ds(q * (SPAN // 2), SPAN // 2)]

    send(wb.at[d, c], wb.at[d, c], RZ + zl, partner)
    for i in (ms[1], ms[0], ms[2]):
        send(wb.at[d, c], wb.at[d, c], RZ + zl, mdev(i))
    for q in range(2):
        send(piece(t, q), piece(t, q), RT + 2 * t + q, anti)
    spread_x(zl)
    for i in ys:
        send(fown.at[t], fown.at[t], RT + 2 * t, ydev(i))
    for i in ms:
        k = near * 4 + i
        arrived(wb.at[d, x * 8 + k], RZ + k)
        spread_x(k)
    to_sib(x, near)
    k = far * 4 + mate
    arrived(wb.at[d, x * 8 + k], RZ + k)
    for i in (ms[1], ms[0], ms[2]):
        send(wb.at[d, x * 8 + k], wb.at[d, x * 8 + k], RZ + k, mdev(i))
    spread_x(k)
    ta = (1 - zh) * 4 + y

    def tokens_on(q):
        arrived(piece(ta, q), RT + 2 * ta + q)
        for i in ys:
            send(piece(ta, q), piece(ta, q), RT + 2 * ta + q, ydev(i))

    tokens_on(0)
    for i in ms:
        k = far * 4 + i
        arrived(wb.at[d, x * 8 + k], RZ + k)
        spread_x(k)
    to_sib(x, far)
    tokens_on(1)
    for i in (xs[0], xs[2], xs[1]):
        arrived(quad(d, i, near), RX + 2 * i + near)
        to_sib(i, near)
    for i in ys:
        arrived(fown.at[zh * 4 + i], RT + 2 * (zh * 4 + i))
    for q in range(2):
        for i in ys:
            arrived(piece((1 - zh) * 4 + i, q), RT + 2 * ((1 - zh) * 4 + i) + q)
    for i in (xs[0], xs[2], xs[1]):
        arrived(quad(d, i, far), RX + 2 * i + far)
        to_sib(i, far)
    send(fown, fsib, RF, sib)
    for i in range(4):
        for g in range(2):
            arrived(quad(1 - d, i, g), RS + 2 * i + g)

    def wblock(core, j):
        return wb[core, 4 * j : 4 * j + 4].reshape(WID, WID)

    mm = ((1,), (0,))
    value = dot(fown[0], wblock(0, 0), mm)
    gate = dot(fown[0], wblock(1, 0), mm)
    for j in range(1, 8):
        value = value + dot(fown[j], wblock(0, j), mm)
        gate = gate + dot(fown[j], wblock(1, j), mm)
    upstream = cbuf[...].astype(F32)
    gm = upstream * gate

    for m in range(MODES):
        hi, lo = split(value * ep[m])
        s = dot(lower, hi, mm) + dot(lower, lo, mm)
        sloc[m] = s
        sb[0:1, m * WID : (m + 1) * WID] = s[SPAN - 1 :, :] * em[m, SPAN - 1 :, :]
        hi, lo = split(gm * wm[m : m + 1, :] * em[m])
        b = dot(upper, hi, mm) + dot(upper, lo, mm)
        bloc[m] = b
        sb[1:2, m * WID : (m + 1) * WID] = b[0:1, :]
    sh[...] = sb[...].astype(BF)
    zb[zl] = sh[...]
    for i in (zs[6], zs[0], zs[5], zs[1], zs[4], zs[2], zs[3]):
        send(sh, zb.at[zl], RE + zl, zdev(i))
    arrived(fsib, RF)
    for j in range(8):
        wt[j, 0:WID] = wblock(0, j).T
        wt[j, WID:] = wblock(1, j).T
        ft[j, :, 0:SPAN] = fown[j].T
        ft[j, :, SPAN:] = fsib[j].T
    for i in zs:
        arrived(zb.at[i], RE + i)
    for i in range(8):
        zf[i] = zb[i].astype(F32)
    fz, bz = zf[:, 0, :], zf[:, 1, :]
    xsb[0:1, :] = jnp.sum(w_tot_f * fz, axis=0, keepdims=True)
    xsb[1:2, :] = jnp.sum(w_tot_b * bz, axis=0, keepdims=True)
    xb[x] = xsb[...]
    for i in xs:
        send(xsb, xb.at[x], REX + x, xdev(i))
    inc_f = jnp.sum(w_in_f * fz, axis=0, keepdims=True)
    inc_b = jnp.sum(w_in_b * bz, axis=0, keepdims=True)
    for i in xs:
        arrived(xb.at[i], REX + i)
    inc_f = inc_f + jnp.sum(w_x_f * xb[:, 0, :], axis=0, keepdims=True)
    inc_b = inc_b + jnp.sum(w_x_b * xb[:, 1, :], axis=0, keepdims=True)
    inc_f = inc_f * step_f
    inc_b = inc_b * step_b

    sk = skip[...]
    mixed = sk * value
    gval = sk * gm
    pairs, carries = [], []
    for m in range(MODES):
        lanes = slice(m * WID, (m + 1) * WID)
        state = em[m] * (sloc[m] + clearf * inc_f[:, lanes])
        gst = ep[m] * (bloc[m] + clearb * inc_b[:, lanes])
        mixed = mixed + wm[m : m + 1, :] * state
        gval = gval + gst
        pairs.append(jnp.sum(gm * state, axis=0, keepdims=True))
        carries.append(jnp.sum(gst * (state - value), axis=0, keepdims=True))
    stats = [jnp.sum(gm * value, axis=0, keepdims=True)] + pairs + carries
    stats = jnp.concatenate(stats, axis=1)
    stl[0] = stats[:, 0:NSTAT]
    stl[1] = stats[:, NSTAT:]
    out[0] = (gate * mixed).astype(BF)
    cv = gval.astype(BF)
    cg = (upstream * mixed).astype(BF)
    cb[0] = cv
    cb[1] = cg
    send(cb.at[1 - d], cs, RC, sib)
    send(stl.at[1 - d], sti, RQS, sib)

    both = jnp.concatenate([cv, cg], axis=1)

    def share(h, i):
        return dot(both, wt[h * 4 + i], mm).astype(BF)

    def rows(p):
        return slice(p * PART, (p + 1) * PART)

    def other_shares(p, sem):
        h = 1 - zh
        for i in (ys[1], ys[0], ys[2], y):
            part = dot(both[rows(p)], wt[h * 4 + i], mm).astype(BF)
            if i is y:
                pin[h, y, rows(p)] = part
                continue
            pout[h, i, rows(p)] = part
            src = pout.at[h, i, pl.ds(p * PART, PART)]
            dst = pin.at[h, y, pl.ds(p * PART, PART)]
            send(src, dst, sem + 4 * h + y, ydev(i))

    def other_sum(p, sem):
        h = 1 - zh
        for i in ys:
            arrived(pin.at[h, i, pl.ds(p * PART, PART)], sem + 4 * h + i)
        total = pin[h, 0, rows(p)].astype(F32)
        for k in range(1, 4):
            total = total + pin[h, k, rows(p)].astype(F32)
        pa_out[rows(p)] = total.astype(BF)
        cut = pl.ds(p * PART, PART)
        send(pa_out.at[cut], pa_in.at[cut], RPA if p == 0 else RPA2, anti)

    def own_shares():
        for i in (ys[1], ys[0], ys[2]):
            pout[zh, i] = share(zh, i)
            send(pout.at[zh, i], pin.at[zh, y], RP + 4 * zh + y, ydev(i))
        pin[zh, y] = share(zh, y)

    def own_sum():
        for i in ys:
            arrived(pin.at[zh, i], RP + 4 * zh + i)
        total = pin[zh, 0].astype(F32)
        for k in range(1, 4):
            total = total + pin[zh, k].astype(F32)
        return total

    right, left = xs[0], xs[2]

    def slab(h, i):
        return dot(ft[2 * i + h], cots, mm).reshape(4, 64, WID)

    def x_start(h):
        g = slab(h, xs[1]).astype(BF)
        gr_out[h, 0] = g[0:2]
        send(gr_out.at[h, 0], gr_in.at[h, 0], RR + 2 * h, xdev(right))
        gr_out[h, 1] = g[2:4]
        send(gr_out.at[h, 1], gr_in.at[h, 1], RR + 2 * h + 1, xdev(left))

    def x_direct(h):
        g = slab(h, right)
        gk[h, 0] = g[0:2]
        gd[h, 0] = g[2:4].astype(BF)
        send(gd.at[h, 0], gin.at[h, 0, 1], RG + 4 * h + 1, xdev(right))
        g = slab(h, left)
        gk[h, 1] = g[2:4]
        gd[h, 1] = g[0:2].astype(BF)
        send(gd.at[h, 1], gin.at[h, 1, 0], RG + 4 * h + 2, xdev(left))

    def x_relay(h):
        for side, who, part in ((0, right, 0), (1, left, 1)):
            arrived(gr_in.at[h, side], RR + 2 * h + side)
            gc[h, side] = (gk[h, side] + gr_in[h, side].astype(F32)).astype(BF)
            send(gc.at[h, side], gin.at[h, side, part], RG + 4 * h + 3 * side, xdev(who))

    def x_sum(h):
        for side in range(2):
            for part in range(2):
                arrived(gin.at[h, side, part], RG + 4 * h + 2 * side + part)
        for part in range(2):
            g = gown[h, 2 * part : 2 * part + 2]
            g = g + gin[h, 0, part].astype(F32) + gin[h, 1, part].astype(F32)
            mout[h, 2 * part : 2 * part + 2] = g.astype(BF)
        for i in (ms[1], ms[0], ms[2]):
            send(mout.at[h, i], min_.at[h, mate], RM + 4 * h + mate, mdev(i))

    def mates_sum(h):
        for i in ms:
            arrived(min_.at[h, i], RM + 4 * h + i)
        g = mout[h, mate].astype(F32)
        for i in ms:
            g = g + min_[h, i].astype(F32)
        return g

    other_shares(0, RP)
    arrived(sti, RQS)
    stx[x] = stl[d] + sti[...]
    for i in xs:
        send(stx.at[x], stx.at[x], RQX + x, xdev(i))
    arrived(cs, RC)
    cots = jnp.concatenate([cb[d], cs[...]], axis=0)
    x_start(far)
    other_shares(1, RP2)
    x_direct(far)
    x_start(near)
    own_shares()
    other_sum(0, RP)
    x_relay(far)
    x_direct(near)
    other_sum(1, RP2)
    for h in (far, near):
        gown[h] = slab(h, x)
    for i in xs:
        arrived(stx.at[i], RQX + i)
    stm[mate] = (stx[0] + stx[1]) + (stx[2] + stx[3])
    for i in ms:
        send(stm.at[mate], stm.at[mate], RQM + mate, mdev(i))
    x_relay(near)
    x_sum(far)
    x_sum(near)
    for i in ms:
        arrived(stm.at[i], RQM + i)
    stp[half] = (stm[0] + stm[1]) + (stm[2] + stm[3])
    bout[...] = mates_sum(far).astype(BF)
    send(bout, bin_, RB, partner)
    send(stp.at[half], stp.at[half], RQP, partner)
    kept = own_sum()
    g = mates_sum(near)
    arrived(stp.at[1 - half], RQP)
    tfin[d] = stp[0] + stp[1]
    send(tfin.at[d], tfin.at[d], RQ2, sib)

    arrived(bin_, RB)
    gfin[d] = g + bin_[...].astype(F32)
    send(gfin.at[d], gfin.at[d], RW2, sib)
    arrived(tfin.at[1 - d], RQ2)
    tot = jnp.concatenate([tfin[0], tfin[1]], axis=1)
    gskip[...] = tot[:, 0:WID]
    ratio = resid[...] * jnp.exp(-2.0 * rt) / factor
    for m in range(MODES):
        paired = tot[:, WID * (1 + m) : WID * (2 + m)]
        carried = tot[:, WID * (5 + m) : WID * (6 + m)]
        gres[m : m + 1, :] = factor[m : m + 1, :] * paired
        grate[m : m + 1, :] = ratio[m : m + 1, :] * paired - carried
    for p, sem in ((0, RPA), (1, RPA2)):
        arrived(pa_in.at[pl.ds(p * PART, PART)], sem)
    gtok[0] = (kept + pa_in[...].astype(F32)).astype(BF)
    arrived(gfin.at[1 - d], RW2)
    gwv[...] = gfin[0]
    gwg[...] = gfin[1]
    for cp in sends:
        cp.wait_send()


def one_minus_exp(a):
    term = a
    total = a
    for k in range(2, 8):
        term = term * (-a / k)
        total = total + term
    return total


def store(*refs):
    sem = refs[14]
    copies = [pltpu.make_async_copy(refs[k], refs[7 + k], sem.at[k]) for k in range(7)]
    for cp in copies:
        cp.start()
    for cp in copies:
        cp.wait()


def body(tokens, cotangent, w_value, w_gate, decay_rate, residue, skip_gain, contig_len):
    vm = pl.BlockSpec(memory_space=pltpu.VMEM)
    hbm = pl.BlockSpec(memory_space=pltpu.HBM)
    sds = jax.ShapeDtypeStruct
    shapes = (
        sds((1, SPAN, WID), BF),
        sds((1, SPAN, WID), BF),
        sds((64, WID), F32),
        sds((64, WID), F32),
        sds((1, WID), F32),
        sds((MODES, WID), F32),
        sds((MODES, WID), F32),
    )
    outs = pl.pallas_call(
        kernel,
        out_shape=shapes,
        in_specs=[hbm] * 8,
        out_specs=(vm,) * 7,
        scratch_shapes=[
            pltpu.VMEM((8, SPAN, WID), BF),
            pltpu.VMEM((8, SPAN, WID), BF),
            pltpu.VMEM((2, 32, 64, WID), BF),
            pltpu.VMEM((SPAN, WID), BF),
            pltpu.VMEM((MODES, SPAN, WID), F32),
            pltpu.VMEM((MODES, SPAN, WID), F32),
            pltpu.VMEM((MODES, SPAN, WID), F32),
            pltpu.VMEM((MODES, SPAN, WID), F32),
            pltpu.VMEM((2, MODES * WID), F32),
            pltpu.VMEM((2, MODES * WID), BF),
            pltpu.VMEM((8, 2, MODES * WID), BF),
            pltpu.VMEM((8, 2, MODES * WID), F32),
            pltpu.VMEM((2, MODES * WID), F32),
            pltpu.VMEM((4, 2, MODES * WID), F32),
            pltpu.VMEM((2, SPAN, WID), BF),
            pltpu.VMEM((SPAN, WID), BF),
            pltpu.VMEM((2, 4, SPAN, WID), BF),
            pltpu.VMEM((2, 4, SPAN, WID), BF),
            pltpu.VMEM((SPAN, WID), BF),
            pltpu.VMEM((SPAN, WID), BF),
            pltpu.VMEM((2, 2, 2, 64, WID), BF),
            pltpu.VMEM((2, 2, 2, 64, WID), BF),
            pltpu.VMEM((2, 2, 2, 64, WID), F32),
            pltpu.VMEM((2, 2, 2, 64, WID), BF),
            pltpu.VMEM((2, 2, 2, 64, WID), BF),
            pltpu.VMEM((2, 2, 2, 2, 64, WID), BF),
            pltpu.VMEM((2, 4, 64, WID), F32),
            pltpu.VMEM((2, 4, 64, WID), BF),
            pltpu.VMEM((2, 4, 64, WID), BF),
            pltpu.VMEM((64, WID), BF),
            pltpu.VMEM((64, WID), BF),
            pltpu.VMEM((2, 64, WID), F32),
            pltpu.VMEM((8, 2 * WID, WID), BF),
            pltpu.VMEM((8, WID, 2 * SPAN), BF),
            pltpu.VMEM((2, 1, NSTAT), F32),
            pltpu.VMEM((1, NSTAT), F32),
            pltpu.VMEM((4, 1, NSTAT), F32),
            pltpu.VMEM((4, 1, NSTAT), F32),
            pltpu.VMEM((2, 1, NSTAT), F32),
            pltpu.VMEM((2, 1, NSTAT), F32),
            pltpu.VMEM((MODES, WID), F32),
            pltpu.VMEM((MODES, WID), F32),
            pltpu.VMEM((1, WID), F32),
            pltpu.SMEM((1, 8), jnp.int32),
            pltpu.SemaphoreType.DMA((NSEND,)),
            pltpu.SemaphoreType.DMA((NRECV,)),
            pltpu.SemaphoreType.DMA((7,)),
        ],
        compiler_params=pltpu.CompilerParams(
            collective_id=0, has_side_effects=True, vmem_limit_bytes=67043328
        ),
        name="step",
    )(
        tokens, cotangent, w_value, w_gate, decay_rate, residue,
        skip_gain.reshape(1, WID), contig_len,
    )
    outs = pl.pallas_call(
        store,
        out_shape=shapes,
        in_specs=[vm] * 7,
        out_specs=(hbm,) * 7,
        scratch_shapes=[pltpu.SemaphoreType.DMA((7,))],
        name="store",
    )(*outs)
    outs = list(outs)
    outs[4] = outs[4].reshape(WID)
    return tuple(outs)


def solution(mesh):
    in_specs = (
        P("dp", "ctx", "tensor"),
        P("dp", "ctx", "tensor"),
        P("ctx", "tensor"),
        P("ctx", "tensor"),
        P(None, "tensor"),
        P(None, "tensor"),
        P("tensor"),
        P("dp", None),
    )
    out_specs = (
        P("dp", "ctx", "tensor"),
        P("dp", "ctx", "tensor"),
        P("ctx", "tensor"),
        P("ctx", "tensor"),
        P("tensor"),
        P(None, "tensor"),
        P(None, "tensor"),
    )
    return jax.shard_map(body, mesh=mesh, in_specs=in_specs, out_specs=out_specs, check_vma=False)
```

```python
import jax
import jax.numpy as jnp
from jax import lax
from jax.experimental import pallas as pl
from jax.experimental.pallas import tpu as pltpu
from jax.sharding import PartitionSpec as P

MESH = pl.DeviceIdType.MESH
F32 = jnp.float32
BF = jnp.bfloat16
SPAN = 128
WID = 256
MODES = 4
LINE = 8 * SPAN
NSTAT = 9 * WID // 2
PART = SPAN // 2

RT, RZ, RX, RS, RF = 0, 16, 24, 32, 40
RE, REX, RC, RP, RPA = 41, 49, 53, 54, 62
RG, RR, RM, RB, RW2 = 63, 71, 75, 83, 84
RQS, RQX, RQM, RQP, RQ2 = 85, 86, 90, 94, 95
RP2, RPA2 = 96, 104
NRECV = 105
NSEND = 140


def dot(a, b, dims):
    return lax.dot_general(a, b, (dims, ((), ())), preferred_element_type=F32)


def split(u):
    hi = u.astype(BF)
    lo = (u - hi.astype(F32)).astype(BF)
    return hi, lo


def kernel(
    tok, cot, wv, wg, rate_h, resid_h, skip_h, clen_h,
    out, gtok, gwv, gwg, gskip, gres, grate,
    fown, fsib, wb, cbuf, ep, em, sloc, bloc, sb, sh, zb, wtot, win, wx, xsb, xb,
    cb, cs, pout, pin, pa_out, pa_in, gr_out, gr_in, gk, gd, gc, gin, gown,
    mout, min_, bout, bin_, gfin, wt, ft, stl, sti, stx, stm, stp, tfin, rate, resid, skip, clen, ssem, rsem, lsem,
):
    d = lax.axis_index("dp")
    c = lax.axis_index("ctx")
    t = lax.axis_index("tensor")
    x, zl = c // 8, c % 8
    zh, y = t // 4, t % 4
    half, mate = zl // 4, zl % 4

    sib = {"dp": 1 - d}
    anti = {"tensor": (1 - zh) * 4 + y}
    partner = {"ctx": x * 8 + (1 - half) * 4 + mate}
    ys = [lax.rem(y + i, 4) for i in (1, 2, 3)]
    xs = [lax.rem(x + i, 4) for i in (1, 2, 3)]
    zs = [lax.rem(zl + i, 8) for i in range(1, 8)]
    ms = [lax.rem(mate + i, 4) for i in (1, 2, 3)]

    def ydev(k):
        return {"tensor": zh * 4 + k}

    def xdev(k):
        return {"ctx": k * 8 + zl}

    def zdev(k):
        return {"ctx": x * 8 + k}

    def mdev(k):
        return {"ctx": x * 8 + half * 4 + k}

    loads = [
        pltpu.make_async_copy(tok.at[0], fown.at[t], lsem.at[0]),
        pltpu.make_async_copy(cot.at[0], cbuf, lsem.at[1]),
    ]
    small = [
        pltpu.make_async_copy(rate_h, rate, lsem.at[3]),
        pltpu.make_async_copy(resid_h, resid, lsem.at[4]),
        pltpu.make_async_copy(skip_h, skip, lsem.at[5]),
        pltpu.make_async_copy(clen_h, clen, lsem.at[6]),
    ]
    for cp in small + loads:
        cp.start()

    @pl.when(d == 0)
    def _():
        pltpu.make_async_copy(wv, wb.at[0, c], lsem.at[2]).start()

    @pl.when(d == 1)
    def _():
        pltpu.make_async_copy(wg, wb.at[1, c], lsem.at[2]).start()

    barrier = pltpu.get_barrier_semaphore()
    peers = (
        [sib, anti]
        + [ydev(k) for k in ys]
        + [xdev(k) for k in xs]
        + [zdev(k) for k in zs]
    )
    for who in peers:
        pl.semaphore_signal(barrier, inc=1, device_id=who, device_id_type=MESH)

    for cp in small:
        cp.wait()
    first = c * SPAN
    starts = [jnp.int32(0)]
    for k in range(7):
        starts.append(starts[-1] + clen[0, k])

    def seg(pos):
        total = (pos >= starts[0]).astype(jnp.int32)
        for s in starts[1:]:
            total = total + (pos >= s).astype(jnp.int32)
        return total

    def row(a):
        return jnp.concatenate([a[m : m + 1, :] for m in range(MODES)], axis=1)

    rt = rate[...]
    factor = jnp.sqrt(one_minus_exp(2.0 * rt))
    wm = resid[...] * factor
    r1 = row(rt)
    tcol = lax.broadcasted_iota(jnp.int32, (SPAN, WID), 0).astype(F32)
    for m in range(MODES):
        rm = rt[m : m + 1, :]
        ep[m] = jnp.exp(rm * tcol)
        em[m] = jnp.exp(-rm * tcol)
    ri = lax.broadcasted_iota(jnp.int32, (SPAN, SPAN), 0)
    ci = lax.broadcasted_iota(jnp.int32, (SPAN, SPAN), 1)
    sr, sc = seg(first + ri), seg(first + ci)
    lower = jnp.where((sr == sc) & (ci <= ri), 1.0, 0.0).astype(BF)
    upper = jnp.where((sr == sc) & (ci >= ri), 1.0, 0.0).astype(BF)
    seg_prev, seg_next = seg(first - 1), seg(first + SPAN)
    stc = seg(first + lax.broadcasted_iota(jnp.int32, (SPAN, WID), 0))
    clearf = jnp.where(stc == seg_prev, 1.0, 0.0)
    clearb = jnp.where(stc == seg_next, 1.0, 0.0)

    back = lax.broadcasted_iota(jnp.int32, (2, MODES * WID), 0) == 1
    base = x * LINE

    def weight(source, target, later_ok, earlier_ok):
        dist = jnp.where(back, source[1] - target[1], target[0] - source[0])
        ok_f = earlier_ok & (seg(source[0]) == seg(target[0]))
        ok_b = later_ok & (seg(source[1]) == seg(target[1]))
        scale = jnp.exp(-r1 * jnp.maximum(dist, 0).astype(F32))
        keep = jnp.where(back, ok_b.astype(F32), ok_f.astype(F32))
        return scale * keep

    yes = c >= 0
    here = (first - 1, first + SPAN)
    for k in range(8):
        ends = (base + SPAN * k + SPAN - 1, base + SPAN * k)
        wtot[k] = weight(ends, (base + LINE - 1, base), yes, yes)
        win[k] = weight(ends, here, k > zl, k < zl)
    for k in range(4):
        ends = ((k + 1) * LINE - 1, k * LINE)
        wx[k] = weight(ends, here, k > x, k < x)
    step2 = jnp.exp(-r1 * jnp.where(back, float(SPAN), 1.0))

    sends = []

    def send(src, dst, recv, who):
        cp = pltpu.make_async_remote_copy(
            src_ref=src,
            dst_ref=dst,
            send_sem=ssem.at[len(sends)],
            recv_sem=rsem.at[recv],
            device_id=who,
            device_id_type=MESH,
        )
        cp.start()
        sends.append(cp)

    def arrived(ref, recv):
        pltpu.make_async_copy(ref, ref, rsem.at[recv]).wait()

    for cp in loads:
        cp.wait()
    pltpu.make_async_copy(wv, wb.at[d, c], lsem.at[2]).wait()
    pl.semaphore_wait(barrier, len(peers))

    def spread_x(k):
        for i in (xs[1], xs[0], xs[2]):
            send(wb.at[d, x * 8 + k], wb.at[d, x * 8 + k], RX + 2 * x + k // 4, xdev(i))

    def quad(core, k, g):
        return wb.at[core, pl.ds(k * 8 + 4 * g, 4)]

    def to_sib(k, g):
        send(quad(d, k, g), quad(d, k, g), RS + 2 * k + g, sib)

    near, far = half, 1 - half
    def piece(j, q):
        return fown.at[j, pl.ds(q * (SPAN // 2), SPAN // 2)]

    send(wb.at[d, c], wb.at[d, c], RZ + zl, partner)
    for i in (ms[1], ms[0], ms[2]):
        send(wb.at[d, c], wb.at[d, c], RZ + zl, mdev(i))
    for q in range(2):
        send(piece(t, q), piece(t, q), RT + 2 * t + q, anti)
    spread_x(zl)
    for i in ys:
        send(fown.at[t], fown.at[t], RT + 2 * t, ydev(i))
    for i in ms:
        k = near * 4 + i
        arrived(wb.at[d, x * 8 + k], RZ + k)
        spread_x(k)
    to_sib(x, near)
    k = far * 4 + mate
    arrived(wb.at[d, x * 8 + k], RZ + k)
    for i in (ms[1], ms[0], ms[2]):
        send(wb.at[d, x * 8 + k], wb.at[d, x * 8 + k], RZ + k, mdev(i))
    spread_x(k)
    ta = (1 - zh) * 4 + y

    def tokens_on(q):
        arrived(piece(ta, q), RT + 2 * ta + q)
        for i in ys:
            send(piece(ta, q), piece(ta, q), RT + 2 * ta + q, ydev(i))

    tokens_on(0)
    for i in ms:
        k = far * 4 + i
        arrived(wb.at[d, x * 8 + k], RZ + k)
        spread_x(k)
    to_sib(x, far)
    tokens_on(1)
    for i in (xs[0], xs[2], xs[1]):
        arrived(quad(d, i, near), RX + 2 * i + near)
        to_sib(i, near)
    for i in ys:
        arrived(fown.at[zh * 4 + i], RT + 2 * (zh * 4 + i))
    for q in range(2):
        for i in ys:
            arrived(piece((1 - zh) * 4 + i, q), RT + 2 * ((1 - zh) * 4 + i) + q)
    for i in (xs[0], xs[2], xs[1]):
        arrived(quad(d, i, far), RX + 2 * i + far)
        to_sib(i, far)
    send(fown, fsib, RF, sib)
    for i in range(4):
        for g in range(2):
            arrived(quad(1 - d, i, g), RS + 2 * i + g)

    def wblock(core, j):
        return wb[core, 4 * j : 4 * j + 4].reshape(WID, WID)

    mm = ((1,), (0,))
    value = dot(fown[0], wblock(0, 0), mm)
    gate = dot(fown[0], wblock(1, 0), mm)
    for j in range(1, 8):
        value = value + dot(fown[j], wblock(0, j), mm)
        gate = gate + dot(fown[j], wblock(1, j), mm)
    upstream = cbuf[...].astype(F32)
    gm = upstream * gate

    for m in range(MODES):
        hi, lo = split(value * ep[m])
        s = dot(lower, hi, mm) + dot(lower, lo, mm)
        sloc[m] = s
        sb[0:1, m * WID : (m + 1) * WID] = s[SPAN - 1 :, :] * em[m, SPAN - 1 :, :]
        hi, lo = split(gm * wm[m : m + 1, :] * em[m])
        b = dot(upper, hi, mm) + dot(upper, lo, mm)
        bloc[m] = b
        sb[1:2, m * WID : (m + 1) * WID] = b[0:1, :]
    sh[...] = sb[...].astype(BF)
    zb[zl] = sh[...]
    for i in (zs[6], zs[0], zs[5], zs[1], zs[4], zs[2], zs[3]):
        send(sh, zb.at[zl], RE + zl, zdev(i))
    arrived(fsib, RF)
    for j in range(8):
        wt[j, 0:WID] = wblock(0, j).T
        wt[j, WID:] = wblock(1, j).T
        ft[j, :, 0:SPAN] = fown[j].T
        ft[j, :, SPAN:] = fsib[j].T
    for i in zs:
        arrived(zb.at[i], RE + i)
    total = wtot[0] * zb[0].astype(F32)
    for k in range(1, 8):
        total = total + wtot[k] * zb[k].astype(F32)
    xsb[...] = total
    xb[x] = total
    for i in (xs[1], xs[0], xs[2]):
        send(xsb, xb.at[x], REX + x, xdev(i))
    inc = win[0] * zb[0].astype(F32)
    for k in range(1, 8):
        inc = inc + win[k] * zb[k].astype(F32)
    for i in xs:
        arrived(xb.at[i], REX + i)
    for k in range(4):
        inc = inc + wx[k] * xb[k]
    inc = inc * step2
    inc_f, inc_b = inc[0:1, :], inc[1:2, :]

    sk = skip[...]
    mixed = sk * value
    gval = sk * gm
    pairs, carries = [], []
    for m in range(MODES):
        lanes = slice(m * WID, (m + 1) * WID)
        state = em[m] * (sloc[m] + clearf * inc_f[:, lanes])
        gst = ep[m] * (bloc[m] + clearb * inc_b[:, lanes])
        mixed = mixed + wm[m : m + 1, :] * state
        gval = gval + gst
        pairs.append(jnp.sum(gm * state, axis=0, keepdims=True))
        carries.append(jnp.sum(gst * (state - value), axis=0, keepdims=True))
    stats = [jnp.sum(gm * value, axis=0, keepdims=True)] + pairs + carries
    stats = jnp.concatenate(stats, axis=1)
    stl[0] = stats[:, 0:NSTAT]
    stl[1] = stats[:, NSTAT:]
    out[0] = (gate * mixed).astype(BF)
    cv = gval.astype(BF)
    cg = (upstream * mixed).astype(BF)
    cb[0] = cv
    cb[1] = cg
    send(cb.at[1 - d], cs, RC, sib)
    send(stl.at[1 - d], sti, RQS, sib)

    both = jnp.concatenate([cv, cg], axis=1)

    def share(h, i):
        return dot(both, wt[h * 4 + i], mm).astype(BF)

    def rows(p):
        return slice(p * PART, (p + 1) * PART)

    def other_shares(p, sem):
        h = 1 - zh
        for i in (ys[1], ys[0], ys[2], y):
            part = dot(both[rows(p)], wt[h * 4 + i], mm).astype(BF)
            if i is y:
                pin[h, y, rows(p)] = part
                continue
            pout[h, i, rows(p)] = part
            src = pout.at[h, i, pl.ds(p * PART, PART)]
            dst = pin.at[h, y, pl.ds(p * PART, PART)]
            send(src, dst, sem + 4 * h + y, ydev(i))

    def other_sum(p, sem):
        h = 1 - zh
        for i in ys:
            arrived(pin.at[h, i, pl.ds(p * PART, PART)], sem + 4 * h + i)
        total = pin[h, 0, rows(p)].astype(F32)
        for k in range(1, 4):
            total = total + pin[h, k, rows(p)].astype(F32)
        pa_out[rows(p)] = total.astype(BF)
        cut = pl.ds(p * PART, PART)
        send(pa_out.at[cut], pa_in.at[cut], RPA if p == 0 else RPA2, anti)

    def own_shares():
        for i in (ys[1], ys[0], ys[2]):
            pout[zh, i] = share(zh, i)
            send(pout.at[zh, i], pin.at[zh, y], RP + 4 * zh + y, ydev(i))
        pin[zh, y] = share(zh, y)

    def own_sum():
        for i in ys:
            arrived(pin.at[zh, i], RP + 4 * zh + i)
        total = pin[zh, 0].astype(F32)
        for k in range(1, 4):
            total = total + pin[zh, k].astype(F32)
        return total

    right, left = xs[0], xs[2]

    def slab(h, i):
        return dot(ft[2 * i + h], cots, mm).reshape(4, 64, WID)

    def x_start(h):
        g = slab(h, xs[1]).astype(BF)
        gr_out[h, 0] = g[0:2]
        send(gr_out.at[h, 0], gr_in.at[h, 0], RR + 2 * h, xdev(right))
        gr_out[h, 1] = g[2:4]
        send(gr_out.at[h, 1], gr_in.at[h, 1], RR + 2 * h + 1, xdev(left))

    def x_direct(h):
        g = slab(h, right)
        gk[h, 0] = g[0:2]
        gd[h, 0] = g[2:4].astype(BF)
        send(gd.at[h, 0], gin.at[h, 0, 1], RG + 4 * h + 1, xdev(right))
        g = slab(h, left)
        gk[h, 1] = g[2:4]
        gd[h, 1] = g[0:2].astype(BF)
        send(gd.at[h, 1], gin.at[h, 1, 0], RG + 4 * h + 2, xdev(left))

    def x_relay(h):
        for side, who, part in ((0, right, 0), (1, left, 1)):
            arrived(gr_in.at[h, side], RR + 2 * h + side)
            gc[h, side] = (gk[h, side] + gr_in[h, side].astype(F32)).astype(BF)
            send(gc.at[h, side], gin.at[h, side, part], RG + 4 * h + 3 * side, xdev(who))

    def x_sum(h):
        for side in range(2):
            for part in range(2):
                arrived(gin.at[h, side, part], RG + 4 * h + 2 * side + part)
        for part in range(2):
            g = gown[h, 2 * part : 2 * part + 2]
            g = g + gin[h, 0, part].astype(F32) + gin[h, 1, part].astype(F32)
            mout[h, 2 * part : 2 * part + 2] = g.astype(BF)
        for i in (ms[1], ms[0], ms[2]):
            send(mout.at[h, i], min_.at[h, mate], RM + 4 * h + mate, mdev(i))

    def mates_sum(h):
        for i in ms:
            arrived(min_.at[h, i], RM + 4 * h + i)
        g = mout[h, mate].astype(F32)
        for i in ms:
            g = g + min_[h, i].astype(F32)
        return g

    other_shares(0, RP)
    arrived(sti, RQS)
    stx[x] = stl[d] + sti[...]
    for i in xs:
        send(stx.at[x], stx.at[x], RQX + x, xdev(i))
    arrived(cs, RC)
    cots = jnp.concatenate([cb[d], cs[...]], axis=0)
    x_start(far)
    other_shares(1, RP2)
    x_direct(far)
    x_start(near)
    own_shares()
    other_sum(0, RP)
    x_relay(far)
    x_direct(near)
    other_sum(1, RP2)
    for h in (far, near):
        gown[h] = slab(h, x)
    for i in xs:
        arrived(stx.at[i], RQX + i)
    stm[mate] = (stx[0] + stx[1]) + (stx[2] + stx[3])
    for i in ms:
        send(stm.at[mate], stm.at[mate], RQM + mate, mdev(i))
    x_relay(near)
    x_sum(far)
    x_sum(near)
    for i in ms:
        arrived(stm.at[i], RQM + i)
    stp[half] = (stm[0] + stm[1]) + (stm[2] + stm[3])
    send(stp.at[half], stp.at[half], RQP, partner)
    bout[...] = mates_sum(far).astype(BF)
    send(bout, bin_, RB, partner)
    kept = own_sum()
    g = mates_sum(near)
    arrived(stp.at[1 - half], RQP)
    tfin[d] = stp[0] + stp[1]
    send(tfin.at[d], tfin.at[d], RQ2, sib)

    arrived(bin_, RB)
    gfin[d] = g + bin_[...].astype(F32)
    send(gfin.at[d], gfin.at[d], RW2, sib)
    arrived(tfin.at[1 - d], RQ2)
    tot = jnp.concatenate([tfin[0], tfin[1]], axis=1)
    gskip[...] = tot[:, 0:WID]
    ratio = resid[...] * jnp.exp(-2.0 * rt) / factor
    for m in range(MODES):
        paired = tot[:, WID * (1 + m) : WID * (2 + m)]
        carried = tot[:, WID * (5 + m) : WID * (6 + m)]
        gres[m : m + 1, :] = factor[m : m + 1, :] * paired
        grate[m : m + 1, :] = ratio[m : m + 1, :] * paired - carried
    for p, sem in ((0, RPA), (1, RPA2)):
        arrived(pa_in.at[pl.ds(p * PART, PART)], sem)
    gtok[0] = (kept + pa_in[...].astype(F32)).astype(BF)
    arrived(gfin.at[1 - d], RW2)
    gwv[...] = gfin[0]
    gwg[...] = gfin[1]
    for cp in sends:
        cp.wait_send()


def one_minus_exp(a):
    term = a
    total = a
    for k in range(2, 8):
        term = term * (-a / k)
        total = total + term
    return total


def store(*refs):
    sem = refs[14]
    copies = [pltpu.make_async_copy(refs[k], refs[7 + k], sem.at[k]) for k in range(7)]
    for cp in copies:
        cp.start()
    for cp in copies:
        cp.wait()


def body(tokens, cotangent, w_value, w_gate, decay_rate, residue, skip_gain, contig_len):
    vm = pl.BlockSpec(memory_space=pltpu.VMEM)
    hbm = pl.BlockSpec(memory_space=pltpu.HBM)
    sds = jax.ShapeDtypeStruct
    shapes = (
        sds((1, SPAN, WID), BF),
        sds((1, SPAN, WID), BF),
        sds((64, WID), F32),
        sds((64, WID), F32),
        sds((1, WID), F32),
        sds((MODES, WID), F32),
        sds((MODES, WID), F32),
    )
    outs = pl.pallas_call(
        kernel,
        out_shape=shapes,
        in_specs=[hbm] * 8,
        out_specs=(vm,) * 7,
        scratch_shapes=[
            pltpu.VMEM((8, SPAN, WID), BF),
            pltpu.VMEM((8, SPAN, WID), BF),
            pltpu.VMEM((2, 32, 64, WID), BF),
            pltpu.VMEM((SPAN, WID), BF),
            pltpu.VMEM((MODES, SPAN, WID), F32),
            pltpu.VMEM((MODES, SPAN, WID), F32),
            pltpu.VMEM((MODES, SPAN, WID), F32),
            pltpu.VMEM((MODES, SPAN, WID), F32),
            pltpu.VMEM((2, MODES * WID), F32),
            pltpu.VMEM((2, MODES * WID), BF),
            pltpu.VMEM((8, 2, MODES * WID), BF),
            pltpu.VMEM((8, 2, MODES * WID), F32),
            pltpu.VMEM((8, 2, MODES * WID), F32),
            pltpu.VMEM((4, 2, MODES * WID), F32),
            pltpu.VMEM((2, MODES * WID), F32),
            pltpu.VMEM((4, 2, MODES * WID), F32),
            pltpu.VMEM((2, SPAN, WID), BF),
            pltpu.VMEM((SPAN, WID), BF),
            pltpu.VMEM((2, 4, SPAN, WID), BF),
            pltpu.VMEM((2, 4, SPAN, WID), BF),
            pltpu.VMEM((SPAN, WID), BF),
            pltpu.VMEM((SPAN, WID), BF),
            pltpu.VMEM((2, 2, 2, 64, WID), BF),
            pltpu.VMEM((2, 2, 2, 64, WID), BF),
            pltpu.VMEM((2, 2, 2, 64, WID), F32),
            pltpu.VMEM((2, 2, 2, 64, WID), BF),
            pltpu.VMEM((2, 2, 2, 64, WID), BF),
            pltpu.VMEM((2, 2, 2, 2, 64, WID), BF),
            pltpu.VMEM((2, 4, 64, WID), F32),
            pltpu.VMEM((2, 4, 64, WID), BF),
            pltpu.VMEM((2, 4, 64, WID), BF),
            pltpu.VMEM((64, WID), BF),
            pltpu.VMEM((64, WID), BF),
            pltpu.VMEM((2, 64, WID), F32),
            pltpu.VMEM((8, 2 * WID, WID), BF),
            pltpu.VMEM((8, WID, 2 * SPAN), BF),
            pltpu.VMEM((2, 1, NSTAT), F32),
            pltpu.VMEM((1, NSTAT), F32),
            pltpu.VMEM((4, 1, NSTAT), F32),
            pltpu.VMEM((4, 1, NSTAT), F32),
            pltpu.VMEM((2, 1, NSTAT), F32),
            pltpu.VMEM((2, 1, NSTAT), F32),
            pltpu.VMEM((MODES, WID), F32),
            pltpu.VMEM((MODES, WID), F32),
            pltpu.VMEM((1, WID), F32),
            pltpu.SMEM((1, 8), jnp.int32),
            pltpu.SemaphoreType.DMA((NSEND,)),
            pltpu.SemaphoreType.DMA((NRECV,)),
            pltpu.SemaphoreType.DMA((7,)),
        ],
        compiler_params=pltpu.CompilerParams(
            collective_id=0, has_side_effects=True, vmem_limit_bytes=67043328
        ),
        name="step",
    )(
        tokens, cotangent, w_value, w_gate, decay_rate, residue,
        skip_gain.reshape(1, WID), contig_len,
    )
    outs = pl.pallas_call(
        store,
        out_shape=shapes,
        in_specs=[vm] * 7,
        out_specs=(hbm,) * 7,
        scratch_shapes=[pltpu.SemaphoreType.DMA((7,))],
        name="store",
    )(*outs)
    outs = list(outs)
    outs[4] = outs[4].reshape(WID)
    return tuple(outs)


def solution(mesh):
    in_specs = (
        P("dp", "ctx", "tensor"),
        P("dp", "ctx", "tensor"),
        P("ctx", "tensor"),
        P("ctx", "tensor"),
        P(None, "tensor"),
        P(None, "tensor"),
        P("tensor"),
        P("dp", None),
    )
    out_specs = (
        P("dp", "ctx", "tensor"),
        P("dp", "ctx", "tensor"),
        P("ctx", "tensor"),
        P("ctx", "tensor"),
        P("tensor"),
        P(None, "tensor"),
        P(None, "tensor"),
    )
    return jax.shard_map(body, mesh=mesh, in_specs=in_specs, out_specs=out_specs, check_vma=False)
```

```python
import jax
import jax.numpy as jnp
from jax import lax
from jax.experimental import pallas as pl
from jax.experimental.pallas import tpu as pltpu
from jax.sharding import PartitionSpec as P

MESH = pl.DeviceIdType.MESH
F32 = jnp.float32
BF = jnp.bfloat16
SPAN = 128
WID = 256
MODES = 4
LINE = 8 * SPAN
NSTAT = 9 * WID // 2
PART = SPAN // 2

RT, RZ, RX, RS, RF = 0, 16, 24, 32, 40
RE, REX, RC, RP, RPA = 41, 49, 53, 54, 62
RG, RR, RM, RB, RW2 = 63, 71, 75, 83, 84
RQS, RQX, RQM, RQP, RQ2 = 85, 86, 90, 94, 95
RP2, RPA2 = 96, 104
RM2, RB2 = 105, 109
NRECV = 110
NSEND = 144


def dot(a, b, dims):
    return lax.dot_general(a, b, (dims, ((), ())), preferred_element_type=F32)


def split(u):
    hi = u.astype(BF)
    lo = (u - hi.astype(F32)).astype(BF)
    return hi, lo


def kernel(
    tok, cot, wv, wg, rate_h, resid_h, skip_h, clen_h,
    out, gtok, gwv, gwg, gskip, gres, grate,
    fown, fsib, wb, cbuf, ep, em, sloc, bloc, sb, sh, zb, wtot, win, wx, xsb, xb,
    cb, cs, pout, pin, pa_out, pa_in, gr_out, gr_in, gk, gd, gc, gin, gown,
    mout, min_, bout, bin_, gfin, wt, ft, stl, sti, stx, stm, stp, tfin, rate, resid, skip, clen, ssem, rsem, lsem,
):
    d = lax.axis_index("dp")
    c = lax.axis_index("ctx")
    t = lax.axis_index("tensor")
    x, zl = c // 8, c % 8
    zh, y = t // 4, t % 4
    half, mate = zl // 4, zl % 4

    sib = {"dp": 1 - d}
    anti = {"tensor": (1 - zh) * 4 + y}
    partner = {"ctx": x * 8 + (1 - half) * 4 + mate}
    ys = [lax.rem(y + i, 4) for i in (1, 2, 3)]
    xs = [lax.rem(x + i, 4) for i in (1, 2, 3)]
    zs = [lax.rem(zl + i, 8) for i in range(1, 8)]
    ms = [lax.rem(mate + i, 4) for i in (1, 2, 3)]

    def ydev(k):
        return {"tensor": zh * 4 + k}

    def xdev(k):
        return {"ctx": k * 8 + zl}

    def zdev(k):
        return {"ctx": x * 8 + k}

    def mdev(k):
        return {"ctx": x * 8 + half * 4 + k}

    loads = [
        pltpu.make_async_copy(tok.at[0], fown.at[t], lsem.at[0]),
        pltpu.make_async_copy(cot.at[0], cbuf, lsem.at[1]),
    ]
    small = [
        pltpu.make_async_copy(rate_h, rate, lsem.at[3]),
        pltpu.make_async_copy(resid_h, resid, lsem.at[4]),
        pltpu.make_async_copy(skip_h, skip, lsem.at[5]),
        pltpu.make_async_copy(clen_h, clen, lsem.at[6]),
    ]
    for cp in small + loads:
        cp.start()

    @pl.when(d == 0)
    def _():
        pltpu.make_async_copy(wv, wb.at[0, c], lsem.at[2]).start()

    @pl.when(d == 1)
    def _():
        pltpu.make_async_copy(wg, wb.at[1, c], lsem.at[2]).start()

    barrier = pltpu.get_barrier_semaphore()
    peers = (
        [sib, anti]
        + [ydev(k) for k in ys]
        + [xdev(k) for k in xs]
        + [zdev(k) for k in zs]
    )
    for who in peers:
        pl.semaphore_signal(barrier, inc=1, device_id=who, device_id_type=MESH)

    for cp in small:
        cp.wait()
    first = c * SPAN
    starts = [jnp.int32(0)]
    for k in range(7):
        starts.append(starts[-1] + clen[0, k])

    def seg(pos):
        total = (pos >= starts[0]).astype(jnp.int32)
        for s in starts[1:]:
            total = total + (pos >= s).astype(jnp.int32)
        return total

    def row(a):
        return jnp.concatenate([a[m : m + 1, :] for m in range(MODES)], axis=1)

    rt = rate[...]
    factor = jnp.sqrt(one_minus_exp(2.0 * rt))
    wm = resid[...] * factor
    r1 = row(rt)
    tcol = lax.broadcasted_iota(jnp.int32, (SPAN, WID), 0).astype(F32)
    for m in range(MODES):
        rm = rt[m : m + 1, :]
        ep[m] = jnp.exp(rm * tcol)
        em[m] = jnp.exp(-rm * tcol)
    ri = lax.broadcasted_iota(jnp.int32, (SPAN, SPAN), 0)
    ci = lax.broadcasted_iota(jnp.int32, (SPAN, SPAN), 1)
    sr, sc = seg(first + ri), seg(first + ci)
    lower = jnp.where((sr == sc) & (ci <= ri), 1.0, 0.0).astype(BF)
    upper = jnp.where((sr == sc) & (ci >= ri), 1.0, 0.0).astype(BF)
    seg_prev, seg_next = seg(first - 1), seg(first + SPAN)
    stc = seg(first + lax.broadcasted_iota(jnp.int32, (SPAN, WID), 0))
    clearf = jnp.where(stc == seg_prev, 1.0, 0.0)
    clearb = jnp.where(stc == seg_next, 1.0, 0.0)

    back = lax.broadcasted_iota(jnp.int32, (2, MODES * WID), 0) == 1
    base = x * LINE

    def weight(source, target, later_ok, earlier_ok):
        dist = jnp.where(back, source[1] - target[1], target[0] - source[0])
        ok_f = earlier_ok & (seg(source[0]) == seg(target[0]))
        ok_b = later_ok & (seg(source[1]) == seg(target[1]))
        scale = jnp.exp(-r1 * jnp.maximum(dist, 0).astype(F32))
        keep = jnp.where(back, ok_b.astype(F32), ok_f.astype(F32))
        return scale * keep

    yes = c >= 0
    here = (first - 1, first + SPAN)
    for k in range(8):
        ends = (base + SPAN * k + SPAN - 1, base + SPAN * k)
        wtot[k] = weight(ends, (base + LINE - 1, base), yes, yes)
        win[k] = weight(ends, here, k > zl, k < zl)
    for k in range(4):
        ends = ((k + 1) * LINE - 1, k * LINE)
        wx[k] = weight(ends, here, k > x, k < x)
    step2 = jnp.exp(-r1 * jnp.where(back, float(SPAN), 1.0))

    sends = []

    def send(src, dst, recv, who):
        cp = pltpu.make_async_remote_copy(
            src_ref=src,
            dst_ref=dst,
            send_sem=ssem.at[len(sends)],
            recv_sem=rsem.at[recv],
            device_id=who,
            device_id_type=MESH,
        )
        cp.start()
        sends.append(cp)

    def arrived(ref, recv):
        pltpu.make_async_copy(ref, ref, rsem.at[recv]).wait()

    for cp in loads:
        cp.wait()
    pltpu.make_async_copy(wv, wb.at[d, c], lsem.at[2]).wait()
    pl.semaphore_wait(barrier, len(peers))

    def spread_x(k):
        for i in (xs[1], xs[0], xs[2]):
            send(wb.at[d, x * 8 + k], wb.at[d, x * 8 + k], RX + 2 * x + k // 4, xdev(i))

    def quad(core, k, g):
        return wb.at[core, pl.ds(k * 8 + 4 * g, 4)]

    def to_sib(k, g):
        send(quad(d, k, g), quad(d, k, g), RS + 2 * k + g, sib)

    near, far = half, 1 - half
    def piece(j, q):
        return fown.at[j, pl.ds(q * (SPAN // 2), SPAN // 2)]

    send(wb.at[d, c], wb.at[d, c], RZ + zl, partner)
    for i in (ms[1], ms[0], ms[2]):
        send(wb.at[d, c], wb.at[d, c], RZ + zl, mdev(i))
    for q in range(2):
        send(piece(t, q), piece(t, q), RT + 2 * t + q, anti)
    spread_x(zl)
    for i in ys:
        send(fown.at[t], fown.at[t], RT + 2 * t, ydev(i))
    for i in ms:
        k = near * 4 + i
        arrived(wb.at[d, x * 8 + k], RZ + k)
        spread_x(k)
    to_sib(x, near)
    k = far * 4 + mate
    arrived(wb.at[d, x * 8 + k], RZ + k)
    for i in (ms[1], ms[0], ms[2]):
        send(wb.at[d, x * 8 + k], wb.at[d, x * 8 + k], RZ + k, mdev(i))
    spread_x(k)
    ta = (1 - zh) * 4 + y

    def tokens_on(q):
        arrived(piece(ta, q), RT + 2 * ta + q)
        for i in ys:
            send(piece(ta, q), piece(ta, q), RT + 2 * ta + q, ydev(i))

    tokens_on(0)
    for i in ms:
        k = far * 4 + i
        arrived(wb.at[d, x * 8 + k], RZ + k)
        spread_x(k)
    to_sib(x, far)
    tokens_on(1)
    for i in (xs[0], xs[2], xs[1]):
        arrived(quad(d, i, near), RX + 2 * i + near)
        to_sib(i, near)
    for i in ys:
        arrived(fown.at[zh * 4 + i], RT + 2 * (zh * 4 + i))
    for q in range(2):
        for i in ys:
            arrived(piece((1 - zh) * 4 + i, q), RT + 2 * ((1 - zh) * 4 + i) + q)
    for i in (xs[0], xs[2], xs[1]):
        arrived(quad(d, i, far), RX + 2 * i + far)
        to_sib(i, far)
    send(fown, fsib, RF, sib)
    for i in range(4):
        for g in range(2):
            arrived(quad(1 - d, i, g), RS + 2 * i + g)

    def wblock(core, j):
        return wb[core, 4 * j : 4 * j + 4].reshape(WID, WID)

    mm = ((1,), (0,))
    value = dot(fown[0], wblock(0, 0), mm)
    gate = dot(fown[0], wblock(1, 0), mm)
    for j in range(1, 8):
        value = value + dot(fown[j], wblock(0, j), mm)
        gate = gate + dot(fown[j], wblock(1, j), mm)
    upstream = cbuf[...].astype(F32)
    gm = upstream * gate

    for m in range(MODES):
        hi, lo = split(value * ep[m])
        s = dot(lower, hi, mm) + dot(lower, lo, mm)
        sloc[m] = s
        sb[0:1, m * WID : (m + 1) * WID] = s[SPAN - 1 :, :] * em[m, SPAN - 1 :, :]
        hi, lo = split(gm * wm[m : m + 1, :] * em[m])
        b = dot(upper, hi, mm) + dot(upper, lo, mm)
        bloc[m] = b
        sb[1:2, m * WID : (m + 1) * WID] = b[0:1, :]
    sh[...] = sb[...].astype(BF)
    zb[zl] = sh[...]
    for i in (zs[6], zs[0], zs[5], zs[1], zs[4], zs[2], zs[3]):
        send(sh, zb.at[zl], RE + zl, zdev(i))
    arrived(fsib, RF)
    for j in range(8):
        wt[j, 0:WID] = wblock(0, j).T
        wt[j, WID:] = wblock(1, j).T
        ft[j, :, 0:SPAN] = fown[j].T
        ft[j, :, SPAN:] = fsib[j].T
    for i in zs:
        arrived(zb.at[i], RE + i)
    total = wtot[0] * zb[0].astype(F32)
    for k in range(1, 8):
        total = total + wtot[k] * zb[k].astype(F32)
    xsb[...] = total
    xb[x] = total
    for i in (xs[1], xs[0], xs[2]):
        send(xsb, xb.at[x], REX + x, xdev(i))
    inc = win[0] * zb[0].astype(F32)
    for k in range(1, 8):
        inc = inc + win[k] * zb[k].astype(F32)
    for i in xs:
        arrived(xb.at[i], REX + i)
    for k in range(4):
        inc = inc + wx[k] * xb[k]
    inc = inc * step2
    inc_f, inc_b = inc[0:1, :], inc[1:2, :]

    sk = skip[...]
    mixed = sk * value
    gval = sk * gm
    pairs, carries = [], []
    for m in range(MODES):
        lanes = slice(m * WID, (m + 1) * WID)
        state = em[m] * (sloc[m] + clearf * inc_f[:, lanes])
        gst = ep[m] * (bloc[m] + clearb * inc_b[:, lanes])
        mixed = mixed + wm[m : m + 1, :] * state
        gval = gval + gst
        pairs.append(jnp.sum(gm * state, axis=0, keepdims=True))
        carries.append(jnp.sum(gst * (state - value), axis=0, keepdims=True))
    stats = [jnp.sum(gm * value, axis=0, keepdims=True)] + pairs + carries
    stats = jnp.concatenate(stats, axis=1)
    stl[0] = stats[:, 0:NSTAT]
    stl[1] = stats[:, NSTAT:]
    out[0] = (gate * mixed).astype(BF)
    cv = gval.astype(BF)
    cg = (upstream * mixed).astype(BF)
    cb[0] = cv
    cb[1] = cg
    send(cb.at[1 - d], cs, RC, sib)
    send(stl.at[1 - d], sti, RQS, sib)

    both = jnp.concatenate([cv, cg], axis=1)

    def share(h, i):
        return dot(both, wt[h * 4 + i], mm).astype(BF)

    def rows(p):
        return slice(p * PART, (p + 1) * PART)

    def other_shares(p, sem):
        h = 1 - zh
        for i in (ys[1], ys[0], ys[2], y):
            part = dot(both[rows(p)], wt[h * 4 + i], mm).astype(BF)
            if i is y:
                pin[h, y, rows(p)] = part
                continue
            pout[h, i, rows(p)] = part
            src = pout.at[h, i, pl.ds(p * PART, PART)]
            dst = pin.at[h, y, pl.ds(p * PART, PART)]
            send(src, dst, sem + 4 * h + y, ydev(i))

    def other_sum(p, sem):
        h = 1 - zh
        for i in ys:
            arrived(pin.at[h, i, pl.ds(p * PART, PART)], sem + 4 * h + i)
        total = pin[h, 0, rows(p)].astype(F32)
        for k in range(1, 4):
            total = total + pin[h, k, rows(p)].astype(F32)
        pa_out[rows(p)] = total.astype(BF)
        cut = pl.ds(p * PART, PART)
        send(pa_out.at[cut], pa_in.at[cut], RPA if p == 0 else RPA2, anti)

    def own_shares():
        for i in (ys[1], ys[0], ys[2]):
            pout[zh, i] = share(zh, i)
            send(pout.at[zh, i], pin.at[zh, y], RP + 4 * zh + y, ydev(i))
        pin[zh, y] = share(zh, y)

    def own_sum():
        for i in ys:
            arrived(pin.at[zh, i], RP + 4 * zh + i)
        total = pin[zh, 0].astype(F32)
        for k in range(1, 4):
            total = total + pin[zh, k].astype(F32)
        return total

    right, left = xs[0], xs[2]

    def slab(h, i):
        return dot(ft[2 * i + h], cots, mm).reshape(4, 64, WID)

    def x_start(h):
        g = slab(h, xs[1]).astype(BF)
        gr_out[h, 0] = g[0:2]
        send(gr_out.at[h, 0], gr_in.at[h, 0], RR + 2 * h, xdev(right))
        gr_out[h, 1] = g[2:4]
        send(gr_out.at[h, 1], gr_in.at[h, 1], RR + 2 * h + 1, xdev(left))

    def x_direct(h):
        g = slab(h, right)
        gk[h, 0] = g[0:2]
        gd[h, 0] = g[2:4].astype(BF)
        send(gd.at[h, 0], gin.at[h, 0, 1], RG + 4 * h + 1, xdev(right))
        g = slab(h, left)
        gk[h, 1] = g[2:4]
        gd[h, 1] = g[0:2].astype(BF)
        send(gd.at[h, 1], gin.at[h, 1, 0], RG + 4 * h + 2, xdev(left))

    def x_relay(h):
        for side, who, part in ((0, right, 0), (1, left, 1)):
            arrived(gr_in.at[h, side], RR + 2 * h + side)
            gc[h, side] = (gk[h, side] + gr_in[h, side].astype(F32)).astype(BF)
            send(gc.at[h, side], gin.at[h, side, part], RG + 4 * h + 3 * side, xdev(who))

    def x_sum(h):
        for side in range(2):
            for part in range(2):
                arrived(gin.at[h, side, part], RG + 4 * h + 2 * side + part)
        for part in range(2):
            g = gown[h, 2 * part : 2 * part + 2]
            g = g + gin[h, 0, part].astype(F32) + gin[h, 1, part].astype(F32)
            mout[h, 2 * part : 2 * part + 2] = g.astype(BF)
        if h is near:
            for i in (ms[1], ms[0], ms[2]):
                send(mout.at[h, i], min_.at[h, mate], RM + 4 * h + mate, mdev(i))
            return
        for r, sem in ((0, RM + 4 * h), (1, RM2)):
            for i in (ms[1], ms[0], ms[2]):
                cut = pl.ds(32 * r, 32)
                send(mout.at[h, i, cut], min_.at[h, mate, cut], sem + mate, mdev(i))

    def mates_near():
        for i in ms:
            arrived(min_.at[near, i], RM + 4 * near + i)
        g = mout[near, mate].astype(F32)
        for i in ms:
            g = g + min_[near, i].astype(F32)
        return g

    def mates_far(r, sem, out_sem):
        cut = slice(32 * r, 32 * r + 32)
        part = pl.ds(32 * r, 32)
        for i in ms:
            arrived(min_.at[far, i, part], sem + i)
        g = mout[far, mate, cut].astype(F32)
        for i in ms:
            g = g + min_[far, i, cut].astype(F32)
        bout[cut] = g.astype(BF)
        send(bout.at[part], bin_.at[part], out_sem, partner)

    other_shares(0, RP)
    arrived(sti, RQS)
    stx[x] = stl[d] + sti[...]
    for i in xs:
        send(stx.at[x], stx.at[x], RQX + x, xdev(i))
    arrived(cs, RC)
    cots = jnp.concatenate([cb[d], cs[...]], axis=0)
    x_start(far)
    other_shares(1, RP2)
    x_direct(far)
    x_start(near)
    own_shares()
    other_sum(0, RP)
    x_relay(far)
    x_direct(near)
    other_sum(1, RP2)
    for h in (far, near):
        gown[h] = slab(h, x)
    for i in xs:
        arrived(stx.at[i], RQX + i)
    stm[mate] = (stx[0] + stx[1]) + (stx[2] + stx[3])
    for i in ms:
        send(stm.at[mate], stm.at[mate], RQM + mate, mdev(i))
    x_relay(near)
    x_sum(far)
    x_sum(near)
    for i in ms:
        arrived(stm.at[i], RQM + i)
    stp[half] = (stm[0] + stm[1]) + (stm[2] + stm[3])
    send(stp.at[half], stp.at[half], RQP, partner)
    mates_far(0, RM + 4 * far, RB)
    mates_far(1, RM2, RB2)
    kept = own_sum()
    g = mates_near()
    arrived(stp.at[1 - half], RQP)
    tfin[d] = stp[0] + stp[1]
    send(tfin.at[d], tfin.at[d], RQ2, sib)

    arrived(bin_.at[pl.ds(0, 32)], RB)
    arrived(bin_.at[pl.ds(32, 32)], RB2)
    gfin[d] = g + bin_[...].astype(F32)
    send(gfin.at[d], gfin.at[d], RW2, sib)
    arrived(tfin.at[1 - d], RQ2)
    tot = jnp.concatenate([tfin[0], tfin[1]], axis=1)
    gskip[...] = tot[:, 0:WID]
    ratio = resid[...] * jnp.exp(-2.0 * rt) / factor
    for m in range(MODES):
        paired = tot[:, WID * (1 + m) : WID * (2 + m)]
        carried = tot[:, WID * (5 + m) : WID * (6 + m)]
        gres[m : m + 1, :] = factor[m : m + 1, :] * paired
        grate[m : m + 1, :] = ratio[m : m + 1, :] * paired - carried
    for p, sem in ((0, RPA), (1, RPA2)):
        arrived(pa_in.at[pl.ds(p * PART, PART)], sem)
    gtok[0] = (kept + pa_in[...].astype(F32)).astype(BF)
    arrived(gfin.at[1 - d], RW2)
    gwv[...] = gfin[0]
    gwg[...] = gfin[1]
    assert len(sends) <= NSEND
    for cp in sends:
        cp.wait_send()


def one_minus_exp(a):
    term = a
    total = a
    for k in range(2, 8):
        term = term * (-a / k)
        total = total + term
    return total


def store(*refs):
    sem = refs[14]
    copies = [pltpu.make_async_copy(refs[k], refs[7 + k], sem.at[k]) for k in range(7)]
    for cp in copies:
        cp.start()
    for cp in copies:
        cp.wait()


def body(tokens, cotangent, w_value, w_gate, decay_rate, residue, skip_gain, contig_len):
    vm = pl.BlockSpec(memory_space=pltpu.VMEM)
    hbm = pl.BlockSpec(memory_space=pltpu.HBM)
    sds = jax.ShapeDtypeStruct
    shapes = (
        sds((1, SPAN, WID), BF),
        sds((1, SPAN, WID), BF),
        sds((64, WID), F32),
        sds((64, WID), F32),
        sds((1, WID), F32),
        sds((MODES, WID), F32),
        sds((MODES, WID), F32),
    )
    outs = pl.pallas_call(
        kernel,
        out_shape=shapes,
        in_specs=[hbm] * 8,
        out_specs=(vm,) * 7,
        scratch_shapes=[
            pltpu.VMEM((8, SPAN, WID), BF),
            pltpu.VMEM((8, SPAN, WID), BF),
            pltpu.VMEM((2, 32, 64, WID), BF),
            pltpu.VMEM((SPAN, WID), BF),
            pltpu.VMEM((MODES, SPAN, WID), F32),
            pltpu.VMEM((MODES, SPAN, WID), F32),
            pltpu.VMEM((MODES, SPAN, WID), F32),
            pltpu.VMEM((MODES, SPAN, WID), F32),
            pltpu.VMEM((2, MODES * WID), F32),
            pltpu.VMEM((2, MODES * WID), BF),
            pltpu.VMEM((8, 2, MODES * WID), BF),
            pltpu.VMEM((8, 2, MODES * WID), F32),
            pltpu.VMEM((8, 2, MODES * WID), F32),
            pltpu.VMEM((4, 2, MODES * WID), F32),
            pltpu.VMEM((2, MODES * WID), F32),
            pltpu.VMEM((4, 2, MODES * WID), F32),
            pltpu.VMEM((2, SPAN, WID), BF),
            pltpu.VMEM((SPAN, WID), BF),
            pltpu.VMEM((2, 4, SPAN, WID), BF),
            pltpu.VMEM((2, 4, SPAN, WID), BF),
            pltpu.VMEM((SPAN, WID), BF),
            pltpu.VMEM((SPAN, WID), BF),
            pltpu.VMEM((2, 2, 2, 64, WID), BF),
            pltpu.VMEM((2, 2, 2, 64, WID), BF),
            pltpu.VMEM((2, 2, 2, 64, WID), F32),
            pltpu.VMEM((2, 2, 2, 64, WID), BF),
            pltpu.VMEM((2, 2, 2, 64, WID), BF),
            pltpu.VMEM((2, 2, 2, 2, 64, WID), BF),
            pltpu.VMEM((2, 4, 64, WID), F32),
            pltpu.VMEM((2, 4, 64, WID), BF),
            pltpu.VMEM((2, 4, 64, WID), BF),
            pltpu.VMEM((64, WID), BF),
            pltpu.VMEM((64, WID), BF),
            pltpu.VMEM((2, 64, WID), F32),
            pltpu.VMEM((8, 2 * WID, WID), BF),
            pltpu.VMEM((8, WID, 2 * SPAN), BF),
            pltpu.VMEM((2, 1, NSTAT), F32),
            pltpu.VMEM((1, NSTAT), F32),
            pltpu.VMEM((4, 1, NSTAT), F32),
            pltpu.VMEM((4, 1, NSTAT), F32),
            pltpu.VMEM((2, 1, NSTAT), F32),
            pltpu.VMEM((2, 1, NSTAT), F32),
            pltpu.VMEM((MODES, WID), F32),
            pltpu.VMEM((MODES, WID), F32),
            pltpu.VMEM((1, WID), F32),
            pltpu.SMEM((1, 8), jnp.int32),
            pltpu.SemaphoreType.DMA((NSEND,)),
            pltpu.SemaphoreType.DMA((NRECV,)),
            pltpu.SemaphoreType.DMA((7,)),
        ],
        compiler_params=pltpu.CompilerParams(
            collective_id=0, has_side_effects=True, vmem_limit_bytes=48 << 20
        ),
        name="step",
    )(
        *[
            pltpu.with_memory_space_constraint(a, pltpu.HBM)
            for a in (
                tokens, cotangent, w_value, w_gate, decay_rate, residue,
                skip_gain.reshape(1, WID), contig_len,
            )
        ]
    )
    outs = pl.pallas_call(
        store,
        out_shape=shapes,
        in_specs=[vm] * 7,
        out_specs=(hbm,) * 7,
        scratch_shapes=[pltpu.SemaphoreType.DMA((7,))],
        compiler_params=pltpu.CompilerParams(vmem_limit_bytes=1 << 20),
        name="store",
    )(*outs)
    outs = list(outs)
    outs[4] = outs[4].reshape(WID)
    return tuple(outs)


def solution(mesh):
    in_specs = (
        P("dp", "ctx", "tensor"),
        P("dp", "ctx", "tensor"),
        P("ctx", "tensor"),
        P("ctx", "tensor"),
        P(None, "tensor"),
        P(None, "tensor"),
        P("tensor"),
        P("dp", None),
    )
    out_specs = (
        P("dp", "ctx", "tensor"),
        P("dp", "ctx", "tensor"),
        P("ctx", "tensor"),
        P("ctx", "tensor"),
        P("tensor"),
        P(None, "tensor"),
        P(None, "tensor"),
    )
    return jax.shard_map(body, mesh=mesh, in_specs=in_specs, out_specs=out_specs, check_vma=False)
```

```python
import jax
import jax.numpy as jnp
from jax import lax
from jax.experimental import pallas as pl
from jax.experimental.pallas import tpu as pltpu
from jax.sharding import PartitionSpec as P

MESH = pl.DeviceIdType.MESH
F32 = jnp.float32
BF = jnp.bfloat16
SPAN = 128
WID = 256
MODES = 4
LINE = 8 * SPAN
NSTAT = 9 * WID // 2
PART = SPAN // 2

RT, RZ, RX, RS, RF = 0, 16, 24, 32, 40
RE, REX, RC, RP, RPA = 41, 49, 53, 54, 62
RG, RR, RM, RB, RW2 = 63, 71, 75, 83, 84
RQS, RQX, RQM, RQP, RQ2 = 85, 86, 90, 94, 95
RP2, RPA2 = 96, 104
RM2, RB2 = 105, 109
NRECV = 110
NSEND = 144


def dot(a, b, dims):
    return lax.dot_general(a, b, (dims, ((), ())), preferred_element_type=F32)


def split(u):
    hi = u.astype(BF)
    lo = (u - hi.astype(F32)).astype(BF)
    return hi, lo


def kernel(
    tok, cot, wv, wg, rate_h, resid_h, skip_h, clen_h,
    out, gtok, gwv, gwg, gskip, gres, grate,
    fown, fsib, wb, cbuf, ep, em, sloc, bloc, sb, sh, zb, wtot, win, wx, xsb, xb,
    cb, cs, pout, pin, pa_out, pa_in, gr_out, gr_in, gk, gd, gc, gin, gown,
    mout, min_, bout, bin_, gfin, wt, ft, stl, sti, stx, stm, stp, tfin, rate, resid, skip, clen, ssem, rsem, lsem,
):
    d = lax.axis_index("dp")
    c = lax.axis_index("ctx")
    t = lax.axis_index("tensor")
    x, zl = c // 8, c % 8
    zh, y = t // 4, t % 4
    half, mate = zl // 4, zl % 4

    sib = {"dp": 1 - d}
    anti = {"tensor": (1 - zh) * 4 + y}
    partner = {"ctx": x * 8 + (1 - half) * 4 + mate}
    ys = [lax.rem(y + i, 4) for i in (1, 2, 3)]
    xs = [lax.rem(x + i, 4) for i in (1, 2, 3)]
    zs = [lax.rem(zl + i, 8) for i in range(1, 8)]
    ms = [lax.rem(mate + i, 4) for i in (1, 2, 3)]

    def ydev(k):
        return {"tensor": zh * 4 + k}

    def xdev(k):
        return {"ctx": k * 8 + zl}

    def zdev(k):
        return {"ctx": x * 8 + k}

    def mdev(k):
        return {"ctx": x * 8 + half * 4 + k}

    barrier = pltpu.get_barrier_semaphore()
    peers = (
        [sib, anti]
        + [ydev(k) for k in ys]
        + [xdev(k) for k in xs]
        + [zdev(k) for k in zs]
    )
    for who in peers:
        pl.semaphore_signal(barrier, inc=1, device_id=who, device_id_type=MESH)

    loads = [
        pltpu.make_async_copy(tok.at[0], fown.at[t], lsem.at[0]),
        pltpu.make_async_copy(cot.at[0], cbuf, lsem.at[1]),
    ]
    small = [
        pltpu.make_async_copy(rate_h, rate, lsem.at[3]),
        pltpu.make_async_copy(resid_h, resid, lsem.at[4]),
        pltpu.make_async_copy(skip_h, skip, lsem.at[5]),
        pltpu.make_async_copy(clen_h, clen, lsem.at[6]),
    ]
    for cp in small + loads:
        cp.start()

    @pl.when(d == 0)
    def _():
        pltpu.make_async_copy(wv, wb.at[0, c], lsem.at[2]).start()

    @pl.when(d == 1)
    def _():
        pltpu.make_async_copy(wg, wb.at[1, c], lsem.at[2]).start()

    for cp in small:
        cp.wait()
    first = c * SPAN
    starts = [jnp.int32(0)]
    for k in range(7):
        starts.append(starts[-1] + clen[0, k])

    def seg(pos):
        total = (pos >= starts[0]).astype(jnp.int32)
        for s in starts[1:]:
            total = total + (pos >= s).astype(jnp.int32)
        return total

    def row(a):
        return jnp.concatenate([a[m : m + 1, :] for m in range(MODES)], axis=1)

    rt = rate[...]
    factor = jnp.sqrt(one_minus_exp(2.0 * rt))
    wm = resid[...] * factor
    r1 = row(rt)
    tcol = lax.broadcasted_iota(jnp.int32, (SPAN, WID), 0).astype(F32)
    for m in range(MODES):
        rm = rt[m : m + 1, :]
        ep[m] = jnp.exp(rm * tcol)
        em[m] = jnp.exp(-rm * tcol)
    ri = lax.broadcasted_iota(jnp.int32, (SPAN, SPAN), 0)
    ci = lax.broadcasted_iota(jnp.int32, (SPAN, SPAN), 1)
    sr, sc = seg(first + ri), seg(first + ci)
    lower = jnp.where((sr == sc) & (ci <= ri), 1.0, 0.0).astype(BF)
    upper = jnp.where((sr == sc) & (ci >= ri), 1.0, 0.0).astype(BF)
    seg_prev, seg_next = seg(first - 1), seg(first + SPAN)
    stc = seg(first + lax.broadcasted_iota(jnp.int32, (SPAN, WID), 0))
    clearf = jnp.where(stc == seg_prev, 1.0, 0.0)
    clearb = jnp.where(stc == seg_next, 1.0, 0.0)

    back = lax.broadcasted_iota(jnp.int32, (2, MODES * WID), 0) == 1
    base = x * LINE

    def weight(source, target, later_ok, earlier_ok):
        dist = jnp.where(back, source[1] - target[1], target[0] - source[0])
        ok_f = earlier_ok & (seg(source[0]) == seg(target[0]))
        ok_b = later_ok & (seg(source[1]) == seg(target[1]))
        scale = jnp.exp(-r1 * jnp.maximum(dist, 0).astype(F32))
        keep = jnp.where(back, ok_b.astype(F32), ok_f.astype(F32))
        return scale * keep

    yes = c >= 0
    here = (first - 1, first + SPAN)
    for k in range(8):
        ends = (base + SPAN * k + SPAN - 1, base + SPAN * k)
        wtot[k] = weight(ends, (base + LINE - 1, base), yes, yes)
        win[k] = weight(ends, here, k > zl, k < zl)
    for k in range(4):
        ends = ((k + 1) * LINE - 1, k * LINE)
        wx[k] = weight(ends, here, k > x, k < x)
    step2 = jnp.exp(-r1 * jnp.where(back, float(SPAN), 1.0))

    sends = []

    def send(src, dst, recv, who):
        cp = pltpu.make_async_remote_copy(
            src_ref=src,
            dst_ref=dst,
            send_sem=ssem.at[len(sends)],
            recv_sem=rsem.at[recv],
            device_id=who,
            device_id_type=MESH,
        )
        cp.start()
        sends.append(cp)

    def arrived(ref, recv):
        pltpu.make_async_copy(ref, ref, rsem.at[recv]).wait()

    for cp in loads:
        cp.wait()
    pltpu.make_async_copy(wv, wb.at[d, c], lsem.at[2]).wait()
    pl.semaphore_wait(barrier, len(peers))

    def spread_x(k):
        for i in (xs[1], xs[0], xs[2]):
            send(wb.at[d, x * 8 + k], wb.at[d, x * 8 + k], RX + 2 * x + k // 4, xdev(i))

    def quad(core, k, g):
        return wb.at[core, pl.ds(k * 8 + 4 * g, 4)]

    def to_sib(k, g):
        send(quad(d, k, g), quad(d, k, g), RS + 2 * k + g, sib)

    near, far = half, 1 - half
    def piece(j, q):
        return fown.at[j, pl.ds(q * (SPAN // 2), SPAN // 2)]

    send(wb.at[d, c], wb.at[d, c], RZ + zl, partner)
    for i in (ms[1], ms[0], ms[2]):
        send(wb.at[d, c], wb.at[d, c], RZ + zl, mdev(i))
    for q in range(2):
        send(piece(t, q), piece(t, q), RT + 2 * t + q, anti)
    spread_x(zl)
    for i in ys:
        send(fown.at[t], fown.at[t], RT + 2 * t, ydev(i))
    for i in ms:
        k = near * 4 + i
        arrived(wb.at[d, x * 8 + k], RZ + k)
        spread_x(k)
    to_sib(x, near)
    k = far * 4 + mate
    arrived(wb.at[d, x * 8 + k], RZ + k)
    for i in (ms[1], ms[0], ms[2]):
        send(wb.at[d, x * 8 + k], wb.at[d, x * 8 + k], RZ + k, mdev(i))
    spread_x(k)
    ta = (1 - zh) * 4 + y

    def tokens_on(q):
        arrived(piece(ta, q), RT + 2 * ta + q)
        for i in ys:
            send(piece(ta, q), piece(ta, q), RT + 2 * ta + q, ydev(i))

    tokens_on(0)
    for i in ms:
        k = far * 4 + i
        arrived(wb.at[d, x * 8 + k], RZ + k)
        spread_x(k)
    to_sib(x, far)
    tokens_on(1)
    for i in (xs[0], xs[2], xs[1]):
        arrived(quad(d, i, near), RX + 2 * i + near)
        to_sib(i, near)
    for i in ys:
        arrived(fown.at[zh * 4 + i], RT + 2 * (zh * 4 + i))
    for q in range(2):
        for i in ys:
            arrived(piece((1 - zh) * 4 + i, q), RT + 2 * ((1 - zh) * 4 + i) + q)
    for i in (xs[0], xs[2], xs[1]):
        arrived(quad(d, i, far), RX + 2 * i + far)
        to_sib(i, far)
    send(fown, fsib, RF, sib)
    for i in range(4):
        for g in range(2):
            arrived(quad(1 - d, i, g), RS + 2 * i + g)

    def wblock(core, j):
        return wb[core, 4 * j : 4 * j + 4].reshape(WID, WID)

    mm = ((1,), (0,))
    value = dot(fown[0], wblock(0, 0), mm)
    gate = dot(fown[0], wblock(1, 0), mm)
    for j in range(1, 8):
        value = value + dot(fown[j], wblock(0, j), mm)
        gate = gate + dot(fown[j], wblock(1, j), mm)
    upstream = cbuf[...].astype(F32)
    gm = upstream * gate

    for m in range(MODES):
        hi, lo = split(value * ep[m])
        s = dot(lower, hi, mm) + dot(lower, lo, mm)
        sloc[m] = s
        sb[0:1, m * WID : (m + 1) * WID] = s[SPAN - 1 :, :] * em[m, SPAN - 1 :, :]
        hi, lo = split(gm * wm[m : m + 1, :] * em[m])
        b = dot(upper, hi, mm) + dot(upper, lo, mm)
        bloc[m] = b
        sb[1:2, m * WID : (m + 1) * WID] = b[0:1, :]
    sh[...] = sb[...].astype(BF)
    zb[zl] = sh[...]
    for i in (zs[6], zs[0], zs[5], zs[1], zs[4], zs[2], zs[3]):
        send(sh, zb.at[zl], RE + zl, zdev(i))
    arrived(fsib, RF)
    for j in range(8):
        wt[j, 0:WID] = wblock(0, j).T
        wt[j, WID:] = wblock(1, j).T
        ft[j, :, 0:SPAN] = fown[j].T
        ft[j, :, SPAN:] = fsib[j].T
    for i in zs:
        arrived(zb.at[i], RE + i)
    total = wtot[0] * zb[0].astype(F32)
    for k in range(1, 8):
        total = total + wtot[k] * zb[k].astype(F32)
    xsb[...] = total
    xb[x] = total
    for i in (xs[1], xs[0], xs[2]):
        send(xsb, xb.at[x], REX + x, xdev(i))
    inc = win[0] * zb[0].astype(F32)
    for k in range(1, 8):
        inc = inc + win[k] * zb[k].astype(F32)
    for i in xs:
        arrived(xb.at[i], REX + i)
    for k in range(4):
        inc = inc + wx[k] * xb[k]
    inc = inc * step2
    inc_f, inc_b = inc[0:1, :], inc[1:2, :]

    sk = skip[...]
    mixed = sk * value
    gval = sk * gm
    pairs, carries = [], []
    for m in range(MODES):
        lanes = slice(m * WID, (m + 1) * WID)
        state = em[m] * (sloc[m] + clearf * inc_f[:, lanes])
        gst = ep[m] * (bloc[m] + clearb * inc_b[:, lanes])
        mixed = mixed + wm[m : m + 1, :] * state
        gval = gval + gst
        pairs.append(jnp.sum(gm * state, axis=0, keepdims=True))
        carries.append(jnp.sum(gst * (state - value), axis=0, keepdims=True))
    stats = [jnp.sum(gm * value, axis=0, keepdims=True)] + pairs + carries
    stats = jnp.concatenate(stats, axis=1)
    stl[0] = stats[:, 0:NSTAT]
    stl[1] = stats[:, NSTAT:]
    out[0] = (gate * mixed).astype(BF)
    cv = gval.astype(BF)
    cg = (upstream * mixed).astype(BF)
    cb[0] = cv
    cb[1] = cg
    send(cb.at[1 - d], cs, RC, sib)
    send(stl.at[1 - d], sti, RQS, sib)

    both = jnp.concatenate([cv, cg], axis=1)

    def share(h, i):
        return dot(both, wt[h * 4 + i], mm).astype(BF)

    def rows(p):
        return slice(p * PART, (p + 1) * PART)

    def other_shares(p, sem):
        h = 1 - zh
        for i in (ys[1], ys[0], ys[2], y):
            part = dot(both[rows(p)], wt[h * 4 + i], mm).astype(BF)
            if i is y:
                pin[h, y, rows(p)] = part
                continue
            pout[h, i, rows(p)] = part
            src = pout.at[h, i, pl.ds(p * PART, PART)]
            dst = pin.at[h, y, pl.ds(p * PART, PART)]
            send(src, dst, sem + 4 * h + y, ydev(i))

    def other_sum(p, sem):
        h = 1 - zh
        for i in ys:
            arrived(pin.at[h, i, pl.ds(p * PART, PART)], sem + 4 * h + i)
        total = pin[h, 0, rows(p)].astype(F32)
        for k in range(1, 4):
            total = total + pin[h, k, rows(p)].astype(F32)
        pa_out[rows(p)] = total.astype(BF)
        cut = pl.ds(p * PART, PART)
        send(pa_out.at[cut], pa_in.at[cut], RPA if p == 0 else RPA2, anti)

    def own_shares():
        for i in (ys[1], ys[0], ys[2]):
            pout[zh, i] = share(zh, i)
            send(pout.at[zh, i], pin.at[zh, y], RP + 4 * zh + y, ydev(i))
        pin[zh, y] = share(zh, y)

    def own_sum():
        for i in ys:
            arrived(pin.at[zh, i], RP + 4 * zh + i)
        total = pin[zh, 0].astype(F32)
        for k in range(1, 4):
            total = total + pin[zh, k].astype(F32)
        return total

    right, left = xs[0], xs[2]

    def slab(h, i):
        return dot(ft[2 * i + h], cots, mm).reshape(4, 64, WID)

    def x_start(h):
        g = slab(h, xs[1]).astype(BF)
        gr_out[h, 0] = g[0:2]
        send(gr_out.at[h, 0], gr_in.at[h, 0], RR + 2 * h, xdev(right))
        gr_out[h, 1] = g[2:4]
        send(gr_out.at[h, 1], gr_in.at[h, 1], RR + 2 * h + 1, xdev(left))

    def x_direct(h):
        g = slab(h, right)
        gk[h, 0] = g[0:2]
        gd[h, 0] = g[2:4].astype(BF)
        send(gd.at[h, 0], gin.at[h, 0, 1], RG + 4 * h + 1, xdev(right))
        g = slab(h, left)
        gk[h, 1] = g[2:4]
        gd[h, 1] = g[0:2].astype(BF)
        send(gd.at[h, 1], gin.at[h, 1, 0], RG + 4 * h + 2, xdev(left))

    def x_relay(h):
        for side, who, part in ((0, right, 0), (1, left, 1)):
            arrived(gr_in.at[h, side], RR + 2 * h + side)
            gc[h, side] = (gk[h, side] + gr_in[h, side].astype(F32)).astype(BF)
            send(gc.at[h, side], gin.at[h, side, part], RG + 4 * h + 3 * side, xdev(who))

    def x_sum(h):
        for side in range(2):
            for part in range(2):
                arrived(gin.at[h, side, part], RG + 4 * h + 2 * side + part)
        for part in range(2):
            g = gown[h, 2 * part : 2 * part + 2]
            g = g + gin[h, 0, part].astype(F32) + gin[h, 1, part].astype(F32)
            mout[h, 2 * part : 2 * part + 2] = g.astype(BF)
        if h is near:
            for i in (ms[1], ms[0], ms[2]):
                send(mout.at[h, i], min_.at[h, mate], RM + 4 * h + mate, mdev(i))
            return
        for r, sem in ((0, RM + 4 * h), (1, RM2)):
            for i in (ms[1], ms[0], ms[2]):
                cut = pl.ds(32 * r, 32)
                send(mout.at[h, i, cut], min_.at[h, mate, cut], sem + mate, mdev(i))

    def mates_near():
        for i in ms:
            arrived(min_.at[near, i], RM + 4 * near + i)
        g = mout[near, mate].astype(F32)
        for i in ms:
            g = g + min_[near, i].astype(F32)
        return g

    def mates_far(r, sem, out_sem):
        cut = slice(32 * r, 32 * r + 32)
        part = pl.ds(32 * r, 32)
        for i in ms:
            arrived(min_.at[far, i, part], sem + i)
        g = mout[far, mate, cut].astype(F32)
        for i in ms:
            g = g + min_[far, i, cut].astype(F32)
        bout[cut] = g.astype(BF)
        send(bout.at[part], bin_.at[part], out_sem, partner)

    other_shares(0, RP)
    arrived(sti, RQS)
    stx[x] = stl[d] + sti[...]
    for i in xs:
        send(stx.at[x], stx.at[x], RQX + x, xdev(i))
    arrived(cs, RC)
    cots = jnp.concatenate([cb[d], cs[...]], axis=0)
    x_start(far)
    other_shares(1, RP2)
    x_direct(far)
    x_start(near)
    own_shares()
    other_sum(0, RP)
    x_relay(far)
    x_direct(near)
    other_sum(1, RP2)
    for h in (far, near):
        gown[h] = slab(h, x)
    for i in xs:
        arrived(stx.at[i], RQX + i)
    stm[mate] = (stx[0] + stx[1]) + (stx[2] + stx[3])
    for i in ms:
        send(stm.at[mate], stm.at[mate], RQM + mate, mdev(i))
    x_relay(near)
    x_sum(far)
    x_sum(near)
    for i in ms:
        arrived(stm.at[i], RQM + i)
    stp[half] = (stm[0] + stm[1]) + (stm[2] + stm[3])
    send(stp.at[half], stp.at[half], RQP, partner)
    mates_far(0, RM + 4 * far, RB)
    mates_far(1, RM2, RB2)
    kept = own_sum()
    g = mates_near()
    arrived(stp.at[1 - half], RQP)
    tfin[d] = stp[0] + stp[1]
    send(tfin.at[d], tfin.at[d], RQ2, sib)

    arrived(bin_.at[pl.ds(0, 32)], RB)
    arrived(bin_.at[pl.ds(32, 32)], RB2)
    gfin[d] = g + bin_[...].astype(F32)
    send(gfin.at[d], gfin.at[d], RW2, sib)
    arrived(tfin.at[1 - d], RQ2)
    tot = jnp.concatenate([tfin[0], tfin[1]], axis=1)
    gskip[...] = tot[:, 0:WID]
    ratio = resid[...] * jnp.exp(-2.0 * rt) / factor
    for m in range(MODES):
        paired = tot[:, WID * (1 + m) : WID * (2 + m)]
        carried = tot[:, WID * (5 + m) : WID * (6 + m)]
        gres[m : m + 1, :] = factor[m : m + 1, :] * paired
        grate[m : m + 1, :] = ratio[m : m + 1, :] * paired - carried
    for p, sem in ((0, RPA), (1, RPA2)):
        arrived(pa_in.at[pl.ds(p * PART, PART)], sem)
    gtok[0] = (kept + pa_in[...].astype(F32)).astype(BF)
    arrived(gfin.at[1 - d], RW2)
    gwv[...] = gfin[0]
    gwg[...] = gfin[1]
    assert len(sends) <= NSEND
    for cp in sends:
        cp.wait_send()


def one_minus_exp(a):
    term = a
    total = a
    for k in range(2, 8):
        term = term * (-a / k)
        total = total + term
    return total


def store(*refs):
    sem = refs[14]
    copies = [pltpu.make_async_copy(refs[k], refs[7 + k], sem.at[k]) for k in range(7)]
    for cp in copies:
        cp.start()
    for cp in copies:
        cp.wait()


def body(tokens, cotangent, w_value, w_gate, decay_rate, residue, skip_gain, contig_len):
    vm = pl.BlockSpec(memory_space=pltpu.VMEM)
    hbm = pl.BlockSpec(memory_space=pltpu.HBM)
    sds = jax.ShapeDtypeStruct
    shapes = (
        sds((1, SPAN, WID), BF),
        sds((1, SPAN, WID), BF),
        sds((64, WID), F32),
        sds((64, WID), F32),
        sds((1, WID), F32),
        sds((MODES, WID), F32),
        sds((MODES, WID), F32),
    )
    outs = pl.pallas_call(
        kernel,
        out_shape=shapes,
        in_specs=[hbm] * 8,
        out_specs=(vm,) * 7,
        scratch_shapes=[
            pltpu.VMEM((8, SPAN, WID), BF),
            pltpu.VMEM((8, SPAN, WID), BF),
            pltpu.VMEM((2, 32, 64, WID), BF),
            pltpu.VMEM((SPAN, WID), BF),
            pltpu.VMEM((MODES, SPAN, WID), F32),
            pltpu.VMEM((MODES, SPAN, WID), F32),
            pltpu.VMEM((MODES, SPAN, WID), F32),
            pltpu.VMEM((MODES, SPAN, WID), F32),
            pltpu.VMEM((2, MODES * WID), F32),
            pltpu.VMEM((2, MODES * WID), BF),
            pltpu.VMEM((8, 2, MODES * WID), BF),
            pltpu.VMEM((8, 2, MODES * WID), F32),
            pltpu.VMEM((8, 2, MODES * WID), F32),
            pltpu.VMEM((4, 2, MODES * WID), F32),
            pltpu.VMEM((2, MODES * WID), F32),
            pltpu.VMEM((4, 2, MODES * WID), F32),
            pltpu.VMEM((2, SPAN, WID), BF),
            pltpu.VMEM((SPAN, WID), BF),
            pltpu.VMEM((2, 4, SPAN, WID), BF),
            pltpu.VMEM((2, 4, SPAN, WID), BF),
            pltpu.VMEM((SPAN, WID), BF),
            pltpu.VMEM((SPAN, WID), BF),
            pltpu.VMEM((2, 2, 2, 64, WID), BF),
            pltpu.VMEM((2, 2, 2, 64, WID), BF),
            pltpu.VMEM((2, 2, 2, 64, WID), F32),
            pltpu.VMEM((2, 2, 2, 64, WID), BF),
            pltpu.VMEM((2, 2, 2, 64, WID), BF),
            pltpu.VMEM((2, 2, 2, 2, 64, WID), BF),
            pltpu.VMEM((2, 4, 64, WID), F32),
            pltpu.VMEM((2, 4, 64, WID), BF),
            pltpu.VMEM((2, 4, 64, WID), BF),
            pltpu.VMEM((64, WID), BF),
            pltpu.VMEM((64, WID), BF),
            pltpu.VMEM((2, 64, WID), F32),
            pltpu.VMEM((8, 2 * WID, WID), BF),
            pltpu.VMEM((8, WID, 2 * SPAN), BF),
            pltpu.VMEM((2, 1, NSTAT), F32),
            pltpu.VMEM((1, NSTAT), F32),
            pltpu.VMEM((4, 1, NSTAT), F32),
            pltpu.VMEM((4, 1, NSTAT), F32),
            pltpu.VMEM((2, 1, NSTAT), F32),
            pltpu.VMEM((2, 1, NSTAT), F32),
            pltpu.VMEM((MODES, WID), F32),
            pltpu.VMEM((MODES, WID), F32),
            pltpu.VMEM((1, WID), F32),
            pltpu.SMEM((1, 8), jnp.int32),
            pltpu.SemaphoreType.DMA((NSEND,)),
            pltpu.SemaphoreType.DMA((NRECV,)),
            pltpu.SemaphoreType.DMA((7,)),
        ],
        compiler_params=pltpu.CompilerParams(
            collective_id=0, has_side_effects=True, vmem_limit_bytes=48 << 20
        ),
        name="step",
    )(
        *[
            pltpu.with_memory_space_constraint(a, pltpu.HBM)
            for a in (
                tokens, cotangent, w_value, w_gate, decay_rate, residue,
                skip_gain.reshape(1, WID), contig_len,
            )
        ]
    )
    outs = pl.pallas_call(
        store,
        out_shape=shapes,
        in_specs=[vm] * 7,
        out_specs=(hbm,) * 7,
        scratch_shapes=[pltpu.SemaphoreType.DMA((7,))],
        compiler_params=pltpu.CompilerParams(vmem_limit_bytes=1 << 20),
        name="store",
    )(*outs)
    outs = list(outs)
    outs[4] = outs[4].reshape(WID)
    return tuple(outs)


def solution(mesh):
    in_specs = (
        P("dp", "ctx", "tensor"),
        P("dp", "ctx", "tensor"),
        P("ctx", "tensor"),
        P("ctx", "tensor"),
        P(None, "tensor"),
        P(None, "tensor"),
        P("tensor"),
        P("dp", None),
    )
    out_specs = (
        P("dp", "ctx", "tensor"),
        P("dp", "ctx", "tensor"),
        P("ctx", "tensor"),
        P("ctx", "tensor"),
        P("tensor"),
        P(None, "tensor"),
        P(None, "tensor"),
    )
    return jax.shard_map(body, mesh=mesh, in_specs=in_specs, out_specs=out_specs, check_vma=False)
```

```python
import jax
import jax.numpy as jnp
from jax import lax
from jax.experimental import pallas as pl
from jax.experimental.pallas import tpu as pltpu
from jax.sharding import PartitionSpec as P

MESH = pl.DeviceIdType.MESH
F32 = jnp.float32
BF = jnp.bfloat16
SPAN = 128
WID = 256
MODES = 4
LINE = 8 * SPAN
NSTAT = 9 * WID // 2
PART = SPAN // 2

RT, RZ, RX, RS, RF = 0, 16, 24, 32, 40
RE, REX, RC, RP, RPA = 41, 49, 53, 54, 62
RG, RR, RM, RB, RW2 = 63, 71, 75, 83, 84
RQS, RQX, RQM, RQP, RQ2 = 85, 86, 90, 94, 95
RP2, RPA2 = 96, 104
RM2, RB2 = 105, 109
NRECV = 110
NSEND = 144


def dot(a, b, dims):
    return lax.dot_general(a, b, (dims, ((), ())), preferred_element_type=F32)


def split(u):
    hi = u.astype(BF)
    lo = (u - hi.astype(F32)).astype(BF)
    return hi, lo


def kernel(
    tok, cot, wv, wg, rate_h, resid_h, skip_h, clen_h,
    out, gtok, gwv, gwg, gskip, gres, grate,
    fown, fsib, wb, cbuf, ep, em, sloc, bloc, sb, sh, zb, wtot, win, wx, xsb, xb,
    cb, cs, pout, pin, pa_out, pa_in, gr_out, gr_in, gk, gd, gc, gin, gown,
    mout, min_, bout, bin_, gfin, wt, ft, stl, sti, stx, stm, stp, tfin, rate, resid, skip, clen, ssem, rsem, lsem,
):
    d = lax.axis_index("dp")
    c = lax.axis_index("ctx")
    t = lax.axis_index("tensor")
    x, zl = c // 8, c % 8
    zh, y = t // 4, t % 4
    half, mate = zl // 4, zl % 4

    sib = {"dp": 1 - d}
    anti = {"tensor": (1 - zh) * 4 + y}
    partner = {"ctx": x * 8 + (1 - half) * 4 + mate}
    ys = [lax.rem(y + i, 4) for i in (1, 2, 3)]
    xs = [lax.rem(x + i, 4) for i in (1, 2, 3)]
    zs = [lax.rem(zl + i, 8) for i in range(1, 8)]
    ms = [lax.rem(mate + i, 4) for i in (1, 2, 3)]

    def ydev(k):
        return {"tensor": zh * 4 + k}

    def xdev(k):
        return {"ctx": k * 8 + zl}

    def zdev(k):
        return {"ctx": x * 8 + k}

    def mdev(k):
        return {"ctx": x * 8 + half * 4 + k}

    barrier = pltpu.get_barrier_semaphore()
    peers = (
        [sib, anti]
        + [ydev(k) for k in ys]
        + [xdev(k) for k in xs]
        + [zdev(k) for k in zs]
    )
    for who in peers:
        pl.semaphore_signal(barrier, inc=1, device_id=who, device_id_type=MESH)

    loads = [
        pltpu.make_async_copy(tok.at[0], fown.at[t], lsem.at[0]),
        pltpu.make_async_copy(cot.at[0], cbuf, lsem.at[1]),
    ]
    small = [
        pltpu.make_async_copy(rate_h, rate, lsem.at[3]),
        pltpu.make_async_copy(resid_h, resid, lsem.at[4]),
        pltpu.make_async_copy(skip_h, skip, lsem.at[5]),
        pltpu.make_async_copy(clen_h, clen, lsem.at[6]),
    ]
    for cp in small + loads:
        cp.start()

    @pl.when(d == 0)
    def _():
        pltpu.make_async_copy(wv, wb.at[0, c], lsem.at[2]).start()

    @pl.when(d == 1)
    def _():
        pltpu.make_async_copy(wg, wb.at[1, c], lsem.at[2]).start()

    for cp in small:
        cp.wait()
    first = c * SPAN
    starts = [jnp.int32(0)]
    for k in range(7):
        starts.append(starts[-1] + clen[0, k])

    def seg(pos):
        total = (pos >= starts[0]).astype(jnp.int32)
        for s in starts[1:]:
            total = total + (pos >= s).astype(jnp.int32)
        return total

    def row(a):
        return jnp.concatenate([a[m : m + 1, :] for m in range(MODES)], axis=1)

    rt = rate[...]
    factor = jnp.sqrt(one_minus_exp(2.0 * rt))
    wm = resid[...] * factor
    r1 = row(rt)
    tcol = lax.broadcasted_iota(jnp.int32, (SPAN, WID), 0).astype(F32)
    for m in range(MODES):
        rm = rt[m : m + 1, :]
        ep[m] = jnp.exp(rm * tcol)
        em[m] = jnp.exp(-rm * tcol)
    ri = lax.broadcasted_iota(jnp.int32, (SPAN, SPAN), 0)
    ci = lax.broadcasted_iota(jnp.int32, (SPAN, SPAN), 1)
    sr, sc = seg(first + ri), seg(first + ci)
    lower = jnp.where((sr == sc) & (ci <= ri), 1.0, 0.0).astype(BF)
    upper = jnp.where((sr == sc) & (ci >= ri), 1.0, 0.0).astype(BF)
    seg_prev, seg_next = seg(first - 1), seg(first + SPAN)
    stc = seg(first + lax.broadcasted_iota(jnp.int32, (SPAN, WID), 0))
    clearf = jnp.where(stc == seg_prev, 1.0, 0.0)
    clearb = jnp.where(stc == seg_next, 1.0, 0.0)

    back = lax.broadcasted_iota(jnp.int32, (2, MODES * WID), 0) == 1
    base = x * LINE

    def weight(source, target, later_ok, earlier_ok):
        dist = jnp.where(back, source[1] - target[1], target[0] - source[0])
        ok_f = earlier_ok & (seg(source[0]) == seg(target[0]))
        ok_b = later_ok & (seg(source[1]) == seg(target[1]))
        scale = jnp.exp(-r1 * jnp.maximum(dist, 0).astype(F32))
        keep = jnp.where(back, ok_b.astype(F32), ok_f.astype(F32))
        return scale * keep

    yes = c >= 0
    here = (first - 1, first + SPAN)
    for k in range(8):
        ends = (base + SPAN * k + SPAN - 1, base + SPAN * k)
        wtot[k] = weight(ends, (base + LINE - 1, base), yes, yes)
        win[k] = weight(ends, here, k > zl, k < zl)
    for k in range(4):
        ends = ((k + 1) * LINE - 1, k * LINE)
        wx[k] = weight(ends, here, k > x, k < x)
    step2 = jnp.exp(-r1 * jnp.where(back, float(SPAN), 1.0))

    sends = []

    def send(src, dst, recv, who):
        cp = pltpu.make_async_remote_copy(
            src_ref=src,
            dst_ref=dst,
            send_sem=ssem.at[len(sends)],
            recv_sem=rsem.at[recv],
            device_id=who,
            device_id_type=MESH,
        )
        cp.start()
        sends.append(cp)

    def arrived(ref, recv):
        pltpu.make_async_copy(ref, ref, rsem.at[recv]).wait()

    for cp in loads:
        cp.wait()
    pltpu.make_async_copy(wv, wb.at[d, c], lsem.at[2]).wait()
    pl.semaphore_wait(barrier, len(peers))

    def spread_x(k):
        for i in (xs[1], xs[0], xs[2]):
            send(wb.at[d, x * 8 + k], wb.at[d, x * 8 + k], RX + 2 * x + k // 4, xdev(i))

    def quad(core, k, g):
        return wb.at[core, pl.ds(k * 8 + 4 * g, 4)]

    def to_sib(k, g):
        send(quad(d, k, g), quad(d, k, g), RS + 2 * k + g, sib)

    near, far = half, 1 - half
    def piece(j, q):
        return fown.at[j, pl.ds(q * (SPAN // 2), SPAN // 2)]

    send(wb.at[d, c], wb.at[d, c], RZ + zl, partner)
    for i in (ms[1], ms[0], ms[2]):
        send(wb.at[d, c], wb.at[d, c], RZ + zl, mdev(i))
    for q in range(2):
        send(piece(t, q), piece(t, q), RT + 2 * t + q, anti)
    spread_x(zl)
    for i in ys:
        send(fown.at[t], fown.at[t], RT + 2 * t, ydev(i))
    for i in ms:
        k = near * 4 + i
        arrived(wb.at[d, x * 8 + k], RZ + k)
        spread_x(k)
    to_sib(x, near)
    k = far * 4 + mate
    arrived(wb.at[d, x * 8 + k], RZ + k)
    for i in (ms[1], ms[0], ms[2]):
        send(wb.at[d, x * 8 + k], wb.at[d, x * 8 + k], RZ + k, mdev(i))
    spread_x(k)
    ta = (1 - zh) * 4 + y

    def tokens_on(q):
        arrived(piece(ta, q), RT + 2 * ta + q)
        for i in ys:
            send(piece(ta, q), piece(ta, q), RT + 2 * ta + q, ydev(i))

    tokens_on(0)
    for i in ms:
        k = far * 4 + i
        arrived(wb.at[d, x * 8 + k], RZ + k)
        spread_x(k)
    to_sib(x, far)
    tokens_on(1)
    for i in (xs[0], xs[2], xs[1]):
        arrived(quad(d, i, near), RX + 2 * i + near)
        to_sib(i, near)
    for i in ys:
        arrived(fown.at[zh * 4 + i], RT + 2 * (zh * 4 + i))
    for q in range(2):
        for i in ys:
            arrived(piece((1 - zh) * 4 + i, q), RT + 2 * ((1 - zh) * 4 + i) + q)
    for i in (xs[0], xs[2], xs[1]):
        arrived(quad(d, i, far), RX + 2 * i + far)
        to_sib(i, far)
    send(fown, fsib, RF, sib)
    for i in range(4):
        for g in range(2):
            arrived(quad(1 - d, i, g), RS + 2 * i + g)

    def wblock(core, j):
        return wb[core, 4 * j : 4 * j + 4].reshape(WID, WID)

    mm = ((1,), (0,))
    value = dot(fown[0], wblock(0, 0), mm)
    gate = dot(fown[0], wblock(1, 0), mm)
    for j in range(1, 8):
        value = value + dot(fown[j], wblock(0, j), mm)
        gate = gate + dot(fown[j], wblock(1, j), mm)
    upstream = cbuf[...].astype(F32)
    gm = upstream * gate

    for m in range(MODES):
        hi, lo = split(value * ep[m])
        s = dot(lower, hi, mm) + dot(lower, lo, mm)
        sloc[m] = s
        sb[0:1, m * WID : (m + 1) * WID] = s[SPAN - 1 :, :] * em[m, SPAN - 1 :, :]
        hi, lo = split(gm * wm[m : m + 1, :] * em[m])
        b = dot(upper, hi, mm) + dot(upper, lo, mm)
        bloc[m] = b
        sb[1:2, m * WID : (m + 1) * WID] = b[0:1, :]
    sh[...] = sb[...].astype(BF)
    zb[zl] = sh[...]
    for i in (zs[6], zs[0], zs[5], zs[1], zs[4], zs[2], zs[3]):
        send(sh, zb.at[zl], RE + zl, zdev(i))
    arrived(fsib, RF)
    for j in range(8):
        wt[j, 0:WID] = wblock(0, j).T
        wt[j, WID:] = wblock(1, j).T
        ft[j, :, 0:SPAN] = fown[j].T
        ft[j, :, SPAN:] = fsib[j].T
    for i in zs:
        arrived(zb.at[i], RE + i)
    total = wtot[0] * zb[0].astype(F32)
    for k in range(1, 8):
        total = total + wtot[k] * zb[k].astype(F32)
    xsb[...] = total
    xb[x] = total
    for i in (xs[1], xs[0], xs[2]):
        send(xsb, xb.at[x], REX + x, xdev(i))
    inc = win[0] * zb[0].astype(F32)
    for k in range(1, 8):
        inc = inc + win[k] * zb[k].astype(F32)
    for i in xs:
        arrived(xb.at[i], REX + i)
    for k in range(4):
        inc = inc + wx[k] * xb[k]
    inc = inc * step2
    inc_f, inc_b = inc[0:1, :], inc[1:2, :]

    sk = skip[...]
    mixed = sk * value
    gval = sk * gm
    pairs, carries = [], []
    for m in range(MODES):
        lanes = slice(m * WID, (m + 1) * WID)
        state = em[m] * (sloc[m] + clearf * inc_f[:, lanes])
        gst = ep[m] * (bloc[m] + clearb * inc_b[:, lanes])
        mixed = mixed + wm[m : m + 1, :] * state
        gval = gval + gst
        pairs.append(jnp.sum(gm * state, axis=0, keepdims=True))
        carries.append(jnp.sum(gst * (state - value), axis=0, keepdims=True))
    stats = [jnp.sum(gm * value, axis=0, keepdims=True)] + pairs + carries
    stats = jnp.concatenate(stats, axis=1)
    stl[0] = stats[:, 0:NSTAT]
    stl[1] = stats[:, NSTAT:]
    out[0] = (gate * mixed).astype(BF)
    cv = gval.astype(BF)
    cg = (upstream * mixed).astype(BF)
    cb[0] = cv
    cb[1] = cg
    send(cb.at[1 - d], cs, RC, sib)
    send(stl.at[1 - d], sti, RQS, sib)

    both = jnp.concatenate([cv, cg], axis=1)

    def share(h, i):
        return dot(both, wt[h * 4 + i], mm).astype(BF)

    def rows(p):
        return slice(p * PART, (p + 1) * PART)

    def other_shares(p, sem):
        h = 1 - zh
        for i in (ys[1], ys[0], ys[2], y):
            part = dot(both[rows(p)], wt[h * 4 + i], mm).astype(BF)
            if i is y:
                pin[h, y, rows(p)] = part
                continue
            pout[h, i, rows(p)] = part
            src = pout.at[h, i, pl.ds(p * PART, PART)]
            dst = pin.at[h, y, pl.ds(p * PART, PART)]
            send(src, dst, sem + 4 * h + y, ydev(i))

    def other_sum(p, sem):
        h = 1 - zh
        for i in ys:
            arrived(pin.at[h, i, pl.ds(p * PART, PART)], sem + 4 * h + i)
        total = pin[h, 0, rows(p)].astype(F32)
        for k in range(1, 4):
            total = total + pin[h, k, rows(p)].astype(F32)
        pa_out[rows(p)] = total.astype(BF)
        cut = pl.ds(p * PART, PART)
        send(pa_out.at[cut], pa_in.at[cut], RPA if p == 0 else RPA2, anti)

    def own_shares():
        for i in (ys[1], ys[0], ys[2]):
            pout[zh, i] = share(zh, i)
            send(pout.at[zh, i], pin.at[zh, y], RP + 4 * zh + y, ydev(i))
        pin[zh, y] = share(zh, y)

    def own_sum():
        for i in ys:
            arrived(pin.at[zh, i], RP + 4 * zh + i)
        total = pin[zh, 0].astype(F32)
        for k in range(1, 4):
            total = total + pin[zh, k].astype(F32)
        return total

    right, left = xs[0], xs[2]

    def slab(h, i):
        return dot(ft[2 * i + h], cots, mm).reshape(4, 64, WID)

    def x_start(h):
        g = slab(h, xs[1]).astype(BF)
        gr_out[h, 0] = g[0:2]
        send(gr_out.at[h, 0], gr_in.at[h, 0], RR + 2 * h, xdev(right))
        gr_out[h, 1] = g[2:4]
        send(gr_out.at[h, 1], gr_in.at[h, 1], RR + 2 * h + 1, xdev(left))

    def x_direct(h):
        g = slab(h, right)
        gk[h, 0] = g[0:2]
        gd[h, 0] = g[2:4].astype(BF)
        send(gd.at[h, 0], gin.at[h, 0, 1], RG + 4 * h + 1, xdev(right))
        g = slab(h, left)
        gk[h, 1] = g[2:4]
        gd[h, 1] = g[0:2].astype(BF)
        send(gd.at[h, 1], gin.at[h, 1, 0], RG + 4 * h + 2, xdev(left))

    def x_relay(h):
        for side, who, part in ((0, right, 0), (1, left, 1)):
            arrived(gr_in.at[h, side], RR + 2 * h + side)
            gc[h, side] = (gk[h, side] + gr_in[h, side].astype(F32)).astype(BF)
            send(gc.at[h, side], gin.at[h, side, part], RG + 4 * h + 3 * side, xdev(who))

    def x_sum(h):
        for side in range(2):
            for part in range(2):
                arrived(gin.at[h, side, part], RG + 4 * h + 2 * side + part)
        for part in range(2):
            g = gown[h, 2 * part : 2 * part + 2]
            g = g + gin[h, 0, part].astype(F32) + gin[h, 1, part].astype(F32)
            mout[h, 2 * part : 2 * part + 2] = g.astype(BF)
        if h is near:
            for i in (ms[1], ms[0], ms[2]):
                send(mout.at[h, i], min_.at[h, mate], RM + 4 * h + mate, mdev(i))
            return
        for r, sem in ((0, RM + 4 * h), (1, RM2)):
            for i in (ms[1], ms[0], ms[2]):
                cut = pl.ds(32 * r, 32)
                send(mout.at[h, i, cut], min_.at[h, mate, cut], sem + mate, mdev(i))

    def mates_near():
        for i in ms:
            arrived(min_.at[near, i], RM + 4 * near + i)
        g = mout[near, mate].astype(F32)
        for i in ms:
            g = g + min_[near, i].astype(F32)
        return g

    def mates_far(r, sem, out_sem):
        cut = slice(32 * r, 32 * r + 32)
        part = pl.ds(32 * r, 32)
        for i in ms:
            arrived(min_.at[far, i, part], sem + i)
        g = mout[far, mate, cut].astype(F32)
        for i in ms:
            g = g + min_[far, i, cut].astype(F32)
        bout[cut] = g.astype(BF)
        send(bout.at[part], bin_.at[part], out_sem, partner)

    other_shares(0, RP)
    arrived(sti, RQS)
    stx[x] = stl[d] + sti[...]
    for i in xs:
        send(stx.at[x], stx.at[x], RQX + x, xdev(i))
    arrived(cs, RC)
    cots = jnp.concatenate([cb[d], cs[...]], axis=0)
    x_start(far)
    other_shares(1, RP2)
    x_direct(far)
    x_start(near)
    other_sum(0, RP)
    x_relay(far)
    x_direct(near)
    other_sum(1, RP2)
    own_shares()
    for h in (far, near):
        gown[h] = slab(h, x)
    for i in xs:
        arrived(stx.at[i], RQX + i)
    stm[mate] = (stx[0] + stx[1]) + (stx[2] + stx[3])
    for i in ms:
        send(stm.at[mate], stm.at[mate], RQM + mate, mdev(i))
    x_relay(near)
    x_sum(far)
    x_sum(near)
    for i in ms:
        arrived(stm.at[i], RQM + i)
    stp[half] = (stm[0] + stm[1]) + (stm[2] + stm[3])
    send(stp.at[half], stp.at[half], RQP, partner)
    mates_far(0, RM + 4 * far, RB)
    mates_far(1, RM2, RB2)
    kept = own_sum()
    g = mates_near()
    arrived(stp.at[1 - half], RQP)
    tfin[d] = stp[0] + stp[1]
    send(tfin.at[d], tfin.at[d], RQ2, sib)

    arrived(bin_.at[pl.ds(0, 32)], RB)
    arrived(bin_.at[pl.ds(32, 32)], RB2)
    gfin[d] = g + bin_[...].astype(F32)
    send(gfin.at[d], gfin.at[d], RW2, sib)
    arrived(tfin.at[1 - d], RQ2)
    tot = jnp.concatenate([tfin[0], tfin[1]], axis=1)
    gskip[...] = tot[:, 0:WID]
    ratio = resid[...] * jnp.exp(-2.0 * rt) / factor
    for m in range(MODES):
        paired = tot[:, WID * (1 + m) : WID * (2 + m)]
        carried = tot[:, WID * (5 + m) : WID * (6 + m)]
        gres[m : m + 1, :] = factor[m : m + 1, :] * paired
        grate[m : m + 1, :] = ratio[m : m + 1, :] * paired - carried
    for p, sem in ((0, RPA), (1, RPA2)):
        arrived(pa_in.at[pl.ds(p * PART, PART)], sem)
    gtok[0] = (kept + pa_in[...].astype(F32)).astype(BF)
    arrived(gfin.at[1 - d], RW2)
    gwv[...] = gfin[0]
    gwg[...] = gfin[1]
    assert len(sends) <= NSEND
    for cp in sends:
        cp.wait_send()


def one_minus_exp(a):
    term = a
    total = a
    for k in range(2, 8):
        term = term * (-a / k)
        total = total + term
    return total


def store(*refs):
    sem = refs[14]
    copies = [pltpu.make_async_copy(refs[k], refs[7 + k], sem.at[k]) for k in range(7)]
    for cp in copies:
        cp.start()
    for cp in copies:
        cp.wait()


def body(tokens, cotangent, w_value, w_gate, decay_rate, residue, skip_gain, contig_len):
    vm = pl.BlockSpec(memory_space=pltpu.VMEM)
    hbm = pl.BlockSpec(memory_space=pltpu.HBM)
    sds = jax.ShapeDtypeStruct
    shapes = (
        sds((1, SPAN, WID), BF),
        sds((1, SPAN, WID), BF),
        sds((64, WID), F32),
        sds((64, WID), F32),
        sds((1, WID), F32),
        sds((MODES, WID), F32),
        sds((MODES, WID), F32),
    )
    outs = pl.pallas_call(
        kernel,
        out_shape=shapes,
        in_specs=[hbm] * 8,
        out_specs=(vm,) * 7,
        scratch_shapes=[
            pltpu.VMEM((8, SPAN, WID), BF),
            pltpu.VMEM((8, SPAN, WID), BF),
            pltpu.VMEM((2, 32, 64, WID), BF),
            pltpu.VMEM((SPAN, WID), BF),
            pltpu.VMEM((MODES, SPAN, WID), F32),
            pltpu.VMEM((MODES, SPAN, WID), F32),
            pltpu.VMEM((MODES, SPAN, WID), F32),
            pltpu.VMEM((MODES, SPAN, WID), F32),
            pltpu.VMEM((2, MODES * WID), F32),
            pltpu.VMEM((2, MODES * WID), BF),
            pltpu.VMEM((8, 2, MODES * WID), BF),
            pltpu.VMEM((8, 2, MODES * WID), F32),
            pltpu.VMEM((8, 2, MODES * WID), F32),
            pltpu.VMEM((4, 2, MODES * WID), F32),
            pltpu.VMEM((2, MODES * WID), F32),
            pltpu.VMEM((4, 2, MODES * WID), F32),
            pltpu.VMEM((2, SPAN, WID), BF),
            pltpu.VMEM((SPAN, WID), BF),
            pltpu.VMEM((2, 4, SPAN, WID), BF),
            pltpu.VMEM((2, 4, SPAN, WID), BF),
            pltpu.VMEM((SPAN, WID), BF),
            pltpu.VMEM((SPAN, WID), BF),
            pltpu.VMEM((2, 2, 2, 64, WID), BF),
            pltpu.VMEM((2, 2, 2, 64, WID), BF),
            pltpu.VMEM((2, 2, 2, 64, WID), F32),
            pltpu.VMEM((2, 2, 2, 64, WID), BF),
            pltpu.VMEM((2, 2, 2, 64, WID), BF),
            pltpu.VMEM((2, 2, 2, 2, 64, WID), BF),
            pltpu.VMEM((2, 4, 64, WID), F32),
            pltpu.VMEM((2, 4, 64, WID), BF),
            pltpu.VMEM((2, 4, 64, WID), BF),
            pltpu.VMEM((64, WID), BF),
            pltpu.VMEM((64, WID), BF),
            pltpu.VMEM((2, 64, WID), F32),
            pltpu.VMEM((8, 2 * WID, WID), BF),
            pltpu.VMEM((8, WID, 2 * SPAN), BF),
            pltpu.VMEM((2, 1, NSTAT), F32),
            pltpu.VMEM((1, NSTAT), F32),
            pltpu.VMEM((4, 1, NSTAT), F32),
            pltpu.VMEM((4, 1, NSTAT), F32),
            pltpu.VMEM((2, 1, NSTAT), F32),
            pltpu.VMEM((2, 1, NSTAT), F32),
            pltpu.VMEM((MODES, WID), F32),
            pltpu.VMEM((MODES, WID), F32),
            pltpu.VMEM((1, WID), F32),
            pltpu.SMEM((1, 8), jnp.int32),
            pltpu.SemaphoreType.DMA((NSEND,)),
            pltpu.SemaphoreType.DMA((NRECV,)),
            pltpu.SemaphoreType.DMA((7,)),
        ],
        compiler_params=pltpu.CompilerParams(
            collective_id=0, has_side_effects=True, vmem_limit_bytes=48 << 20
        ),
        name="step",
    )(
        *[
            pltpu.with_memory_space_constraint(a, pltpu.HBM)
            for a in (
                tokens, cotangent, w_value, w_gate, decay_rate, residue,
                skip_gain.reshape(1, WID), contig_len,
            )
        ]
    )
    outs = pl.pallas_call(
        store,
        out_shape=shapes,
        in_specs=[vm] * 7,
        out_specs=(hbm,) * 7,
        scratch_shapes=[pltpu.SemaphoreType.DMA((7,))],
        compiler_params=pltpu.CompilerParams(vmem_limit_bytes=1 << 20),
        name="store",
    )(*outs)
    outs = list(outs)
    outs[4] = outs[4].reshape(WID)
    return tuple(outs)


def solution(mesh):
    in_specs = (
        P("dp", "ctx", "tensor"),
        P("dp", "ctx", "tensor"),
        P("ctx", "tensor"),
        P("ctx", "tensor"),
        P(None, "tensor"),
        P(None, "tensor"),
        P("tensor"),
        P("dp", None),
    )
    out_specs = (
        P("dp", "ctx", "tensor"),
        P("dp", "ctx", "tensor"),
        P("ctx", "tensor"),
        P("ctx", "tensor"),
        P("tensor"),
        P(None, "tensor"),
        P(None, "tensor"),
    )
    return jax.shard_map(body, mesh=mesh, in_specs=in_specs, out_specs=out_specs, check_vma=False)
```
